32 devices in a mesh: groups: 2 (over y), seq: 4 (over z), head: 2 (over x), rep: 2 (over core).
Axes of the slice: x: 2, y: 2, z: 4, core: 2. Of those that a mesh axis runs over, the one named last changes fastest.
Arguments:
- book_tokens: bfloat16 [16384, 1024], P(('groups', 'seq', 'rep')), parts along dimension 0, may hold values from -6 to 6
- norm_gain: float32 [1024], replicated, may hold values from 0.1 to 1.9
- query_weight: bfloat16 [1024, 1024], P(None, 'head'), may hold values from -0.1875 to 0.1875
- key_weight: bfloat16 [1024, 1024], P(None, 'head'), may hold values from -0.1875 to 0.1875
- value_weight: bfloat16 [1024, 1024], P(None, 'head'), may hold values from -0.1875 to 0.1875
- proj_weight: bfloat16 [1024, 4096], P(None, 'head'), may hold values from -0.75 to 0.75
- dual_gains: float32 [4, 1024], P(None, 'head'), may hold values from 0.1 to 1.9
- out_weight: bfloat16 [1024, 1024], P(None, 'head'), may hold values from -1.5 to 1.5
- span_bounds: int32 [128, 2], P('groups'), parts along dimension 0, may hold values from 0 to 8192, as said below
Outputs:
- attended: bfloat16 [16384, 1024], P(('groups', 'seq', 'rep'), 'head'), parts along dimension 0
- pooled: float32 [128, 1024], P(('groups', 'seq', 'rep'), 'head'), parts along dimension 0
The draws below stay inside these ranges and needn't reach their ends.
There are 2 independent parts, one for each index of `groups`. The reference program is written for one: setup_inputs(seed, part) draws one part's arguments, and reference() takes and returns one part's arrays. A program takes and returns all parts, laid end to end along the dimension named above; an argument that names none is the same for every part. Nothing has to cross between parts.
Inputs may be any that keep to these rules, and one draw needn't show every extreme that they name: `span_bounds`: each span lies inside the book and holds 1 to 512 tokens; spans may intersect and come in any order; the longest holds exactly 512 tokens.
All inputs are finite; a program needn't handle non-finite values.
Results may differ from the reference program's by a relative error of at most 0.023.
Values may be sent and summed in bfloat16 or wider, within the bound.
No kernel may reach another device: no remote copies, remote signals or barrier semaphores. Data moves between devices by JAX's collectives and lax.ppermute only.
A program may use at most 64 MiB of HBM per device.

```python
import jax
import jax.numpy as jnp
from jax import lax

D = 1024
H = 16
DH = 64
R = 256
SEG = 128
TOK_DEV = 1024
SEQ_LEN = 8192
SPANS = 64


def draw_span_bounds(key, part):
    longest = SEQ_LEN // 16
    key_len = jax.random.fold_in(key, 11)
    key_start = jax.random.fold_in(key, 12)
    key_first = jax.random.fold_in(key, 13)
    lengths = jax.random.randint(key_len, (SPANS,), 1, longest + 1).astype(jnp.int32)
    lengths = lengths.at[0].set(longest)
    starts = jax.random.randint(key_start, (SPANS,), 0, SEQ_LEN - lengths + 1).astype(jnp.int32)
    first = SEQ_LEN // 2 + jax.random.randint(key_first, (), 0, TOK_DEV // 2).astype(jnp.int32)
    starts = starts.at[0].set(first)
    return jnp.stack([starts, starts + lengths], axis=1).astype(jnp.int32)


def block_scale(stream_key, extent, pieces, low, top_value):
    gain = 1.0
    for dim, shards_of in pieces:
        steps = jax.random.uniform(jax.random.fold_in(jax.random.fold_in(stream_key, 6), dim), (shards_of,), jnp.float32, low / len(pieces), top_value / len(pieces))
        gain = gain * jnp.repeat(jnp.exp(steps), extent[dim] // shards_of).reshape((-1,) + (1,) * (len(extent) - 1 - dim))
    return gain


def gaussian(stream_key, shape, width, limit, shards=(), kind=jnp.bfloat16):
    array = width * jax.random.normal(stream_key, shape, jnp.float32)
    if shards:
        array = array * block_scale(stream_key, shape, shards, -0.22, 0.18)
    return jnp.clip(array, -limit, limit).astype(kind)


def setup_inputs(seed: int = 0, part: int = 0) -> dict:
    streams_of = jax.random.split(jax.random.key(seed), 10)
    own_keys = jax.random.split(jax.random.fold_in(streams_of[9], part), 10)
    book_tokens = gaussian(own_keys[0], (SEQ_LEN, D), 1.0, 6.0, ((0, 8),))
    norm_gain = jnp.clip(1.0 + 0.18 * jax.random.normal(streams_of[1], (D,), jnp.float32), 0.1, 1.9)
    query_weight = gaussian(streams_of[2], (D, H * DH), D ** -0.5, 0.1875, ((1, 2),))
    key_weight = gaussian(streams_of[3], (D, H * DH), D ** -0.5, 0.1875, ((1, 2),))
    value_weight = gaussian(streams_of[4], (D, H * DH), D ** -0.5, 0.1875, ((1, 2),))
    proj_weight = gaussian(streams_of[5], (D, H * R), (D // 16) ** -0.5, 0.75, ((1, 2),))
    dual_gains = jnp.clip(1.0 + 0.18 * jax.random.normal(streams_of[6], (4, H * DH), jnp.float32), 0.1, 1.9)
    out_weight = gaussian(streams_of[7], (H * DH, D), (D // 64) ** -0.5, 1.5, ((1, 2),))
    span_bounds = draw_span_bounds(jax.random.fold_in(jax.random.fold_in(streams_of[9], part), 71), part)
    return dict(book_tokens=book_tokens, norm_gain=norm_gain, query_weight=query_weight, key_weight=key_weight, value_weight=value_weight, proj_weight=proj_weight, dual_gains=dual_gains, out_weight=out_weight, span_bounds=span_bounds)


softcap = 5.0
epsilon = 1e-05

def normalize(values, gain_row):
    centre = lax.optimization_barrier(jnp.mean(values, axis=-1, keepdims=True))
    spread = lax.optimization_barrier(jnp.mean(jnp.square(values - centre), axis=-1, keepdims=True))
    return (values - centre) * lax.rsqrt(spread + epsilon) * gain_row

def capped(values):
    return softcap * jnp.tanh(values / softcap)

def window_head(queries, near_keys, near_values, land_keys, land_values):
    length = queries.shape[0]
    segments = length // SEG
    half_seg = SEG // 2
    query_blocks = queries.reshape(segments, SEG, DH).astype(jnp.float32)

    def windows(source):
        padded = jnp.pad(source, ((half_seg, half_seg), (0, 0)))
        blocks = padded.reshape(segments + 1, SEG, DH)
        return jnp.concatenate([blocks[:-1], blocks[1:]], axis=1).astype(jnp.float32)
    key_window = windows(near_keys)
    value_window = windows(near_values)
    position = jnp.arange(segments)[:, None] * SEG + jnp.arange(2 * SEG)[None, :] - half_seg
    inside = (position >= 0) & (position < length)
    near_scores = capped(jnp.einsum('sqd,skd->sqk', query_blocks, key_window) * DH ** (-0.5))
    near_exp = jnp.where(inside[:, None, :], jnp.exp(near_scores), 0.0)
    far_scores = capped(jnp.einsum('sqd,rd->sqr', query_blocks, land_keys.astype(jnp.float32)) * DH ** (-0.5))
    far_exp = jnp.exp(far_scores)
    summed = lax.optimization_barrier(jnp.sum(near_exp, axis=-1, keepdims=True)) + lax.optimization_barrier(jnp.sum(far_exp, axis=-1, keepdims=True))
    near_probs = (near_exp / summed).astype(jnp.bfloat16)
    far_probs = (far_exp / summed).astype(jnp.bfloat16)
    output = jnp.einsum('sqk,skd->sqd', near_probs.astype(jnp.float32), value_window)
    output = output + jnp.einsum('sqr,rd->sqd', far_probs.astype(jnp.float32), land_values.astype(jnp.float32))
    return output.astype(jnp.bfloat16).reshape(length, DH)

def reference(book_tokens, norm_gain, query_weight, key_weight, value_weight, proj_weight, dual_gains, out_weight, span_bounds):
    length = book_tokens.shape[0]
    normed = normalize(book_tokens.astype(jnp.float32), norm_gain).astype(jnp.bfloat16)
    queries = jnp.dot(normed, query_weight, preferred_element_type=jnp.float32).astype(jnp.bfloat16).reshape(length, H, DH)
    key_raw = jnp.dot(normed, key_weight, preferred_element_type=jnp.float32).reshape(length, H, DH)
    value_raw = jnp.dot(normed, value_weight, preferred_element_type=jnp.float32).reshape(length, H, DH)
    gain_rows = dual_gains.reshape(4, H, DH)
    near_keys = normalize(key_raw, gain_rows[0]).astype(jnp.bfloat16)
    near_values = normalize(value_raw, gain_rows[1]).astype(jnp.bfloat16)
    raw_pairs = jnp.concatenate([key_raw, value_raw], axis=-1).astype(jnp.bfloat16)
    logits = jnp.dot(normed, proj_weight, preferred_element_type=jnp.float32).reshape(length, H, R)
    proj_weights = jnp.exp(capped(logits)).astype(jnp.bfloat16)
    numerator = jnp.einsum('nhr,nhe->hre', proj_weights.astype(jnp.float32), raw_pairs.astype(jnp.float32))
    land_keys = normalize(numerator[:, :, :DH], gain_rows[2][:, None, :]).astype(jnp.bfloat16)
    land_values = normalize(numerator[:, :, DH:], gain_rows[3][:, None, :]).astype(jnp.bfloat16)
    outputs = lax.map(lambda packed: window_head(packed[0], packed[1], packed[2], packed[3], packed[4]), (jnp.transpose(queries, (1, 0, 2)), jnp.transpose(near_keys, (1, 0, 2)), jnp.transpose(near_values, (1, 0, 2)), land_keys, land_values))
    heads_out = jnp.transpose(outputs, (1, 0, 2)).reshape(length, H * DH)
    attended = jnp.dot(heads_out, out_weight, preferred_element_type=jnp.float32).astype(jnp.bfloat16)
    span_start = span_bounds[:, 0]
    span_end = span_bounds[:, 1]
    position = jnp.arange(length).astype(jnp.int32)
    member = ((position[None, :] >= span_start[:, None]) & (position[None, :] < span_end[:, None])).astype(jnp.bfloat16)
    counts = (span_end - span_start).astype(jnp.float32)
    pooled = jnp.dot(member, attended, preferred_element_type=jnp.float32) / counts[:, None]
    return (attended, pooled)
```

```python
import functools

import jax
import jax.numpy as jnp
from jax import lax
from jax.experimental import pallas as pl
from jax.experimental.pallas import tpu as pltpu
from jax.sharding import PartitionSpec as P

DH = 64
R = 256
SEG = 128
HALF = SEG // 2
LANES = 2 * DH
SCORE_SCALE = DH ** (-0.5)
LOG2E = 1.4426950408889634

softcap = 5.0
epsilon = 1e-05

BF = jnp.bfloat16
F32 = jnp.float32
VMEM_LIMIT = 48 << 20


def dot(a, b, dims=((1,), (0,))):
    return lax.dot_general(a, b, (dims, ((), ())), preferred_element_type=F32)


def exp_capped(values, scale):
    return jnp.exp2((softcap * LOG2E) * jnp.tanh(values * (scale / softcap)))


def vmem():
    return pl.BlockSpec(memory_space=pltpu.VMEM)


def smem():
    return pl.BlockSpec(memory_space=pltpu.SMEM)


def head_mean_matrix(width):
    row = lax.broadcasted_iota(jnp.int32, (width, width), 0) // DH
    col = lax.broadcasted_iota(jnp.int32, (width, width), 1) // DH
    return jnp.where(row == col, 1.0 / DH, 0.0).astype(BF)


def head_norm(values, means, gain):
    high = values.astype(BF)
    low = (values - high.astype(F32)).astype(BF)
    centred = values - (dot(high, means) + dot(low, means))
    spread = dot((centred * centred).astype(BF), means)
    return (centred * lax.rsqrt(spread + epsilon) * gain).astype(BF)


def front_kernel(first, pairs, tile, *refs):
    if first:
        (ids_ref, x_ref, gain_ref, wq_ref, wk_ref, wv_ref, wp_ref, dual_ref,
         normed_ref, q_ref, near_ref, keep_ref, send_ref, raw_ref, p_ref) = refs
    else:
        (ids_ref, normed_ref, wq_ref, wk_ref, wv_ref, wp_ref, dual_ref,
         q_ref, near_ref, keep_ref, send_ref, raw_ref, p_ref) = refs
    rows = normed_ref.shape[0]
    width = pairs * LANES
    means = head_mean_matrix(width)
    for start in range(0, rows, tile):
        at = pl.ds(start, tile)
        if first:
            x = x_ref[at, :].astype(F32)
            centred = x - jnp.mean(x, axis=-1, keepdims=True)
            spread = jnp.mean(centred * centred, axis=-1, keepdims=True)
            normed_ref[at, :] = (centred * lax.rsqrt(spread + epsilon) * gain_ref[...]).astype(BF)
        normed = normed_ref[at, :]
        q_ref[at, :] = dot(normed, wq_ref[...]).astype(BF)
        key = dot(normed, wk_ref[...])
        value = dot(normed, wv_ref[...])
        near_ref[at, :width] = head_norm(key, means, dual_ref[0:1, :])
        near_ref[at, width:] = head_norm(value, means, dual_ref[1:2, :])
        for p in range(pairs):
            raw_ref[at, 2 * p * LANES : (2 * p + 1) * LANES] = key[:, p * LANES : (p + 1) * LANES].astype(BF)
            raw_ref[at, (2 * p + 1) * LANES : (2 * p + 2) * LANES] = value[:, p * LANES : (p + 1) * LANES].astype(BF)
        for p in range(pairs):
            cols = slice(2 * p * R, 2 * (p + 1) * R)
            p_ref[at, cols] = exp_capped(dot(normed, wp_ref[:, cols]), 1.0).astype(BF)
    total = []
    for p in range(pairs):
        full = dot(raw_ref[:, 2 * p * LANES : 2 * (p + 1) * LANES], p_ref[:, 2 * p * R : 2 * (p + 1) * R], ((0,), (0,)))
        for part in range(4):
            head = part % 2
            total.append(full[part * DH : (part + 1) * DH, head * R : (head + 1) * R])
    total = jnp.concatenate(total, axis=0).astype(BF)
    half = total.shape[0] // 2
    mine = ids_ref[0] == 0
    keep_ref[...] = jnp.where(mine, total[:half], total[half:])
    send_ref[...] = jnp.where(mine, total[half:], total[:half])


def front(first, group, pairs, ids, tokens, gain, wq, wk, wv, wp, dual):
    rows, depth = tokens.shape
    width = pairs * LANES
    half = pairs * R // 2
    outs = [
        jax.ShapeDtypeStruct((rows, width), BF),
        jax.ShapeDtypeStruct((rows, 2 * width), BF),
        jax.ShapeDtypeStruct((half, R), BF),
        jax.ShapeDtypeStruct((half, R), BF),
    ]
    ins = [smem(), vmem()]
    args = [ids, tokens]
    if first:
        outs = [jax.ShapeDtypeStruct((rows, depth), BF)] + outs
        ins.append(vmem())
        args.append(gain)
    at = lambda i: (0, group)
    ins += [pl.BlockSpec((depth, width), at)] * 3
    ins += [pl.BlockSpec((depth, 2 * pairs * R), at), pl.BlockSpec((4, width), at)]
    args += [wq, wk, wv, wp, dual]
    whole = lambda s: pl.BlockSpec(s.shape, lambda i: (0, 0))
    ins = [
        s if s.block_shape is not None or s.memory_space == pltpu.SMEM else pl.BlockSpec(a.shape, lambda i: (0, 0))
        for s, a in zip(ins, args)
    ]
    return pl.pallas_call(
        functools.partial(front_kernel, first, pairs, min(256, rows)),
        grid=(1,),
        in_specs=ins,
        out_specs=[whole(s) for s in outs],
        out_shape=outs,
        scratch_shapes=[pltpu.VMEM((rows, 2 * width), BF), pltpu.VMEM((rows, 2 * pairs * R), BF)],
        compiler_params=pltpu.CompilerParams(vmem_limit_bytes=VMEM_LIMIT),
        cost_estimate=pl.CostEstimate(
            flops=2 * rows * depth * (3 * width + 2 * pairs * R) * 2, bytes_accessed=8 << 20, transcendentals=0
        ),
        name="front",
    )(*args)


def lane_is_first(shape):
    return lax.broadcasted_iota(jnp.int32, shape, 1) < DH


def stacked(q):
    first = lane_is_first(q.shape)
    zero = jnp.zeros_like(q)
    return jnp.concatenate([jnp.where(first, q, zero), jnp.where(first, zero, q)], axis=0)


def unstack(both):
    rows = both.shape[0] // 2
    first = lane_is_first((rows, LANES))
    return (
        jnp.where(first, both[:rows, :LANES], both[rows:, :LANES]),
        jnp.where(first, both[:rows, LANES:], both[rows:, LANES:]),
    )


def near_kernel(pairs, ids_ref, q_ref, near_ref, prev_ref, next_ref, out_ref, pad_ref):
    rows = q_ref.shape[0]
    width = pairs * LANES
    pad_ref[0:HALF, :] = prev_ref[...]
    pad_ref[HALF : HALF + rows, :] = near_ref[...]
    pad_ref[HALF + rows :, :] = next_ref[...]
    row = lax.broadcasted_iota(jnp.int32, (2 * SEG, LANES), 0)
    ones = jnp.ones((2 * SEG, LANES), F32)
    has_prev = jnp.where(ids_ref[1] != 0, 1.0, 0.0)
    has_next = jnp.where(ids_ref[2] != 0, 1.0, 0.0)
    segments = rows // SEG
    for s in range(segments):
        count = ones
        if s == 0:
            count = jnp.where(row < HALF, has_prev, count)
        if s == segments - 1:
            count = jnp.where(row >= 3 * HALF, has_next, count)
        count = count.astype(BF)
        window = pl.ds(s * SEG, 2 * SEG)
        for p in range(pairs):
            cols = slice(p * LANES, (p + 1) * LANES)
            q = stacked(q_ref[s * SEG : (s + 1) * SEG, cols])
            scores = dot(q, pad_ref[window, cols], ((1,), (1,)))
            weights = exp_capped(scores, SCORE_SCALE).astype(BF)
            values = jnp.concatenate([pad_ref[window, width + p * LANES : width + (p + 1) * LANES], count], axis=1)
            top, bottom = unstack(dot(weights, values))
            out_ref[s * SEG : (s + 1) * SEG, 2 * p * LANES : (2 * p + 1) * LANES] = top
            out_ref[s * SEG : (s + 1) * SEG, (2 * p + 1) * LANES : (2 * p + 2) * LANES] = bottom


def near(pairs, ids, q, pairs_own, prev, following, group):
    rows = q.shape[0]
    width = pairs * LANES
    at = lambda i: (0, 0)
    return pl.pallas_call(
        functools.partial(near_kernel, pairs),
        grid=(1,),
        in_specs=[smem(), pl.BlockSpec(q.shape, at), pl.BlockSpec(pairs_own.shape, at)]
        + [pl.BlockSpec((HALF, 2 * width), lambda i: (0, group))] * 2,
        out_specs=pl.BlockSpec((rows, 2 * width), at),
        out_shape=jax.ShapeDtypeStruct((rows, 2 * width), F32),
        scratch_shapes=[pltpu.VMEM((rows + SEG, 2 * width), BF)],
        compiler_params=pltpu.CompilerParams(vmem_limit_bytes=VMEM_LIMIT),
        cost_estimate=pl.CostEstimate(flops=rows * pairs * (1 << 19), bytes_accessed=4 << 20, transcendentals=0),
        name="near",
    )(ids, q, pairs_own, prev, following)


def far_kernel(pairs, block, ids_ref, q_ref, near_ref, mine_ref, other_ref, gains_ref, bounds_ref, out_ref, sums_ref):
    rows = q_ref.shape[0]
    is_first = ids_ref[0] == 0
    top = jnp.where(is_first, mine_ref[...], other_ref[...])
    bottom = jnp.where(is_first, other_ref[...], mine_ref[...])
    total = jnp.concatenate([top, bottom], axis=0)
    ones = jnp.ones((LANES, R), BF)
    for p in range(pairs):
        cols = slice(p * LANES, (p + 1) * LANES)

        def land(kind):
            parts = []
            for h in range(2):
                at = p * R + kind * LANES + h * DH
                values = total[at : at + DH].astype(F32)
                centred = values - jnp.mean(values, axis=0, keepdims=True)
                spread = jnp.mean(centred * centred, axis=0, keepdims=True)
                gain = gains_ref[p * LANES + h * DH : p * LANES + (h + 1) * DH, 2 + kind : 3 + kind]
                parts.append((centred * lax.rsqrt(spread + epsilon) * gain).astype(BF))
            return jnp.concatenate(parts, axis=0)

        keys = land(0)
        values = jnp.concatenate([land(1), ones], axis=0)
        for start in range(0, rows, block):
            q = stacked(q_ref[start : start + block, cols])
            weights = exp_capped(dot(q, keys), SCORE_SCALE).astype(BF)
            top, bottom = unstack(dot(weights, values, ((1,), (1,))))
            top = top + near_ref[start : start + block, 2 * p * LANES : (2 * p + 1) * LANES]
            bottom = bottom + near_ref[start : start + block, (2 * p + 1) * LANES : (2 * p + 2) * LANES]
            out_ref[start : start + block, cols] = (top / bottom).astype(BF)
    spans = bounds_ref.shape[0]
    position = ids_ref[3] + lax.broadcasted_iota(jnp.int32, (spans, rows), 1)
    member = (position >= bounds_ref[:, 0:1]) & (position < bounds_ref[:, 1:2])
    member = jnp.where(member, 1.0, 0.0).astype(BF)
    sums_ref[...] = dot(member, out_ref[...]).astype(BF)


def far(pairs, ids, q, near_sums, mine, other, gains, bounds, group):
    rows = q.shape[0]
    width = pairs * LANES
    at = lambda i: (0, 0)
    return pl.pallas_call(
        functools.partial(far_kernel, pairs, 256),
        grid=(1,),
        in_specs=[
            smem(),
            pl.BlockSpec(q.shape, at),
            pl.BlockSpec(near_sums.shape, at),
            pl.BlockSpec(mine.shape, at),
            pl.BlockSpec(other.shape, at),
            pl.BlockSpec((width, 4), lambda i: (group, 0)),
            pl.BlockSpec(bounds.shape, at),
        ],
        out_specs=[pl.BlockSpec((rows, width), at), pl.BlockSpec((bounds.shape[0], width), at)],
        out_shape=[jax.ShapeDtypeStruct((rows, width), BF), jax.ShapeDtypeStruct((bounds.shape[0], width), BF)],
        compiler_params=pltpu.CompilerParams(vmem_limit_bytes=VMEM_LIMIT),
        cost_estimate=pl.CostEstimate(flops=rows * pairs * (1 << 19), bytes_accessed=4 << 20, transcendentals=0),
        name="far",
    )(ids, q, near_sums, mine, other, gains, bounds)


def out_kernel(count, final, *refs):
    refs = refs[1:]
    tokens, weights = refs[:count], refs[count : 2 * count]
    out_ref = refs[-1]
    acc = refs[2 * count][...] if len(refs) == 2 * count + 2 else None
    for a, w in zip(tokens, weights):
        term = dot(a[...], w[...])
        acc = term if acc is None else acc + term
    out_ref[...] = acc.astype(out_ref.dtype)


def out_part(parts, index, weight, acc, dtype):
    count = len(parts)
    rows, width = parts[0].shape
    columns = weight.shape[1]
    tile = min(256, rows)
    row_spec = pl.BlockSpec((tile, width), lambda i, ids: (i, 0))
    weight_specs = [pl.BlockSpec((width, columns), lambda i, ids, j=j: (ids[j], 0)) for j in range(count)]
    out_spec = pl.BlockSpec((tile, columns), lambda i, ids: (i, 0))
    extra = [] if acc is None else [acc]
    return pl.pallas_call(
        functools.partial(out_kernel, count, acc is not None),
        grid_spec=pltpu.PrefetchScalarGridSpec(
            num_scalar_prefetch=1,
            grid=(rows // tile,),
            in_specs=[row_spec] * count + weight_specs + [out_spec] * len(extra),
            out_specs=out_spec,
        ),
        out_shape=jax.ShapeDtypeStruct((rows, columns), dtype),
        compiler_params=pltpu.CompilerParams(vmem_limit_bytes=VMEM_LIMIT),
        cost_estimate=pl.CostEstimate(
            flops=2 * rows * width * columns * count, bytes_accessed=4 << 20, transcendentals=0
        ),
        name="out",
    )(index, *parts, *([weight] * count), *extra)


def swap(values, axis, step):
    count = lax.axis_size(axis)
    return lax.ppermute(values, axis, [(i, i ^ step) for i in range(count)])


def add(a, b):
    return (a.astype(F32) + b.astype(F32)).astype(BF)


def steps_of(axis):
    step = 1
    while step < lax.axis_size(axis):
        yield step
        step *= 2


def per_device(
    book_tokens,
    norm_gain,
    query_weight,
    key_weight,
    value_weight,
    proj_weight,
    dual_gains,
    out_weight,
    span_bounds,
):
    rows = book_tokens.shape[0]
    seq_devices = lax.axis_size(("seq", "rep"))
    seq_index = lax.axis_index(("seq", "rep"))
    head_devices = lax.axis_size("head")
    head_index = lax.axis_index("head")
    first_row = seq_index * rows
    all_pairs = query_weight.shape[1] // LANES
    groups = 2 if all_pairs % 2 == 0 else 1
    pairs = all_pairs // groups
    ids = jnp.stack(
        [lax.axis_index("rep"), (seq_index > 0).astype(jnp.int32), (seq_index < seq_devices - 1).astype(jnp.int32), first_row]
    ).astype(jnp.int32)
    gain = norm_gain[None, :]
    gain_columns = dual_gains.T

    fronts = []
    tokens = book_tokens
    for g in range(groups):
        outs = front(g == 0, g, pairs, ids, tokens, gain, query_weight, key_weight, value_weight, proj_weight, dual_gains)
        if g == 0:
            tokens, outs = outs[0], outs[1:]
        fronts.append(outs)

    totals = []
    for q, near_pairs, keep, send in fronts:
        mine = add(keep, swap(send, "rep", 1))
        for step in steps_of("seq"):
            mine = add(mine, swap(mine, "seq", step))
        totals.append((mine, swap(mine, "rep", 1)))

    tails = jnp.concatenate([f[1][rows - HALF :] for f in fronts], axis=1)
    heads = jnp.concatenate([f[1][:HALF] for f in fronts], axis=1)
    both = ("seq", "rep")
    prev = lax.ppermute(tails, both, [(i, i + 1) for i in range(seq_devices - 1)])
    following = lax.ppermute(heads, both, [(i + 1, i) for i in range(seq_devices - 1)])

    nears = [near(pairs, ids, f[0], f[1], prev, following, g) for g, f in enumerate(fronts)]
    outs = [
        far(pairs, ids, fronts[g][0], nears[g], *totals[g], gain_columns, span_bounds, g) for g in range(groups)
    ]

    own_index = [head_index * groups + g for g in range(groups)]
    others, other_index = [], []
    for g in range(groups):
        for k in range(1, head_devices):
            others.append(lax.ppermute(outs[g][0], "head", [(i, (i + k) % head_devices) for i in range(head_devices)]))
            other_index.append(lax.rem(head_index - k + head_devices, head_devices) * groups + g)
    early = len(others) - (head_devices - 1)
    parts = [o[0] for o in outs] + others[:early]
    index = jnp.stack(own_index + other_index[:early]).astype(jnp.int32)
    acc = out_part(parts, index, out_weight, None, F32)
    index = jnp.stack(other_index[early:]).astype(jnp.int32)
    attended = out_part(others[early:], index, out_weight, acc, BF)

    sums = jnp.concatenate([o[1] for o in outs], axis=1)
    sums = add(sums, swap(sums, "rep", 1))
    for step in steps_of("seq"):
        sums = add(sums, swap(sums, "seq", step))
    span_rows = sums.shape[0] // seq_devices
    own_bounds = lax.dynamic_slice_in_dim(span_bounds, seq_index * span_rows, span_rows, 0)
    counts = (own_bounds[:, 1] - own_bounds[:, 0]).astype(F32)
    own = lax.dynamic_slice_in_dim(sums, seq_index * span_rows, span_rows, 0)
    width = own.shape[1]
    spread = [own] + [
        lax.ppermute(own, "head", [(i, (i + k) % head_devices) for i in range(head_devices)])
        for k in range(1, head_devices)
    ]
    pooled = None
    for k, values in enumerate(spread):
        source = lax.rem(head_index - k + head_devices, head_devices)
        weight = lax.dynamic_slice_in_dim(out_weight, source * width, width, 0)
        term = jnp.dot(values, weight, preferred_element_type=F32)
        pooled = term if pooled is None else pooled + term
    pooled = pooled / counts[:, None]
    return (attended, pooled)


def solution(mesh):
    placed = (
        P(("groups", "seq", "rep"), None),
        P(),
        P(None, "head"),
        P(None, "head"),
        P(None, "head"),
        P(None, "head"),
        P(None, "head"),
        P(None, "head"),
        P("groups", None),
    )
    return jax.shard_map(
        per_device,
        mesh=mesh,
        in_specs=placed,
        out_specs=(P(("groups", "seq", "rep"), "head"), P(("groups", "seq", "rep"), "head")),
        check_vma=False,
    )
```

```python
import functools

import jax
import jax.numpy as jnp
from jax import lax
from jax.experimental import pallas as pl
from jax.experimental.pallas import tpu as pltpu
from jax.sharding import PartitionSpec as P

DH = 64
R = 256
SEG = 128
HALF = SEG // 2
LANES = 2 * DH
SCORE_SCALE = DH ** (-0.5)
LOG2E = 1.4426950408889634

softcap = 5.0
epsilon = 1e-05

BF = jnp.bfloat16
F32 = jnp.float32


def dot(a, b, dims=((1,), (0,))):
    return lax.dot_general(a, b, (dims, ((), ())), preferred_element_type=F32)


def exp_capped(values, scale):
    return jnp.exp2((softcap * LOG2E) * jnp.tanh(values * (scale / softcap)))


def vmem():
    return pl.BlockSpec(memory_space=pltpu.VMEM)


def smem():
    return pl.BlockSpec(memory_space=pltpu.SMEM)


def head_norm(values, gain):
    out = []
    for at in range(0, values.shape[1], LANES):
        x = values[:, at : at + LANES]
        first = lane_is_first(x.shape)

        def mean(y):
            low = jnp.sum(jnp.where(first, y, 0.0), axis=-1, keepdims=True)
            high = jnp.sum(jnp.where(first, 0.0, y), axis=-1, keepdims=True)
            return jnp.where(first, low, high) * (1.0 / DH)

        centred = x - mean(x)
        spread = mean(centred * centred)
        out.append((centred * lax.rsqrt(spread + epsilon) * gain[:, at : at + LANES]).astype(BF))
    return jnp.concatenate(out, axis=1)


def token_norm(x, gain):
    x = x.astype(F32)
    centred = x - jnp.mean(x, axis=-1, keepdims=True)
    spread = jnp.mean(centred * centred, axis=-1, keepdims=True)
    return (centred * lax.rsqrt(spread + epsilon) * gain).astype(BF)


def front_kernel(first, group, pairs, tile, *refs):
    if first:
        (ids_ref, x_hbm, gain_ref, wk_hbm, wv_hbm, wp_hbm, dual_ref,
         normed_ref, near_ref, keep_ref, send_ref, raw_ref, p_ref, wk_ref, wv_ref, wp_ref, sem, x_ref) = refs
    else:
        (ids_ref, normed_ref, wk_hbm, wv_hbm, wp_hbm, dual_ref,
         near_ref, keep_ref, send_ref, raw_ref, p_ref, wk_ref, wv_ref, wp_ref, sem) = refs
    rows = normed_ref.shape[0]
    width = pairs * LANES
    chunks = rows // tile
    own = pl.ds(group * width, width)

    def copy(source, target, slot):
        made = pltpu.make_async_copy(source, target, sem.at[slot])
        made.start()
        return made

    def token_copy(i):
        at = pl.ds(i * tile, tile)
        return copy(x_hbm.at[at, :], x_ref.at[at, :], i)

    token_copies = [token_copy(0)] if first else []
    key_copy = copy(wk_hbm.at[:, own], wk_ref, chunks)
    value_copy = copy(wv_hbm.at[:, own], wv_ref, chunks + 1)
    proj_copies = []
    for p in range(pairs):
        cols = pl.ds((group * pairs + p) * 2 * R, 2 * R)
        proj_copies.append(copy(wp_hbm.at[:, cols], wp_ref.at[:, pl.ds(p * 2 * R, 2 * R)], chunks + 2 + p))
        if first and p == 0:
            token_copies += [token_copy(i) for i in range(1, chunks)]
    for i in range(chunks):
        at = pl.ds(i * tile, tile)
        if first:
            token_copies[i].wait()
            normed_ref[at, :] = token_norm(x_ref[at, :], gain_ref[...])
        normed = normed_ref[at, :]
        if i == 0:
            key_copy.wait()
            value_copy.wait()
        key = dot(normed, wk_ref[...])
        value = dot(normed, wv_ref[...])
        for p in range(pairs):
            cols = slice(p * LANES, (p + 1) * LANES)
            raw = jnp.concatenate([key[:, cols], value[:, cols]], axis=1).astype(BF)
            raw_ref[2 * p * LANES : 2 * (p + 1) * LANES, at] = raw.T
        for p in range(pairs):
            cols = slice(2 * p * R, 2 * (p + 1) * R)
            if i == 0:
                proj_copies[p].wait()
            p_ref[at, cols] = exp_capped(dot(normed, wp_ref[:, cols]), 1.0).astype(BF)
        near_ref[at, :width] = head_norm(key, dual_ref[0:1, group * width : (group + 1) * width])
        near_ref[at, width:] = head_norm(value, dual_ref[1:2, group * width : (group + 1) * width])
    total = []
    for p in range(pairs):
        full = dot(raw_ref[2 * p * LANES : 2 * (p + 1) * LANES, :], p_ref[:, 2 * p * R : 2 * (p + 1) * R])
        for part in range(4):
            head = part % 2
            total.append(full[part * DH : (part + 1) * DH, head * R : (head + 1) * R])
    total = jnp.concatenate(total, axis=0).astype(BF)
    half = total.shape[0] // 2
    mine = ids_ref[0] == 0
    keep_ref[...] = jnp.where(mine, total[:half], total[half:])
    send_ref[...] = jnp.where(mine, total[half:], total[:half])


def in_hbm(values):
    return pltpu.with_memory_space_constraint(values, pltpu.HBM)


def front(first, group, pairs, ids, tokens, gain, wk, wv, wp, dual):
    rows, depth = tokens.shape
    width = pairs * LANES
    half = pairs * R // 2
    tile = min(256, rows)
    outs = [
        jax.ShapeDtypeStruct((rows, 2 * width), BF),
        jax.ShapeDtypeStruct((half, R), BF),
        jax.ShapeDtypeStruct((half, R), BF),
    ]
    hbm = pl.BlockSpec(memory_space=pltpu.HBM)
    ins = [smem(), hbm if first else vmem()] + ([vmem()] if first else []) + [hbm] * 3 + [vmem()]
    args = [ids, in_hbm(tokens) if first else tokens] + ([gain] if first else [])
    args += [in_hbm(wk), in_hbm(wv), in_hbm(wp), dual]
    scratch = [
        pltpu.VMEM((2 * width, rows), BF),
        pltpu.VMEM((rows, 2 * pairs * R), BF),
        pltpu.VMEM((depth, width), BF),
        pltpu.VMEM((depth, width), BF),
        pltpu.VMEM((depth, 2 * pairs * R), BF),
        pltpu.SemaphoreType.DMA((rows // tile + 2 + pairs,)),
    ]
    if first:
        outs = [jax.ShapeDtypeStruct((rows, depth), BF)] + outs
        scratch.append(pltpu.VMEM((rows, depth), BF))
    return pl.pallas_call(
        functools.partial(front_kernel, first, group, pairs, tile),
        in_specs=ins,
        out_specs=[vmem()] * len(outs),
        out_shape=outs,
        scratch_shapes=scratch,
        compiler_params=pltpu.CompilerParams(vmem_limit_bytes=24 << 20),
        cost_estimate=pl.CostEstimate(
            flops=2 * rows * depth * (2 * width + 2 * pairs * R) * 2, bytes_accessed=4 << 20, transcendentals=0
        ),
        name="front",
    )(*args)


def lane_is_first(shape):
    return lax.broadcasted_iota(jnp.int32, shape, 1) < DH


def stacked(q):
    first = lane_is_first(q.shape)
    zero = jnp.zeros_like(q)
    return jnp.concatenate([jnp.where(first, q, zero), jnp.where(first, zero, q)], axis=0)


def unstack(both):
    rows = both.shape[0] // 2
    first = lane_is_first((rows, LANES))
    return (
        jnp.where(first, both[:rows, :LANES], both[rows:, :LANES]),
        jnp.where(first, both[:rows, LANES:], both[rows:, LANES:]),
    )


def near_kernel(pairs, group, ids_ref, normed_ref, near_ref, prev_ref, next_ref, gain_ref, wq_ref, wk_ref, wv_ref, dual_ref,
                q_ref, out_ref, pad_ref):
    rows = normed_ref.shape[0]
    width = pairs * LANES
    mine = slice(group * width, (group + 1) * width)
    halo = token_norm(jnp.concatenate([prev_ref[...], next_ref[...]], axis=0), gain_ref[...])
    key = head_norm(dot(halo, wk_ref[:, mine]), dual_ref[0:1, mine])
    value = head_norm(dot(halo, wv_ref[:, mine]), dual_ref[1:2, mine])
    q_ref[...] = dot(normed_ref[...], wq_ref[:, mine]).astype(BF)
    pad_ref[0:HALF, :width] = key[:HALF]
    pad_ref[0:HALF, width:] = value[:HALF]
    pad_ref[HALF : HALF + rows, :] = near_ref[...]
    pad_ref[HALF + rows :, :width] = key[HALF:]
    pad_ref[HALF + rows :, width:] = value[HALF:]
    row = lax.broadcasted_iota(jnp.int32, (2 * SEG, LANES), 0)
    ones = jnp.ones((2 * SEG, LANES), F32)
    has_prev = jnp.where(ids_ref[1] != 0, 1.0, 0.0)
    has_next = jnp.where(ids_ref[2] != 0, 1.0, 0.0)
    segments = rows // SEG
    for s in range(segments):
        count = ones
        if s == 0:
            count = jnp.where(row < HALF, has_prev, count)
        if s == segments - 1:
            count = jnp.where(row >= 3 * HALF, has_next, count)
        count = count.astype(BF)
        window = pl.ds(s * SEG, 2 * SEG)
        for p in range(pairs):
            cols = slice(p * LANES, (p + 1) * LANES)
            q = stacked(q_ref[s * SEG : (s + 1) * SEG, cols])
            scores = dot(q, pad_ref[window, cols], ((1,), (1,)))
            weights = exp_capped(scores, SCORE_SCALE).astype(BF)
            values = jnp.concatenate([pad_ref[window, width + p * LANES : width + (p + 1) * LANES], count], axis=1)
            top, bottom = unstack(dot(weights, values))
            out_ref[s * SEG : (s + 1) * SEG, 2 * p * LANES : (2 * p + 1) * LANES] = top
            out_ref[s * SEG : (s + 1) * SEG, (2 * p + 1) * LANES : (2 * p + 2) * LANES] = bottom


def near(pairs, group, ids, normed, near_pairs, prev, following, gain, wq, wk, wv, dual):
    rows = normed.shape[0]
    width = pairs * LANES
    return pl.pallas_call(
        functools.partial(near_kernel, pairs, group),
        in_specs=[smem()] + [vmem()] * 9,
        out_specs=[vmem()] * 2,
        out_shape=[jax.ShapeDtypeStruct((rows, width), BF), jax.ShapeDtypeStruct((rows, 2 * width), F32)],
        scratch_shapes=[pltpu.VMEM((rows + SEG, 2 * width), BF)],
        compiler_params=pltpu.CompilerParams(vmem_limit_bytes=16 << 20),
        cost_estimate=pl.CostEstimate(flops=rows * pairs * (1 << 20), bytes_accessed=4 << 20, transcendentals=0),
        name="near",
    )(ids, normed, near_pairs, prev, following, gain, wq, wk, wv, dual)


def far_kernel(pairs, group, block, spread, *refs):
    (ids_ref, q_ref, near_ref, mine_ref, other_ref, gains_ref, bounds_ref), refs = refs[:7], refs[7:]
    before, (out_ref, keep_ref, send_ref) = refs[:-3], refs[-3:]
    rows = q_ref.shape[0]
    width = pairs * LANES
    is_first = ids_ref[0] == 0
    top = jnp.where(is_first, mine_ref[...], other_ref[...])
    bottom = jnp.where(is_first, other_ref[...], mine_ref[...])
    total = jnp.concatenate([top, bottom], axis=0)
    ones = jnp.ones((LANES, R), BF)
    for p in range(pairs):
        cols = slice(p * LANES, (p + 1) * LANES)

        def land(kind):
            parts = []
            for h in range(2):
                at = p * R + kind * LANES + h * DH
                values = total[at : at + DH].astype(F32)
                centred = values - jnp.mean(values, axis=0, keepdims=True)
                spread = jnp.mean(centred * centred, axis=0, keepdims=True)
                base = group * width + p * LANES + h * DH
                gain = gains_ref[base : base + DH, 2 + kind : 3 + kind]
                parts.append((centred * lax.rsqrt(spread + epsilon) * gain).astype(BF))
            return jnp.concatenate(parts, axis=0)

        keys = land(0)
        values = jnp.concatenate([land(1), ones], axis=0)
        for start in range(0, rows, block):
            q = stacked(q_ref[start : start + block, cols])
            weights = exp_capped(dot(q, keys), SCORE_SCALE).astype(BF)
            top, bottom = unstack(dot(weights, values, ((1,), (1,))))
            top = top + near_ref[start : start + block, 2 * p * LANES : (2 * p + 1) * LANES]
            bottom = bottom + near_ref[start : start + block, (2 * p + 1) * LANES : (2 * p + 2) * LANES]
            out_ref[start : start + block, cols] = (top / bottom).astype(BF)
    spans = bounds_ref.shape[0]
    position = ids_ref[3] + lax.broadcasted_iota(jnp.int32, (spans, rows), 1)
    member = (position >= bounds_ref[:, 0:1]) & (position < bounds_ref[:, 1:2])
    member = jnp.where(member, 1.0, 0.0).astype(BF)
    sums = dot(member, out_ref[...])
    count = spans // (2 * spread)
    even = jnp.concatenate([sums[2 * i * count : (2 * i + 1) * count] for i in range(spread)], axis=0)
    odd = jnp.concatenate([sums[(2 * i + 1) * count : (2 * i + 2) * count] for i in range(spread)], axis=0)
    lanes = slice(group * width, (group + 1) * width)
    if before:
        keep_ref[:, : group * width] = before[0][...]
        send_ref[:, : group * width] = before[1][...]
    keep_ref[:, lanes] = jnp.where(is_first, even, odd)
    send_ref[:, lanes] = jnp.where(is_first, odd, even).astype(BF)


def far(pairs, group, spread, ids, q, near_sums, mine, other, gains, bounds, before):
    rows = q.shape[0]
    width = pairs * LANES
    spans = bounds.shape[0]
    shape = (spans // 2, (group + 1) * width)
    return pl.pallas_call(
        functools.partial(far_kernel, pairs, group, 256, spread),
        in_specs=[smem()] + [vmem()] * (6 + len(before)),
        out_specs=[vmem()] * 3,
        out_shape=[
            jax.ShapeDtypeStruct((rows, width), BF),
            jax.ShapeDtypeStruct(shape, F32),
            jax.ShapeDtypeStruct(shape, BF),
        ],
        compiler_params=pltpu.CompilerParams(vmem_limit_bytes=16 << 20),
        cost_estimate=pl.CostEstimate(flops=rows * pairs * (1 << 20), bytes_accessed=4 << 20, transcendentals=0),
        name="far",
    )(ids, q, near_sums, mine, other, gains, bounds, *before)


def out_kernel(count, *refs):
    ids_ref, refs = refs[0], refs[1:]
    tokens, (weight_ref, *acc), out_ref = refs[:count], refs[count:-1], refs[-1]
    rows, width = tokens[0].shape
    for start in range(0, rows, 256):
        at = slice(start, start + 256)
        total = acc[0][at, :] if acc else None
        for j in range(count):
            weight = weight_ref[pl.ds(pl.multiple_of(ids_ref[j] * width, width), width), :]
            term = dot(tokens[j][at, :], weight)
            total = term if total is None else total + term
        out_ref[at, :] = total.astype(out_ref.dtype)


def out_part(parts, index, weight, acc, dtype):
    count = len(parts)
    rows, width = parts[0].shape
    columns = weight.shape[1]
    extra = [] if acc is None else [acc]
    return pl.pallas_call(
        functools.partial(out_kernel, count),
        in_specs=[smem()] + [vmem()] * (count + 1 + len(extra)),
        out_specs=vmem(),
        out_shape=jax.ShapeDtypeStruct((rows, columns), dtype),
        compiler_params=pltpu.CompilerParams(vmem_limit_bytes=16 << 20),
        cost_estimate=pl.CostEstimate(
            flops=2 * rows * width * columns * count, bytes_accessed=4 << 20, transcendentals=0
        ),
        name="out",
    )(index, *parts, weight, *extra)


def swap(values, axis, step):
    count = lax.axis_size(axis)
    return lax.ppermute(values, axis, [(i, i ^ step) for i in range(count)])


def add(a, b):
    return (a.astype(F32) + b.astype(F32)).astype(BF)


def steps_of(axis):
    step = 1
    while step < lax.axis_size(axis):
        yield step
        step *= 2


def per_device(
    book_tokens,
    norm_gain,
    query_weight,
    key_weight,
    value_weight,
    proj_weight,
    dual_gains,
    out_weight,
    span_bounds,
):
    rows = book_tokens.shape[0]
    seq_devices = lax.axis_size(("seq", "rep"))
    seq_index = lax.axis_index(("seq", "rep"))
    head_devices = lax.axis_size("head")
    head_index = lax.axis_index("head")
    first_row = seq_index * rows
    all_pairs = query_weight.shape[1] // LANES
    groups = 2 if all_pairs % 2 == 0 else 1
    pairs = all_pairs // groups
    ids = jnp.stack(
        [lax.axis_index("rep"), (seq_index > 0).astype(jnp.int32), (seq_index < seq_devices - 1).astype(jnp.int32), first_row]
    ).astype(jnp.int32)
    gain = norm_gain[None, :]
    gain_columns = dual_gains.T

    both = ("seq", "rep")
    totals, nears, tokens, normed = [], [], book_tokens, None
    for g in range(groups):
        outs = front(g == 0, g, pairs, ids, tokens, gain, key_weight, value_weight, proj_weight, dual_gains)
        if g == 0:
            tokens, outs = outs[0], outs[1:]
            normed = tokens
        near_pairs, keep, send = outs
        if g == 0:
            prev = lax.ppermute(book_tokens[rows - HALF :], both, [(i, i + 1) for i in range(seq_devices - 1)])
            following = lax.ppermute(book_tokens[:HALF], both, [(i + 1, i) for i in range(seq_devices - 1)])
        mine = add(keep, swap(send, "rep", 1))
        tokens, mine = lax.optimization_barrier((tokens, mine))
        for step in steps_of("seq"):
            mine = add(mine, swap(mine, "seq", step))
        totals.append((mine, swap(mine, "rep", 1)))
        nears.append(near(pairs, g, ids, normed, near_pairs, prev, following, gain, query_weight, key_weight, value_weight, dual_gains))

    spread = lax.axis_size("seq")
    outs, before = [], ()
    for g in range(groups):
        q, near_sums = nears[g]
        out, *before = far(pairs, g, spread, ids, q, near_sums, *totals[g], gain_columns, span_bounds, before)
        outs.append(out)

    own_index = [head_index * groups + g for g in range(groups)]
    others, other_index = [], []
    for g in range(groups):
        for k in range(1, head_devices):
            others.append(lax.ppermute(outs[g], "head", [(i, (i + k) % head_devices) for i in range(head_devices)]))
            other_index.append(lax.rem(head_index - k + head_devices, head_devices) * groups + g)
    early = len(others) - (head_devices - 1)
    parts = outs + others[:early]
    index = jnp.stack(own_index + other_index[:early]).astype(jnp.int32)
    acc = out_part(parts, index, out_weight, None, F32)
    index = jnp.stack(other_index[early:]).astype(jnp.int32)
    attended = out_part(others[early:], index, out_weight, acc, BF)

    keep, send = before
    sums = keep + swap(send, "rep", 1).astype(F32)
    span_rows = sums.shape[0] // spread
    place = lax.axis_index("seq")
    own = lax.dynamic_slice_in_dim(sums, place * span_rows, span_rows, 0)
    for k in range(1, spread):
        target = lax.rem(place + k, spread)
        piece = lax.dynamic_slice_in_dim(sums, target * span_rows, span_rows, 0).astype(BF)
        own = own + lax.ppermute(piece, "seq", [(i, (i + k) % spread) for i in range(spread)]).astype(F32)
    own_bounds = lax.dynamic_slice_in_dim(span_bounds, seq_index * span_rows, span_rows, 0)
    counts = (own_bounds[:, 1] - own_bounds[:, 0]).astype(F32)
    own = (own / counts[:, None]).astype(BF)
    width = own.shape[1]
    spread = [own] + [
        lax.ppermute(own, "head", [(i, (i + k) % head_devices) for i in range(head_devices)])
        for k in range(1, head_devices)
    ]
    pooled = None
    for k, values in enumerate(spread):
        source = lax.rem(head_index - k + head_devices, head_devices)
        weight = lax.dynamic_slice_in_dim(out_weight, source * width, width, 0)
        term = jnp.dot(values, weight, preferred_element_type=F32)
        pooled = term if pooled is None else pooled + term
    return (attended, pooled)


def solution(mesh):
    placed = (
        P(("groups", "seq", "rep"), None),
        P(),
        P(None, "head"),
        P(None, "head"),
        P(None, "head"),
        P(None, "head"),
        P(None, "head"),
        P(None, "head"),
        P("groups", None),
    )
    return jax.shard_map(
        per_device,
        mesh=mesh,
        in_specs=placed,
        out_specs=(P(("groups", "seq", "rep"), "head"), P(("groups", "seq", "rep"), "head")),
        check_vma=False,
    )
```

```python
import functools

import jax
import jax.numpy as jnp
from jax import lax
from jax.experimental import pallas as pl
from jax.experimental.pallas import tpu as pltpu
from jax.sharding import PartitionSpec as P

DH = 64
R = 256
SEG = 128
HALF = SEG // 2
LANES = 2 * DH
SCORE_SCALE = DH ** (-0.5)
LOG2E = 1.4426950408889634

VMEM_LIMIT = 40 << 20
COST = pl.CostEstimate(flops=1 << 20, bytes_accessed=1 << 10, transcendentals=0)

TURN = jax.ShapeDtypeStruct((4,), jnp.int32)

softcap = 5.0
epsilon = 1e-05

BF = jnp.bfloat16
F32 = jnp.float32


def dot(a, b, dims=((1,), (0,))):
    return lax.dot_general(a, b, (dims, ((), ())), preferred_element_type=F32)


def exp_capped(values, scale):
    return jnp.exp2((softcap * LOG2E) * jnp.tanh(values * (scale / softcap)))


def pass_turn(ids_ref, turn_ref):
    for i in range(4):
        turn_ref[i] = ids_ref[i]


def vmem():
    return pl.BlockSpec(memory_space=pltpu.VMEM)


def smem():
    return pl.BlockSpec(memory_space=pltpu.SMEM)


def head_norm(values, gain):
    out = []
    for at in range(0, values.shape[1], LANES):
        x = values[:, at : at + LANES]
        first = lane_is_first(x.shape)

        def mean(y):
            low = jnp.sum(jnp.where(first, y, 0.0), axis=-1, keepdims=True)
            high = jnp.sum(jnp.where(first, 0.0, y), axis=-1, keepdims=True)
            return jnp.where(first, low, high) * (1.0 / DH)

        centred = x - mean(x)
        spread = mean(centred * centred)
        out.append((centred * lax.rsqrt(spread + epsilon) * gain[:, at : at + LANES]).astype(BF))
    return jnp.concatenate(out, axis=1)


def token_norm(x, gain):
    x = x.astype(F32)
    centred = x - jnp.mean(x, axis=-1, keepdims=True)
    spread = jnp.mean(centred * centred, axis=-1, keepdims=True)
    return (centred * lax.rsqrt(spread + epsilon) * gain).astype(BF)


def edge_rows(near_ref):
    rows = near_ref.shape[0]
    columns = [slice(at, at + 2 * LANES) for at in range(0, near_ref.shape[1], 2 * LANES)]
    return [jnp.concatenate([near_ref[at, c] for c in columns], axis=0) for at in (slice(0, HALF), slice(rows - HALF, rows))]


def front_kernel(first, last, group, pairs, tile, *refs):
    ids_ref, refs = refs[0], list(refs[1:])
    if first:
        x_hbm, gain_ref = refs.pop(0), refs.pop(0)
    else:
        normed_ref = refs.pop(0)
    wk_hbm, wv_hbm, wp_hbm, dual_ref = refs[:4]
    refs = refs[4:]
    earlier = [refs.pop(0) for _ in range(group)] if last else []
    out = refs.pop(0)
    if first:
        normed_ref = out
    near_ref, keep_ref, send_ref, edge_ref, turn_ref = refs[:5]
    refs = refs[5:]
    pass_turn(ids_ref, turn_ref)
    raw_ref, p_ref, wk_ref, wv_ref, wp_ref, sem = refs[:6]
    if first:
        x_ref, gain_hbm, dual_hbm = refs[6], gain_ref, dual_ref
        gain_ref, dual_ref = refs[7:]
    rows = normed_ref.shape[0]
    width = pairs * LANES
    chunks = rows // tile
    own = pl.ds(group * width, width)

    def copy(source, target, slot):
        made = pltpu.make_async_copy(source, target, sem.at[slot])
        made.start()
        return made

    def token_copy(i):
        at = pl.ds(i * tile, tile)
        return copy(x_hbm.at[at, :], x_ref.at[at, :], i)

    token_copies = [token_copy(0)] if first else []
    if first:
        gain_copy = copy(gain_hbm, gain_ref, chunks + 2 + pairs)
        dual_copy = copy(dual_hbm, dual_ref, chunks + 3 + pairs)
    key_copy = copy(wk_hbm.at[:, own], wk_ref, chunks)
    value_copy = copy(wv_hbm.at[:, own], wv_ref, chunks + 1)
    proj_copies = []
    for p in range(pairs):
        cols = pl.ds((group * pairs + p) * 2 * R, 2 * R)
        proj_copies.append(copy(wp_hbm.at[:, cols], wp_ref.at[:, pl.ds(p * 2 * R, 2 * R)], chunks + 2 + p))
        if first and p == 0:
            token_copies += [token_copy(i) for i in range(1, chunks)]
    for i in range(chunks):
        at = pl.ds(i * tile, tile)
        if first:
            token_copies[i].wait()
            if i == 0:
                gain_copy.wait()
                dual_copy.wait()
            normed_ref[at, :] = token_norm(x_ref[at, :], gain_ref[...])
        normed = normed_ref[at, :]
        if i == 0:
            key_copy.wait()
            value_copy.wait()
        key = dot(normed, wk_ref[...])
        value = dot(normed, wv_ref[...])
        for p in range(pairs):
            cols = slice(p * LANES, (p + 1) * LANES)
            raw = jnp.concatenate([key[:, cols], value[:, cols]], axis=1).astype(BF)
            raw_ref[2 * p * LANES : 2 * (p + 1) * LANES, at] = raw.T
        for p in range(pairs):
            cols = slice(2 * p * R, 2 * (p + 1) * R)
            if i == 0:
                proj_copies[p].wait()
            p_ref[at, cols] = exp_capped(dot(normed, wp_ref[:, cols]), 1.0).astype(BF)
        near_ref[at, :width] = head_norm(key, dual_ref[0:1, group * width : (group + 1) * width])
        near_ref[at, width:] = head_norm(value, dual_ref[1:2, group * width : (group + 1) * width])
    total = []
    for p in range(pairs):
        full = dot(raw_ref[2 * p * LANES : 2 * (p + 1) * LANES, :], p_ref[:, 2 * p * R : 2 * (p + 1) * R])
        for part in range(4):
            head = part % 2
            total.append(full[part * DH : (part + 1) * DH, head * R : (head + 1) * R])
    total = jnp.concatenate(total, axis=0).astype(BF)
    half = total.shape[0] // 2
    mine = ids_ref[0] == 0
    keep_ref[...] = jnp.where(mine, total[:half], total[half:])
    send_ref[:half, :] = jnp.where(mine, total[half:], total[:half])
    head, tail = edge_rows(near_ref)
    edge = head.shape[0]
    if last:
        for i, ref in enumerate(earlier):
            before = jnp.where(mine, ref[edge:, :], ref[:edge, :])
            send_ref[half + i * edge : half + (i + 1) * edge, :] = before
            edge_ref[i * edge : (i + 1) * edge, :] = jnp.where(mine, ref[:edge, :], ref[edge:, :])
        send_ref[half + group * edge :, :] = jnp.where(mine, tail, head)
        edge_ref[group * edge :, :] = jnp.where(mine, head, tail)
    else:
        edge_ref[:edge, :] = head
        edge_ref[edge:, :] = tail


def in_hbm(values):
    return pltpu.with_memory_space_constraint(values, pltpu.HBM)


def front(first, last, group, pairs, ids, tokens, gain, wk, wv, wp, dual, earlier):
    rows, depth = tokens.shape
    width = pairs * LANES
    half = pairs * R // 2
    tile = min(256, rows)
    edge = (group + 1) * pairs * HALF if last else 0
    outs = [
        jax.ShapeDtypeStruct((rows, depth), BF),
        jax.ShapeDtypeStruct((rows, 2 * width), BF),
        jax.ShapeDtypeStruct((half, R), BF),
        jax.ShapeDtypeStruct((half + edge, R), BF),
        jax.ShapeDtypeStruct((edge if last else 2 * pairs * HALF, R), BF),
        TURN,
    ]
    hbm = pl.BlockSpec(memory_space=pltpu.HBM)
    earlier = earlier if last else []
    ins = [smem()] + [hbm if first else vmem()] * (2 if first else 1) + [hbm] * 3 + [hbm if first else vmem()]
    ins += [vmem()] * len(earlier)
    args = [ids] + ([in_hbm(tokens), in_hbm(gain)] if first else [tokens])
    args += [in_hbm(wk), in_hbm(wv), in_hbm(wp), in_hbm(dual) if first else dual] + earlier
    scratch = [
        pltpu.VMEM((2 * width, rows), BF),
        pltpu.VMEM((rows, 2 * pairs * R), BF),
        pltpu.VMEM((depth, width), BF),
        pltpu.VMEM((depth, width), BF),
        pltpu.VMEM((depth, 2 * pairs * R), BF),
        pltpu.SemaphoreType.DMA((rows // tile + 4 + pairs,)),
    ]
    if first:
        scratch += [pltpu.VMEM((rows, depth), BF), pltpu.VMEM((1, depth), F32), pltpu.VMEM(dual.shape, F32)]
    return pl.pallas_call(
        functools.partial(front_kernel, first, last, group, pairs, tile),
        input_output_aliases={} if first else {1: 0},
        in_specs=ins,
        out_specs=[vmem()] * (len(outs) - 1) + [smem()],
        out_shape=outs,
        scratch_shapes=scratch,
        compiler_params=pltpu.CompilerParams(vmem_limit_bytes=VMEM_LIMIT),
        cost_estimate=COST,
        name="front",
    )(*args)


def lane_is_first(shape):
    return lax.broadcasted_iota(jnp.int32, shape, 1) < DH


def stacked(q):
    first = lane_is_first(q.shape)
    zero = jnp.zeros_like(q)
    return jnp.concatenate([jnp.where(first, q, zero), jnp.where(first, zero, q)], axis=0)


def unstack(both):
    rows = both.shape[0] // 2
    first = lane_is_first((rows, LANES))
    return (
        jnp.where(first, both[:rows, :LANES], both[rows:, :LANES]),
        jnp.where(first, both[:rows, LANES:], both[rows:, LANES:]),
    )


def near_kernel(groups, pairs, *refs):
    ids_ref, normed_ref, core_ref, chip_ref, wq_ref = refs[:5]
    near_refs, refs = refs[5 : 5 + groups], refs[5 + groups :]
    q_refs, out_refs, (turn_ref, pad_ref) = refs[:groups], refs[groups : 2 * groups], refs[2 * groups :]
    rows = normed_ref.shape[0]
    width = pairs * LANES
    is_first = ids_ref[0] == 0
    row = lax.broadcasted_iota(jnp.int32, (2 * SEG, LANES), 0)
    ones = jnp.ones((2 * SEG, LANES), F32)
    has_prev = jnp.where(ids_ref[1] != 0, 1.0, 0.0)
    has_next = jnp.where(ids_ref[2] != 0, 1.0, 0.0)
    segments = rows // SEG
    offset = core_ref.shape[0] - chip_ref.shape[0]
    for g in range(groups):
        q_ref, near_ref, out_ref = q_refs[g], near_refs[g], out_refs[g]
        q_ref[...] = dot(normed_ref[...], wq_ref[:, g * width : (g + 1) * width]).astype(BF)
        pad_ref[HALF : HALF + rows, :] = near_ref[...]
        for c in range(pairs):
            at = (g * pairs + c) * HALF
            core = core_ref[offset + at : offset + at + HALF, :]
            chip = chip_ref[at : at + HALF, :]
            lanes = slice(2 * c * LANES, 2 * (c + 1) * LANES)
            pad_ref[0:HALF, lanes] = jnp.where(is_first, chip, core)
            pad_ref[HALF + rows :, lanes] = jnp.where(is_first, core, chip)
        for s in range(segments):
            count = ones
            if s == 0:
                count = jnp.where(row < HALF, has_prev, count)
            if s == segments - 1:
                count = jnp.where(row >= 3 * HALF, has_next, count)
            count = count.astype(BF)
            window = pl.ds(s * SEG, 2 * SEG)
            here = slice(s * SEG, (s + 1) * SEG)
            for p in range(pairs):
                cols = slice(p * LANES, (p + 1) * LANES)
                scores = dot(stacked(q_ref[here, cols]), pad_ref[window, cols], ((1,), (1,)))
                weights = exp_capped(scores, SCORE_SCALE).astype(BF)
                values = jnp.concatenate([pad_ref[window, width + p * LANES : width + (p + 1) * LANES], count], axis=1)
                top, bottom = unstack(dot(weights, values))
                out_ref[here, 2 * p * LANES : (2 * p + 1) * LANES] = top
                out_ref[here, (2 * p + 1) * LANES : (2 * p + 2) * LANES] = bottom
    pass_turn(ids_ref, turn_ref)


def near(pairs, ids, normed, core, chip, wq, near_pairs):
    rows = normed.shape[0]
    width = pairs * LANES
    groups = len(near_pairs)
    outs = pl.pallas_call(
        functools.partial(near_kernel, groups, pairs),
        in_specs=[smem()] + [vmem()] * (4 + groups),
        out_specs=[vmem()] * (2 * groups) + [smem()],
        out_shape=[jax.ShapeDtypeStruct((rows, width), BF)] * groups
        + [jax.ShapeDtypeStruct((rows, 2 * width), F32)] * groups
        + [TURN],
        scratch_shapes=[pltpu.VMEM((rows + SEG, 2 * width), BF)],
        compiler_params=pltpu.CompilerParams(vmem_limit_bytes=VMEM_LIMIT),
        cost_estimate=COST,
        name="near",
    )(ids, normed, core, chip, wq, *near_pairs)
    return list(zip(outs[:groups], outs[groups : 2 * groups])), outs[-1]


def far_kernel(pairs, group, block, spread, *refs):
    (ids_ref, q_ref, near_ref, mine_ref, other_ref, gains_ref, bounds_ref), refs = refs[:7], refs[7:]
    before, (out_ref, keep_ref, send_ref, turn_ref) = refs[:-4], refs[-4:]
    pass_turn(ids_ref, turn_ref)
    rows = q_ref.shape[0]
    width = pairs * LANES
    is_first = ids_ref[0] == 0
    top = jnp.where(is_first, mine_ref[...], other_ref[...])
    bottom = jnp.where(is_first, other_ref[...], mine_ref[...])
    total = jnp.concatenate([top, bottom], axis=0)
    ones = jnp.ones((LANES, R), BF)
    for p in range(pairs):
        cols = slice(p * LANES, (p + 1) * LANES)

        base = group * width + p * LANES
        gains = jnp.concatenate([gains_ref[:, base : base + LANES]] * 2, axis=0).T

        def land(kind):
            parts = []
            for h in range(2):
                at = p * R + kind * LANES + h * DH
                values = total[at : at + DH].astype(F32)
                centred = values - jnp.mean(values, axis=0, keepdims=True)
                spread = jnp.mean(centred * centred, axis=0, keepdims=True)
                gain = gains[h * DH : (h + 1) * DH, 2 + kind : 3 + kind]
                parts.append((centred * lax.rsqrt(spread + epsilon) * gain).astype(BF))
            return jnp.concatenate(parts, axis=0)

        keys = land(0)
        values = jnp.concatenate([land(1), ones], axis=0)
        for start in range(0, rows, block):
            q = stacked(q_ref[start : start + block, cols])
            weights = exp_capped(dot(q, keys), SCORE_SCALE).astype(BF)
            top, bottom = unstack(dot(weights, values, ((1,), (1,))))
            top = top + near_ref[start : start + block, 2 * p * LANES : (2 * p + 1) * LANES]
            bottom = bottom + near_ref[start : start + block, (2 * p + 1) * LANES : (2 * p + 2) * LANES]
            out_ref[start : start + block, cols] = (top / bottom).astype(BF)
    spans = bounds_ref.shape[1]
    position = ids_ref[3] + lax.broadcasted_iota(jnp.int32, (rows, spans), 0)
    member = (position >= bounds_ref[0:1, :]) & (position < bounds_ref[1:2, :])
    sums = dot(jnp.where(member, 1.0, 0.0).astype(BF), out_ref[...], ((0,), (0,)))
    count = spans // (2 * spread)
    even = jnp.concatenate([sums[2 * i * count : (2 * i + 1) * count] for i in range(spread)], axis=0)
    odd = jnp.concatenate([sums[(2 * i + 1) * count : (2 * i + 2) * count] for i in range(spread)], axis=0)
    lanes = slice(group * width, (group + 1) * width)
    if before:
        keep_ref[:, : group * width] = before[0][...]
        send_ref[:, : group * width] = before[1][...]
    keep_ref[:, lanes] = jnp.where(is_first, even, odd)
    send_ref[:, lanes] = jnp.where(is_first, odd, even).astype(BF)


def far(pairs, group, spread, ids, q, near_sums, mine, other, gains, bounds, before):
    rows = q.shape[0]
    width = pairs * LANES
    spans = bounds.shape[1]
    shape = (spans // 2, (group + 1) * width)
    return pl.pallas_call(
        functools.partial(far_kernel, pairs, group, 256, spread),
        in_specs=[smem()] + [vmem()] * (6 + len(before)),
        out_specs=[vmem()] * 3 + [smem()],
        out_shape=[
            jax.ShapeDtypeStruct((rows, width), BF),
            jax.ShapeDtypeStruct(shape, F32),
            jax.ShapeDtypeStruct(shape, BF),
            TURN,
        ],
        compiler_params=pltpu.CompilerParams(vmem_limit_bytes=VMEM_LIMIT),
        cost_estimate=COST,
        name="far",
    )(ids, q, near_sums, mine, other, gains, bounds, *before)


def out_kernel(count, *refs):
    ids_ref, refs = refs[0], refs[1:]
    tokens, (weight_ref, *acc), out_ref = refs[:count], refs[count:-1], refs[-1]
    rows, width = tokens[0].shape
    for start in range(0, rows, 256):
        at = slice(start, start + 256)
        total = acc[0][at, :] if acc else None
        for j in range(count):
            weight = weight_ref[pl.ds(pl.multiple_of(ids_ref[j] * width, width), width), :]
            term = dot(tokens[j][at, :], weight)
            total = term if total is None else total + term
        out_ref[at, :] = total.astype(out_ref.dtype)


def out_part(parts, index, weight, acc, dtype):
    count = len(parts)
    rows, width = parts[0].shape
    columns = weight.shape[1]
    extra = [] if acc is None else [acc]
    return pl.pallas_call(
        functools.partial(out_kernel, count),
        in_specs=[smem()] + [vmem()] * (count + 1 + len(extra)),
        out_specs=vmem(),
        out_shape=jax.ShapeDtypeStruct((rows, columns), dtype),
        compiler_params=pltpu.CompilerParams(vmem_limit_bytes=VMEM_LIMIT),
        cost_estimate=COST,
        name="out",
    )(index, *parts, weight, *extra)


def swap(values, axis, step):
    count = lax.axis_size(axis)
    return lax.ppermute(values, axis, [(i, i ^ step) for i in range(count)])


def add(a, b):
    return (a.astype(F32) + b.astype(F32)).astype(BF)


def steps_of(axis):
    step = 1
    while step < lax.axis_size(axis):
        yield step
        step *= 2


def per_device(
    book_tokens,
    norm_gain,
    query_weight,
    key_weight,
    value_weight,
    proj_weight,
    dual_gains,
    out_weight,
    span_bounds,
):
    rows = book_tokens.shape[0]
    seq_devices = lax.axis_size(("seq", "rep"))
    seq_index = lax.axis_index(("seq", "rep"))
    head_devices = lax.axis_size("head")
    head_index = lax.axis_index("head")
    first_row = seq_index * rows
    all_pairs = query_weight.shape[1] // LANES
    groups = 2 if all_pairs % 2 == 0 else 1
    pairs = all_pairs // groups
    ids = jnp.stack(
        [lax.axis_index("rep"), (seq_index > 0).astype(jnp.int32), (seq_index < seq_devices - 1).astype(jnp.int32), first_row]
    ).astype(jnp.int32)
    gain = norm_gain[None, :]
    bounds = span_bounds.T

    both = ("seq", "rep")
    chips = [(i, i + 1) for i in range(1, seq_devices - 1, 2)]
    chips = chips + [(b, a) for a, b in chips]
    steps = list(steps_of("seq"))
    tie = lax.optimization_barrier

    fronts, mine, normed = [], [], book_tokens
    turn = ids
    for g in range(groups):
        last = g == groups - 1
        normed, *outs, turn = front(g == 0, last, g, pairs, turn, normed, gain, key_weight, value_weight, proj_weight,
                                    dual_gains, [f[3] for f in fronts])
        fronts.append(outs)
        core = swap(outs[2], "rep", 1)
        if last:
            chip = lax.ppermute(outs[3], both, chips)
            for f in range(g):
                for step in steps[:-1]:
                    got, turn = tie((swap(mine[f], "seq", step), turn))
                    mine[f] = add(mine[f], got)
                mine[f], turn = tie((mine[f], turn))
        got, turn = tie((core[: outs[1].shape[0]], turn))
        mine.append(add(outs[1], got))
        mine[g], turn = tie((mine[g], turn))

    nears, turn = near(pairs, turn, normed, core, chip, query_weight, [f[0] for f in fronts])
    got, turn = tie((swap(mine[-1], "seq", steps[0]), turn))
    mine[-1] = add(mine[-1], got)
    for step in steps[1:-1]:
        mine[-1] = add(mine[-1], swap(mine[-1], "seq", step))
    mine[-1], turn = tie((mine[-1], turn))

    spread = lax.axis_size("seq")
    outs, before = [], ()
    for g in range(groups):
        got, turn = tie((swap(mine[g], "seq", steps[-1]), turn))
        total = add(mine[g], got)
        q, near_sums = nears[g]
        out, *before, turn = far(pairs, g, spread, turn, q, near_sums, total, swap(total, "rep", 1), dual_gains,
                                 bounds, before)
        outs.append(out)

    own_index = [head_index * groups + g for g in range(groups)]
    others, other_index = [], []
    for g in range(groups):
        for k in range(1, head_devices):
            others.append(lax.ppermute(outs[g], "head", [(i, (i + k) % head_devices) for i in range(head_devices)]))
            other_index.append(lax.rem(head_index - k + head_devices, head_devices) * groups + g)
    early = len(others) - (head_devices - 1)
    parts = outs + others[:early]
    index = jnp.stack(own_index + other_index[:early]).astype(jnp.int32)
    acc = out_part(parts, index, out_weight, None, F32)
    index = jnp.stack(other_index[early:]).astype(jnp.int32)
    attended = out_part(others[early:], index, out_weight, acc, BF)

    keep, send = before
    sums = keep + swap(send, "rep", 1).astype(F32)
    span_rows = sums.shape[0] // spread
    place = lax.axis_index("seq")
    own = lax.dynamic_slice_in_dim(sums, place * span_rows, span_rows, 0)
    for k in range(1, spread):
        target = lax.rem(place + k, spread)
        piece = lax.dynamic_slice_in_dim(sums, target * span_rows, span_rows, 0).astype(BF)
        own = own + lax.ppermute(piece, "seq", [(i, (i + k) % spread) for i in range(spread)]).astype(F32)
    own_bounds = lax.dynamic_slice_in_dim(span_bounds, seq_index * span_rows, span_rows, 0)
    counts = (own_bounds[:, 1] - own_bounds[:, 0]).astype(F32)
    own = (own / counts[:, None]).astype(BF)
    width = own.shape[1]
    spread = [own] + [
        lax.ppermute(own, "head", [(i, (i + k) % head_devices) for i in range(head_devices)])
        for k in range(1, head_devices)
    ]
    pooled = None
    for k, values in enumerate(spread):
        source = lax.rem(head_index - k + head_devices, head_devices)
        weight = lax.dynamic_slice_in_dim(out_weight, source * width, width, 0)
        term = jnp.dot(values, weight, preferred_element_type=F32)
        pooled = term if pooled is None else pooled + term
    return (attended, pooled)


def solution(mesh):
    placed = (
        P(("groups", "seq", "rep"), None),
        P(),
        P(None, "head"),
        P(None, "head"),
        P(None, "head"),
        P(None, "head"),
        P(None, "head"),
        P(None, "head"),
        P("groups", None),
    )
    return jax.shard_map(
        per_device,
        mesh=mesh,
        in_specs=placed,
        out_specs=(P(("groups", "seq", "rep"), "head"), P(("groups", "seq", "rep"), "head")),
        check_vma=False,
    )
```

```python
import functools

import jax
import jax.numpy as jnp
from jax import lax
from jax.experimental import pallas as pl
from jax.experimental.pallas import tpu as pltpu
from jax.sharding import PartitionSpec as P

DH = 64
R = 256
SEG = 128
HALF = SEG // 2
LANES = 2 * DH
SCORE_SCALE = DH ** (-0.5)
LOG2E = 1.4426950408889634

VMEM_LIMIT = 40 << 20
COST = pl.CostEstimate(flops=1 << 20, bytes_accessed=1 << 10, transcendentals=0)

TURN = jax.ShapeDtypeStruct((4,), jnp.int32)

softcap = 5.0
epsilon = 1e-05

BF = jnp.bfloat16
F32 = jnp.float32


def dot(a, b, dims=((1,), (0,))):
    return lax.dot_general(a, b, (dims, ((), ())), preferred_element_type=F32)


def exp_capped(values, scale):
    return jnp.exp2((softcap * LOG2E) * jnp.tanh(values * (scale / softcap)))


def pass_turn(ids_ref, turn_ref):
    for i in range(4):
        turn_ref[i] = ids_ref[i]


def vmem():
    return pl.BlockSpec(memory_space=pltpu.VMEM)


def smem():
    return pl.BlockSpec(memory_space=pltpu.SMEM)


def head_norm(values, gain):
    out = []
    for at in range(0, values.shape[1], LANES):
        x = values[:, at : at + LANES]
        first = lane_is_first(x.shape)

        def mean(y):
            low = jnp.sum(jnp.where(first, y, 0.0), axis=-1, keepdims=True)
            high = jnp.sum(jnp.where(first, 0.0, y), axis=-1, keepdims=True)
            return jnp.where(first, low, high) * (1.0 / DH)

        centred = x - mean(x)
        spread = mean(centred * centred)
        out.append((centred * lax.rsqrt(spread + epsilon) * gain[:, at : at + LANES]).astype(BF))
    return jnp.concatenate(out, axis=1)


def token_norm(x, gain):
    x = x.astype(F32)
    centred = x - jnp.mean(x, axis=-1, keepdims=True)
    spread = jnp.mean(centred * centred, axis=-1, keepdims=True)
    return (centred * lax.rsqrt(spread + epsilon) * gain).astype(BF)


def edge_rows(near_ref):
    rows = near_ref.shape[0]
    columns = [slice(at, at + 2 * LANES) for at in range(0, near_ref.shape[1], 2 * LANES)]
    return [jnp.concatenate([near_ref[at, c] for c in columns], axis=0) for at in (slice(0, HALF), slice(rows - HALF, rows))]


def front_kernel(first, last, group, pairs, tile, *refs):
    ids_ref, refs = refs[0], list(refs[1:])
    if first:
        x_hbm, gain_ref = refs.pop(0), refs.pop(0)
    else:
        normed_ref = refs.pop(0)
    wk_hbm, wv_hbm, wp_hbm, dual_ref = refs[:4]
    refs = refs[4:]
    earlier = [refs.pop(0) for _ in range(group)] if last else []
    out = refs.pop(0)
    if first:
        normed_ref = out
    near_ref, keep_ref, send_ref, edge_ref, turn_ref = refs[:5]
    refs = refs[5:]
    pass_turn(ids_ref, turn_ref)
    raw_ref, p_ref, wk_ref, wv_ref, wp_ref, sem = refs[:6]
    if first:
        x_ref, gain_hbm, dual_hbm = refs[6], gain_ref, dual_ref
        gain_ref, dual_ref = refs[7:]
    rows = normed_ref.shape[0]
    width = pairs * LANES
    chunks = rows // tile
    own = pl.ds(group * width, width)

    def copy(source, target, slot):
        made = pltpu.make_async_copy(source, target, sem.at[slot])
        made.start()
        return made

    def token_copy(i):
        at = pl.ds(i * tile, tile)
        return copy(x_hbm.at[at, :], x_ref.at[at, :], i)

    token_copies = [token_copy(0)] if first else []
    if first:
        gain_copy = copy(gain_hbm, gain_ref, chunks + 2 + pairs)
        dual_copy = copy(dual_hbm, dual_ref, chunks + 3 + pairs)
    key_copy = copy(wk_hbm.at[:, own], wk_ref, chunks)
    value_copy = copy(wv_hbm.at[:, own], wv_ref, chunks + 1)
    proj_copies = []
    for p in range(pairs):
        cols = pl.ds((group * pairs + p) * 2 * R, 2 * R)
        proj_copies.append(copy(wp_hbm.at[:, cols], wp_ref.at[:, pl.ds(p * 2 * R, 2 * R)], chunks + 2 + p))
        if first and p == 0:
            token_copies += [token_copy(i) for i in range(1, chunks)]
    for i in range(chunks):
        at = pl.ds(i * tile, tile)
        if first:
            token_copies[i].wait()
            if i == 0:
                gain_copy.wait()
                dual_copy.wait()
            normed_ref[at, :] = token_norm(x_ref[at, :], gain_ref[...])
        normed = normed_ref[at, :]
        if i == 0:
            key_copy.wait()
            value_copy.wait()
        key = dot(normed, wk_ref[...])
        value = dot(normed, wv_ref[...])
        for p in range(pairs):
            cols = slice(p * LANES, (p + 1) * LANES)
            raw = jnp.concatenate([key[:, cols], value[:, cols]], axis=1).astype(BF)
            raw_ref[2 * p * LANES : 2 * (p + 1) * LANES, at] = raw.T
        for p in range(pairs):
            cols = slice(2 * p * R, 2 * (p + 1) * R)
            if i == 0:
                proj_copies[p].wait()
            p_ref[at, cols] = exp_capped(dot(normed, wp_ref[:, cols]), 1.0).astype(BF)
        near_ref[at, :width] = head_norm(key, dual_ref[0:1, group * width : (group + 1) * width])
        near_ref[at, width:] = head_norm(value, dual_ref[1:2, group * width : (group + 1) * width])
    total = []
    for p in range(pairs):
        full = dot(raw_ref[2 * p * LANES : 2 * (p + 1) * LANES, :], p_ref[:, 2 * p * R : 2 * (p + 1) * R])
        for part in range(4):
            head = part % 2
            total.append(full[part * DH : (part + 1) * DH, head * R : (head + 1) * R])
    total = jnp.concatenate(total, axis=0).astype(BF)
    half = total.shape[0] // 2
    mine = ids_ref[0] == 0
    keep_ref[...] = jnp.where(mine, total[:half], total[half:])
    send_ref[:half, :] = jnp.where(mine, total[half:], total[:half])
    head, tail = edge_rows(near_ref)
    edge = head.shape[0]
    if last:
        for i, ref in enumerate(earlier):
            before = jnp.where(mine, ref[edge:, :], ref[:edge, :])
            send_ref[half + i * edge : half + (i + 1) * edge, :] = before
            edge_ref[i * edge : (i + 1) * edge, :] = jnp.where(mine, ref[:edge, :], ref[edge:, :])
        send_ref[half + group * edge :, :] = jnp.where(mine, tail, head)
        edge_ref[group * edge :, :] = jnp.where(mine, head, tail)
    else:
        edge_ref[:edge, :] = head
        edge_ref[edge:, :] = tail


def in_hbm(values):
    return pltpu.with_memory_space_constraint(values, pltpu.HBM)


def front(first, last, group, pairs, ids, tokens, gain, wk, wv, wp, dual, earlier):
    rows, depth = tokens.shape
    width = pairs * LANES
    half = pairs * R // 2
    tile = min(256, rows)
    edge = (group + 1) * pairs * HALF if last else 0
    outs = [
        jax.ShapeDtypeStruct((rows, depth), BF),
        jax.ShapeDtypeStruct((rows, 2 * width), BF),
        jax.ShapeDtypeStruct((half, R), BF),
        jax.ShapeDtypeStruct((half + edge, R), BF),
        jax.ShapeDtypeStruct((edge if last else 2 * pairs * HALF, R), BF),
        TURN,
    ]
    hbm = pl.BlockSpec(memory_space=pltpu.HBM)
    earlier = earlier if last else []
    ins = [smem()] + [hbm if first else vmem()] * (2 if first else 1) + [hbm] * 3 + [hbm if first else vmem()]
    ins += [vmem()] * len(earlier)
    args = [ids] + ([in_hbm(tokens), in_hbm(gain)] if first else [tokens])
    args += [in_hbm(wk), in_hbm(wv), in_hbm(wp), in_hbm(dual) if first else dual] + earlier
    scratch = [
        pltpu.VMEM((2 * width, rows), BF),
        pltpu.VMEM((rows, 2 * pairs * R), BF),
        pltpu.VMEM((depth, width), BF),
        pltpu.VMEM((depth, width), BF),
        pltpu.VMEM((depth, 2 * pairs * R), BF),
        pltpu.SemaphoreType.DMA((rows // tile + 4 + pairs,)),
    ]
    if first:
        scratch += [pltpu.VMEM((rows, depth), BF), pltpu.VMEM((1, depth), F32), pltpu.VMEM(dual.shape, F32)]
    return pl.pallas_call(
        functools.partial(front_kernel, first, last, group, pairs, tile),
        input_output_aliases={} if first else {1: 0},
        in_specs=ins,
        out_specs=[vmem()] * (len(outs) - 1) + [smem()],
        out_shape=outs,
        scratch_shapes=scratch,
        compiler_params=pltpu.CompilerParams(vmem_limit_bytes=VMEM_LIMIT),
        cost_estimate=COST,
        name="front",
    )(*args)


def lane_is_first(shape):
    return lax.broadcasted_iota(jnp.int32, shape, 1) < DH


def stacked(q):
    first = lane_is_first(q.shape)
    zero = jnp.zeros_like(q)
    return jnp.concatenate([jnp.where(first, q, zero), jnp.where(first, zero, q)], axis=0)


def unstack(both):
    rows = both.shape[0] // 2
    first = lane_is_first((rows, LANES))
    return (
        jnp.where(first, both[:rows, :LANES], both[rows:, :LANES]),
        jnp.where(first, both[:rows, LANES:], both[rows:, LANES:]),
    )


def near_kernel(groups, pairs, *refs):
    ids_ref, normed_ref, core_ref, chip_ref, wq_ref = refs[:5]
    near_refs, refs = refs[5 : 5 + groups], refs[5 + groups :]
    q_refs, out_refs, (turn_ref, pad_ref) = refs[:groups], refs[groups : 2 * groups], refs[2 * groups :]
    rows = normed_ref.shape[0]
    width = pairs * LANES
    is_first = ids_ref[0] == 0
    row = lax.broadcasted_iota(jnp.int32, (2 * SEG, LANES), 0)
    ones = jnp.ones((2 * SEG, LANES), F32)
    has_prev = jnp.where(ids_ref[1] != 0, 1.0, 0.0)
    has_next = jnp.where(ids_ref[2] != 0, 1.0, 0.0)
    segments = rows // SEG
    offset = core_ref.shape[0] - chip_ref.shape[0]
    for g in range(groups):
        q_ref, near_ref, out_ref = q_refs[g], near_refs[g], out_refs[g]
        q_ref[...] = dot(normed_ref[...], wq_ref[:, g * width : (g + 1) * width]).astype(BF)
        pad_ref[HALF : HALF + rows, :] = near_ref[...]
        for c in range(pairs):
            at = (g * pairs + c) * HALF
            core = core_ref[offset + at : offset + at + HALF, :]
            chip = chip_ref[at : at + HALF, :]
            lanes = slice(2 * c * LANES, 2 * (c + 1) * LANES)
            pad_ref[0:HALF, lanes] = jnp.where(is_first, chip, core)
            pad_ref[HALF + rows :, lanes] = jnp.where(is_first, core, chip)
        for s in range(segments):
            count = ones
            if s == 0:
                count = jnp.where(row < HALF, has_prev, count)
            if s == segments - 1:
                count = jnp.where(row >= 3 * HALF, has_next, count)
            count = count.astype(BF)
            window = pl.ds(s * SEG, 2 * SEG)
            here = slice(s * SEG, (s + 1) * SEG)
            for p in range(pairs):
                cols = slice(p * LANES, (p + 1) * LANES)
                scores = dot(stacked(q_ref[here, cols]), pad_ref[window, cols], ((1,), (1,)))
                weights = exp_capped(scores, SCORE_SCALE).astype(BF)
                values = jnp.concatenate([pad_ref[window, width + p * LANES : width + (p + 1) * LANES], count], axis=1)
                top, bottom = unstack(dot(weights, values))
                out_ref[here, 2 * p * LANES : (2 * p + 1) * LANES] = top
                out_ref[here, (2 * p + 1) * LANES : (2 * p + 2) * LANES] = bottom
    pass_turn(ids_ref, turn_ref)


def near(pairs, ids, normed, core, chip, wq, near_pairs):
    rows = normed.shape[0]
    width = pairs * LANES
    groups = len(near_pairs)
    outs = pl.pallas_call(
        functools.partial(near_kernel, groups, pairs),
        in_specs=[smem()] + [vmem()] * (4 + groups),
        out_specs=[vmem()] * (2 * groups) + [smem()],
        out_shape=[jax.ShapeDtypeStruct((rows, width), BF)] * groups
        + [jax.ShapeDtypeStruct((rows, 2 * width), F32)] * groups
        + [TURN],
        scratch_shapes=[pltpu.VMEM((rows + SEG, 2 * width), BF)],
        compiler_params=pltpu.CompilerParams(vmem_limit_bytes=VMEM_LIMIT),
        cost_estimate=COST,
        name="near",
    )(ids, normed, core, chip, wq, *near_pairs)
    return list(zip(outs[:groups], outs[groups : 2 * groups])), outs[-1]


def far_kernel(pairs, group, block, spread, *refs):
    (ids_ref, q_ref, near_ref, mine_ref, other_ref, gains_ref, bounds_ref), refs = refs[:7], refs[7:]
    before, (out_ref, keep_ref, send_ref, turn_ref) = refs[:-4], refs[-4:]
    pass_turn(ids_ref, turn_ref)
    rows = q_ref.shape[0]
    width = pairs * LANES
    is_first = ids_ref[0] == 0
    top = jnp.where(is_first, mine_ref[...], other_ref[...])
    bottom = jnp.where(is_first, other_ref[...], mine_ref[...])
    total = jnp.concatenate([top, bottom], axis=0)
    ones = jnp.ones((LANES, R), BF)
    for p in range(pairs):
        cols = slice(p * LANES, (p + 1) * LANES)

        base = group * width + p * LANES
        gains = jnp.concatenate([gains_ref[:, base : base + LANES]] * 2, axis=0).T

        def land(kind):
            parts = []
            for h in range(2):
                at = p * R + kind * LANES + h * DH
                values = total[at : at + DH].astype(F32)
                centred = values - jnp.mean(values, axis=0, keepdims=True)
                spread = jnp.mean(centred * centred, axis=0, keepdims=True)
                gain = gains[h * DH : (h + 1) * DH, 2 + kind : 3 + kind]
                parts.append((centred * lax.rsqrt(spread + epsilon) * gain).astype(BF))
            return jnp.concatenate(parts, axis=0)

        keys = land(0)
        values = jnp.concatenate([land(1), ones], axis=0)
        for start in range(0, rows, block):
            q = stacked(q_ref[start : start + block, cols])
            weights = exp_capped(dot(q, keys), SCORE_SCALE).astype(BF)
            top, bottom = unstack(dot(weights, values, ((1,), (1,))))
            top = top + near_ref[start : start + block, 2 * p * LANES : (2 * p + 1) * LANES]
            bottom = bottom + near_ref[start : start + block, (2 * p + 1) * LANES : (2 * p + 2) * LANES]
            out_ref[start : start + block, cols] = (top / bottom).astype(BF)
    spans = bounds_ref.shape[1]
    position = ids_ref[3] + lax.broadcasted_iota(jnp.int32, (rows, spans), 0)
    member = (position >= bounds_ref[0:1, :]) & (position < bounds_ref[1:2, :])
    sums = dot(jnp.where(member, 1.0, 0.0).astype(BF), out_ref[...], ((0,), (0,)))
    count = spans // (2 * spread)
    even = jnp.concatenate([sums[2 * i * count : (2 * i + 1) * count] for i in range(spread)], axis=0)
    odd = jnp.concatenate([sums[(2 * i + 1) * count : (2 * i + 2) * count] for i in range(spread)], axis=0)
    lanes = slice(group * width, (group + 1) * width)
    if before:
        keep_ref[:, : group * width] = before[0][...]
        send_ref[:, : group * width] = before[1][...]
    keep_ref[:, lanes] = jnp.where(is_first, even, odd)
    send_ref[:, lanes] = jnp.where(is_first, odd, even).astype(BF)


def far(pairs, group, spread, ids, q, near_sums, mine, other, gains, bounds, before):
    rows = q.shape[0]
    width = pairs * LANES
    spans = bounds.shape[1]
    shape = (spans // 2, (group + 1) * width)
    return pl.pallas_call(
        functools.partial(far_kernel, pairs, group, 256, spread),
        in_specs=[smem()] + [vmem()] * (6 + len(before)),
        out_specs=[vmem()] * 3 + [smem()],
        out_shape=[
            jax.ShapeDtypeStruct((rows, width), BF),
            jax.ShapeDtypeStruct(shape, F32),
            jax.ShapeDtypeStruct(shape, BF),
            TURN,
        ],
        compiler_params=pltpu.CompilerParams(vmem_limit_bytes=VMEM_LIMIT),
        cost_estimate=COST,
        name="far",
    )(ids, q, near_sums, mine, other, gains, bounds, *before)


def out_kernel(count, spans, *refs):
    ids_ref, refs = refs[0], refs[1:]
    tokens, refs = refs[:count], refs[count:]
    pooled, refs = refs[:spans], refs[spans:]
    outs = refs[-2:] if spans else refs[-1:]
    weight_ref, *acc = refs[: -len(outs)]
    rows, width = tokens[0].shape

    def weight(j, size):
        return weight_ref[pl.ds(pl.multiple_of(ids_ref[j] * size, size), size), :]

    for start in range(0, rows, 256):
        at = slice(start, start + 256)
        total = acc[0][at, :] if acc else None
        for j in range(count):
            term = dot(tokens[j][at, :], weight(j, width))
            total = term if total is None else total + term
        outs[0][at, :] = total.astype(outs[0].dtype)
    if spans:
        outs[1][...] = sum(dot(ref[...], weight(count + k, ref.shape[1])) for k, ref in enumerate(pooled))


def out_part(parts, index, weight, acc, dtype, pooled=()):
    count = len(parts)
    rows = parts[0].shape[0]
    columns = weight.shape[1]
    extra = [] if acc is None else [acc]
    shapes = [jax.ShapeDtypeStruct((rows, columns), dtype)]
    shapes += [jax.ShapeDtypeStruct((pooled[0].shape[0], columns), F32)] if pooled else []
    return pl.pallas_call(
        functools.partial(out_kernel, count, len(pooled)),
        in_specs=[smem()] + [vmem()] * (count + len(pooled) + 1 + len(extra)),
        out_specs=[vmem()] * len(shapes),
        out_shape=shapes,
        compiler_params=pltpu.CompilerParams(vmem_limit_bytes=VMEM_LIMIT),
        cost_estimate=COST,
        name="out",
    )(index, *parts, *pooled, weight, *extra)


def pieces_kernel(ids_ref, keep_ref, got_ref, *out_refs):
    spread = len(out_refs)
    count = keep_ref.shape[0] // spread
    for k, ref in enumerate(out_refs):
        at = pl.ds(pl.multiple_of(lax.rem(ids_ref[0] + k, spread) * count, count), count)
        ref[...] = (keep_ref[at, :] + got_ref[at, :].astype(F32)).astype(ref.dtype)


def pool_pieces(place, keep, got, spread):
    count = keep.shape[0] // spread
    shape = (count, keep.shape[1])
    return pl.pallas_call(
        pieces_kernel,
        in_specs=[smem(), vmem(), vmem()],
        out_specs=[vmem()] * spread,
        out_shape=[jax.ShapeDtypeStruct(shape, F32)] + [jax.ShapeDtypeStruct(shape, BF)] * (spread - 1),
        compiler_params=pltpu.CompilerParams(vmem_limit_bytes=VMEM_LIMIT),
        cost_estimate=COST,
        name="pool_pieces",
    )(place, keep, got)


def own_kernel(ids_ref, bounds_ref, own_ref, *refs):
    total = own_ref[...]
    for ref in refs[:-1]:
        total = total + ref[...].astype(F32)
    count = total.shape[0]
    rows = [
        total[i : i + 1] / (bounds_ref[1, ids_ref[0] + i] - bounds_ref[0, ids_ref[0] + i]).astype(F32)
        for i in range(count)
    ]
    refs[-1][...] = jnp.concatenate(rows, axis=0).astype(BF)


def pool_own(place, bounds, own, others):
    return pl.pallas_call(
        own_kernel,
        in_specs=[smem(), smem()] + [vmem()] * (1 + len(others)),
        out_specs=vmem(),
        out_shape=jax.ShapeDtypeStruct(own.shape, BF),
        compiler_params=pltpu.CompilerParams(vmem_limit_bytes=VMEM_LIMIT),
        cost_estimate=COST,
        name="pool_own",
    )(place, bounds, own, *others)


def swap(values, axis, step):
    count = lax.axis_size(axis)
    return lax.ppermute(values, axis, [(i, i ^ step) for i in range(count)])


def across_heads(values, step):
    count = lax.axis_size("head")
    return lax.ppermute(values, "head", [(i, (i + step) % count) for i in range(count)])


def add(a, b):
    return (a.astype(F32) + b.astype(F32)).astype(BF)


def add_kernel(a_ref, b_ref, out_ref):
    out_ref[...] = (a_ref[...].astype(F32) + b_ref[...].astype(F32)).astype(BF)


def add_call(a, b):
    return pl.pallas_call(
        add_kernel,
        in_specs=[vmem()] * 2,
        out_specs=vmem(),
        out_shape=jax.ShapeDtypeStruct(a.shape, BF),
        compiler_params=pltpu.CompilerParams(vmem_limit_bytes=VMEM_LIMIT),
        cost_estimate=COST,
        name="add",
    )(a, b)


def steps_of(axis):
    step = 1
    while step < lax.axis_size(axis):
        yield step
        step *= 2


def per_device(
    book_tokens,
    norm_gain,
    query_weight,
    key_weight,
    value_weight,
    proj_weight,
    dual_gains,
    out_weight,
    span_bounds,
):
    rows = book_tokens.shape[0]
    seq_devices = lax.axis_size(("seq", "rep"))
    seq_index = lax.axis_index(("seq", "rep"))
    head_devices = lax.axis_size("head")
    head_index = lax.axis_index("head")
    first_row = seq_index * rows
    all_pairs = query_weight.shape[1] // LANES
    groups = 2 if all_pairs % 2 == 0 else 1
    pairs = all_pairs // groups
    ids = jnp.stack(
        [lax.axis_index("rep"), (seq_index > 0).astype(jnp.int32), (seq_index < seq_devices - 1).astype(jnp.int32), first_row]
    ).astype(jnp.int32)
    gain = norm_gain[None, :]
    bounds = span_bounds.T

    both = ("seq", "rep")
    chips = [(i, i + 1) for i in range(1, seq_devices - 1, 2)]
    chips = chips + [(b, a) for a, b in chips]
    steps = list(steps_of("seq"))
    tie = lax.optimization_barrier

    fronts, mine, normed = [], [], book_tokens
    turn = ids
    for g in range(groups):
        last = g == groups - 1
        normed, *outs, turn = front(g == 0, last, g, pairs, turn, normed, gain, key_weight, value_weight, proj_weight,
                                    dual_gains, [f[3] for f in fronts])
        fronts.append(outs)
        core = swap(outs[2], "rep", 1)
        if last:
            chip = lax.ppermute(outs[3], both, chips)
            for f in range(g):
                for step in steps[:-1]:
                    got, turn = tie((swap(mine[f], "seq", step), turn))
                    mine[f] = add(mine[f], got)
                mine[f], turn = tie((mine[f], turn))
        got, turn = tie((core[: outs[1].shape[0]], turn))
        mine.append(add(outs[1], got))
        mine[g], turn = tie((mine[g], turn))

    nears, turn = near(pairs, turn, normed, core, chip, query_weight, [f[0] for f in fronts])
    got, turn = tie((swap(mine[-1], "seq", steps[0]), turn))
    mine[-1] = add(mine[-1], got)
    for step in steps[1:-1]:
        mine[-1] = add(mine[-1], swap(mine[-1], "seq", step))
    mine[-1], turn = tie((mine[-1], turn))

    spread = lax.axis_size("seq")
    outs, before = [], ()
    for g in range(groups):
        got, turn = tie((swap(mine[g], "seq", steps[-1]), turn))
        total = add_call(mine[g], got)
        q, near_sums = nears[g]
        out, *before, turn = far(pairs, g, spread, turn, q, near_sums, total, swap(total, "rep", 1), dual_gains,
                                 bounds, before)
        outs.append(out)

    own_index = [head_index * groups + g for g in range(groups)]
    others, other_index = [], []
    for g in range(groups):
        for k in range(1, head_devices):
            others.append(across_heads(outs[g], k))
            other_index.append(lax.rem(head_index - k + head_devices, head_devices) * groups + g)
    early = len(others) - (head_devices - 1)

    keep, send = before
    place = lax.axis_index("seq").astype(jnp.int32)[None]
    own, *pieces = pool_pieces(place, keep, swap(send, "rep", 1), spread)
    pieces = [
        lax.ppermute(piece, "seq", [(i, (i + k + 1) % spread) for i in range(spread)]) for k, piece in enumerate(pieces)
    ]
    own = pool_own((seq_index * own.shape[0]).astype(jnp.int32)[None], bounds, own, pieces)
    pooled = [own] + [across_heads(own, k) for k in range(1, head_devices)]
    pooled_index = [lax.rem(head_index - k + head_devices, head_devices) for k in range(head_devices)]

    parts = outs + others[:early]
    index = jnp.stack(own_index + other_index[:early]).astype(jnp.int32)
    (acc,) = out_part(parts, index, out_weight, None, F32)
    index = jnp.stack(other_index[early:] + pooled_index).astype(jnp.int32)
    return tuple(out_part(others[early:], index, out_weight, acc, BF, pooled))


def solution(mesh):
    placed = (
        P(("groups", "seq", "rep"), None),
        P(),
        P(None, "head"),
        P(None, "head"),
        P(None, "head"),
        P(None, "head"),
        P(None, "head"),
        P(None, "head"),
        P("groups", None),
    )
    return jax.shard_map(
        per_device,
        mesh=mesh,
        in_specs=placed,
        out_specs=(P(("groups", "seq", "rep"), "head"), P(("groups", "seq", "rep"), "head")),
        check_vma=False,
    )
```

```python
import functools

import jax
import jax.numpy as jnp
from jax import lax
from jax.experimental import pallas as pl
from jax.experimental.pallas import tpu as pltpu
from jax.sharding import PartitionSpec as P

DH = 64
R = 256
SEG = 128
HALF = SEG // 2
LANES = 2 * DH
SCORE_SCALE = DH ** (-0.5)
LOG2E = 1.4426950408889634

VMEM_LIMIT = 40 << 20
COST = pl.CostEstimate(flops=1 << 20, bytes_accessed=1 << 10, transcendentals=0)

TURN = jax.ShapeDtypeStruct((4,), jnp.int32)

softcap = 5.0
epsilon = 1e-05

BF = jnp.bfloat16
F32 = jnp.float32


def dot(a, b, dims=((1,), (0,))):
    return lax.dot_general(a, b, (dims, ((), ())), preferred_element_type=F32)


def exp_capped(values, scale):
    return jnp.exp2((softcap * LOG2E) * jnp.tanh(values * (scale / softcap)))


def pass_turn(ids_ref, turn_ref):
    for i in range(4):
        turn_ref[i] = ids_ref[i]


def vmem():
    return pl.BlockSpec(memory_space=pltpu.VMEM)


def smem():
    return pl.BlockSpec(memory_space=pltpu.SMEM)


def head_norm(values, gain):
    out = []
    for at in range(0, values.shape[1], LANES):
        x = values[:, at : at + LANES]
        first = lane_is_first(x.shape)

        def mean(y):
            low = jnp.sum(jnp.where(first, y, 0.0), axis=-1, keepdims=True)
            high = jnp.sum(jnp.where(first, 0.0, y), axis=-1, keepdims=True)
            return jnp.where(first, low, high) * (1.0 / DH)

        centred = x - mean(x)
        spread = mean(centred * centred)
        out.append((centred * lax.rsqrt(spread + epsilon) * gain[:, at : at + LANES]).astype(BF))
    return jnp.concatenate(out, axis=1)


def token_norm(x, gain):
    x = x.astype(F32)
    centred = x - jnp.mean(x, axis=-1, keepdims=True)
    spread = jnp.mean(centred * centred, axis=-1, keepdims=True)
    return (centred * lax.rsqrt(spread + epsilon) * gain).astype(BF)


def edge_rows(near_ref):
    rows = near_ref.shape[0]
    columns = [slice(at, at + 2 * LANES) for at in range(0, near_ref.shape[1], 2 * LANES)]
    return [jnp.concatenate([near_ref[at, c] for c in columns], axis=0) for at in (slice(0, HALF), slice(rows - HALF, rows))]


def front_kernel(first, last, group, pairs, tile, *refs):
    ids_ref, refs = refs[0], list(refs[1:])
    if first:
        x_hbm, gain_ref = refs.pop(0), refs.pop(0)
    else:
        normed_ref = refs.pop(0)
    wk_hbm, wv_hbm, wp_hbm, dual_ref = refs[:4]
    refs = refs[4:]
    earlier = [refs.pop(0) for _ in range(group)] if last else []
    out = refs.pop(0)
    if first:
        normed_ref = out
    near_ref, keep_ref, send_ref, edge_ref, turn_ref = refs[:5]
    refs = refs[5:]
    pass_turn(ids_ref, turn_ref)
    raw_ref, p_ref, wk_ref, wv_ref, wp_ref, sem = refs[:6]
    if first:
        x_ref, gain_hbm, dual_hbm = refs[6], gain_ref, dual_ref
        gain_ref, dual_ref = refs[7:]
    rows = normed_ref.shape[0]
    width = pairs * LANES
    chunks = rows // tile
    own = pl.ds(group * width, width)

    def copy(source, target, slot):
        made = pltpu.make_async_copy(source, target, sem.at[slot])
        made.start()
        return made

    def token_copy(i):
        at = pl.ds(i * tile, tile)
        return copy(x_hbm.at[at, :], x_ref.at[at, :], i)

    token_copies = [token_copy(0)] if first else []
    if first:
        gain_copy = copy(gain_hbm, gain_ref, chunks + 2 + pairs)
        dual_copy = copy(dual_hbm, dual_ref, chunks + 3 + pairs)
    key_copy = copy(wk_hbm.at[:, own], wk_ref, chunks)
    value_copy = copy(wv_hbm.at[:, own], wv_ref, chunks + 1)
    proj_copies = []
    for p in range(pairs):
        cols = pl.ds((group * pairs + p) * 2 * R, 2 * R)
        proj_copies.append(copy(wp_hbm.at[:, cols], wp_ref.at[:, pl.ds(p * 2 * R, 2 * R)], chunks + 2 + p))
        if first and p == 0:
            token_copies += [token_copy(i) for i in range(1, chunks)]
    for i in range(chunks):
        at = pl.ds(i * tile, tile)
        if first:
            token_copies[i].wait()
            if i == 0:
                gain_copy.wait()
                dual_copy.wait()
            normed_ref[at, :] = token_norm(x_ref[at, :], gain_ref[...])
        normed = normed_ref[at, :]
        if i == 0:
            key_copy.wait()
            value_copy.wait()
        key = dot(normed, wk_ref[...])
        value = dot(normed, wv_ref[...])
        for p in range(pairs):
            cols = slice(p * LANES, (p + 1) * LANES)
            raw = jnp.concatenate([key[:, cols], value[:, cols]], axis=1).astype(BF)
            raw_ref[2 * p * LANES : 2 * (p + 1) * LANES, at] = raw.T
        for p in range(pairs):
            cols = slice(2 * p * R, 2 * (p + 1) * R)
            if i == 0:
                proj_copies[p].wait()
            p_ref[at, cols] = exp_capped(dot(normed, wp_ref[:, cols]), 1.0).astype(BF)
        near_ref[at, :width] = head_norm(key, dual_ref[0:1, group * width : (group + 1) * width])
        near_ref[at, width:] = head_norm(value, dual_ref[1:2, group * width : (group + 1) * width])
    total = []
    for p in range(pairs):
        full = dot(raw_ref[2 * p * LANES : 2 * (p + 1) * LANES, :], p_ref[:, 2 * p * R : 2 * (p + 1) * R])
        for part in range(4):
            head = part % 2
            total.append(full[part * DH : (part + 1) * DH, head * R : (head + 1) * R])
    total = jnp.concatenate(total, axis=0).astype(BF)
    half = total.shape[0] // 2
    mine = ids_ref[0] == 0
    keep_ref[...] = jnp.where(mine, total[:half], total[half:])
    send_ref[:half, :] = jnp.where(mine, total[half:], total[:half])
    head, tail = edge_rows(near_ref)
    edge = head.shape[0]
    if last:
        for i, ref in enumerate(earlier):
            before = jnp.where(mine, ref[edge:, :], ref[:edge, :])
            send_ref[half + i * edge : half + (i + 1) * edge, :] = before
            edge_ref[i * edge : (i + 1) * edge, :] = jnp.where(mine, ref[:edge, :], ref[edge:, :])
        send_ref[half + group * edge :, :] = jnp.where(mine, tail, head)
        edge_ref[group * edge :, :] = jnp.where(mine, head, tail)
    else:
        edge_ref[:edge, :] = head
        edge_ref[edge:, :] = tail


def in_hbm(values):
    return pltpu.with_memory_space_constraint(values, pltpu.HBM)


def front(first, last, group, pairs, ids, tokens, gain, wk, wv, wp, dual, earlier):
    rows, depth = tokens.shape
    width = pairs * LANES
    half = pairs * R // 2
    tile = min(512 if first else 256, rows)
    edge = (group + 1) * pairs * HALF if last else 0
    outs = [
        jax.ShapeDtypeStruct((rows, depth), BF),
        jax.ShapeDtypeStruct((rows, 2 * width), BF),
        jax.ShapeDtypeStruct((half, R), BF),
        jax.ShapeDtypeStruct((half + edge, R), BF),
        jax.ShapeDtypeStruct((edge if last else 2 * pairs * HALF, R), BF),
        TURN,
    ]
    hbm = pl.BlockSpec(memory_space=pltpu.HBM)
    earlier = earlier if last else []
    ins = [smem()] + [hbm if first else vmem()] * (2 if first else 1) + [hbm] * 3 + [hbm if first else vmem()]
    ins += [vmem()] * len(earlier)
    args = [ids] + ([in_hbm(tokens), in_hbm(gain)] if first else [tokens])
    args += [in_hbm(wk), in_hbm(wv), in_hbm(wp), in_hbm(dual) if first else dual] + earlier
    scratch = [
        pltpu.VMEM((2 * width, rows), BF),
        pltpu.VMEM((rows, 2 * pairs * R), BF),
        pltpu.VMEM((depth, width), BF),
        pltpu.VMEM((depth, width), BF),
        pltpu.VMEM((depth, 2 * pairs * R), BF),
        pltpu.SemaphoreType.DMA((rows // tile + 4 + pairs,)),
    ]
    if first:
        scratch += [pltpu.VMEM((rows, depth), BF), pltpu.VMEM((1, depth), F32), pltpu.VMEM(dual.shape, F32)]
    return pl.pallas_call(
        functools.partial(front_kernel, first, last, group, pairs, tile),
        input_output_aliases={} if first else {1: 0},
        in_specs=ins,
        out_specs=[vmem()] * (len(outs) - 1) + [smem()],
        out_shape=outs,
        scratch_shapes=scratch,
        compiler_params=pltpu.CompilerParams(vmem_limit_bytes=VMEM_LIMIT),
        cost_estimate=COST,
        name="front",
    )(*args)


def lane_is_first(shape):
    return lax.broadcasted_iota(jnp.int32, shape, 1) < DH


def stacked(q):
    first = lane_is_first(q.shape)
    zero = jnp.zeros_like(q)
    return jnp.concatenate([jnp.where(first, q, zero), jnp.where(first, zero, q)], axis=0)


def unstack(both):
    rows = both.shape[0] // 2
    first = lane_is_first((rows, LANES))
    return (
        jnp.where(first, both[:rows, :LANES], both[rows:, :LANES]),
        jnp.where(first, both[:rows, LANES:], both[rows:, LANES:]),
    )


def near_kernel(pairs, group, ids_ref, tokens_ref, core_ref, chip_ref, wq_ref, near_ref,
                normed_ref, q_ref, out_ref, turn_ref, pad_ref):
    rows = normed_ref.shape[0]
    width = pairs * LANES
    is_first = ids_ref[0] == 0
    row = lax.broadcasted_iota(jnp.int32, (2 * SEG, LANES), 0)
    ones = jnp.ones((2 * SEG, LANES), F32)
    has_prev = jnp.where(ids_ref[1] != 0, 1.0, 0.0)
    has_next = jnp.where(ids_ref[2] != 0, 1.0, 0.0)
    segments = rows // SEG
    offset = core_ref.shape[0] - chip_ref.shape[0]
    q_ref[...] = dot(normed_ref[...], wq_ref[:, group * width : (group + 1) * width]).astype(BF)
    pad_ref[HALF : HALF + rows, :] = near_ref[...]
    for c in range(pairs):
        at = (group * pairs + c) * HALF
        core = core_ref[offset + at : offset + at + HALF, :]
        chip = chip_ref[at : at + HALF, :]
        lanes = slice(2 * c * LANES, 2 * (c + 1) * LANES)
        pad_ref[0:HALF, lanes] = jnp.where(is_first, chip, core)
        pad_ref[HALF + rows :, lanes] = jnp.where(is_first, core, chip)
    for s in range(segments):
        count = ones
        if s == 0:
            count = jnp.where(row < HALF, has_prev, count)
        if s == segments - 1:
            count = jnp.where(row >= 3 * HALF, has_next, count)
        count = count.astype(BF)
        window = pl.ds(s * SEG, 2 * SEG)
        here = slice(s * SEG, (s + 1) * SEG)
        for p in range(pairs):
            cols = slice(p * LANES, (p + 1) * LANES)
            scores = dot(stacked(q_ref[here, cols]), pad_ref[window, cols], ((1,), (1,)))
            weights = exp_capped(scores, SCORE_SCALE).astype(BF)
            values = jnp.concatenate([pad_ref[window, width + p * LANES : width + (p + 1) * LANES], count], axis=1)
            top, bottom = unstack(dot(weights, values))
            out_ref[here, 2 * p * LANES : (2 * p + 1) * LANES] = top
            out_ref[here, (2 * p + 1) * LANES : (2 * p + 2) * LANES] = bottom
    pass_turn(ids_ref, turn_ref)


def near(pairs, group, ids, normed, core, chip, wq, near_pairs):
    rows = normed.shape[0]
    width = pairs * LANES
    return pl.pallas_call(
        functools.partial(near_kernel, pairs, group),
        in_specs=[smem()] + [vmem()] * 5,
        out_specs=[vmem()] * 3 + [smem()],
        out_shape=[
            jax.ShapeDtypeStruct(normed.shape, BF),
            jax.ShapeDtypeStruct((rows, width), BF),
            jax.ShapeDtypeStruct((rows, 2 * width), F32),
            TURN,
        ],
        input_output_aliases={1: 0},
        scratch_shapes=[pltpu.VMEM((rows + SEG, 2 * width), BF)],
        compiler_params=pltpu.CompilerParams(vmem_limit_bytes=VMEM_LIMIT),
        cost_estimate=COST,
        name="near",
    )(ids, normed, core, chip, wq, near_pairs)


def far_kernel(pairs, group, block, spread, *refs):
    (ids_ref, q_ref, near_ref, mine_ref, other_ref, gains_ref, bounds_ref), refs = refs[:7], refs[7:]
    keep_ref, send_ref, turn_ref = refs[-3:]
    out_refs = refs[-3 - pairs : -3]
    before = refs[:2] if group else ()
    pass_turn(ids_ref, turn_ref)
    rows = q_ref.shape[0]
    width = pairs * LANES
    is_first = ids_ref[0] == 0
    top = jnp.where(is_first, mine_ref[...], other_ref[...])
    bottom = jnp.where(is_first, other_ref[...], mine_ref[...])
    total = jnp.concatenate([top, bottom], axis=0)
    ones = jnp.ones((LANES, R), BF)
    for p in range(pairs):
        cols = slice(p * LANES, (p + 1) * LANES)

        base = group * width + p * LANES
        gains = jnp.concatenate([gains_ref[:, base : base + LANES]] * 2, axis=0).T

        def land(kind):
            parts = []
            for h in range(2):
                at = p * R + kind * LANES + h * DH
                values = total[at : at + DH].astype(F32)
                centred = values - jnp.mean(values, axis=0, keepdims=True)
                spread = jnp.mean(centred * centred, axis=0, keepdims=True)
                gain = gains[h * DH : (h + 1) * DH, 2 + kind : 3 + kind]
                parts.append((centred * lax.rsqrt(spread + epsilon) * gain).astype(BF))
            return jnp.concatenate(parts, axis=0)

        keys = land(0)
        values = jnp.concatenate([land(1), ones], axis=0)
        for start in range(0, rows, block):
            q = stacked(q_ref[start : start + block, cols])
            weights = exp_capped(dot(q, keys), SCORE_SCALE).astype(BF)
            top, bottom = unstack(dot(weights, values, ((1,), (1,))))
            top = top + near_ref[start : start + block, 2 * p * LANES : (2 * p + 1) * LANES]
            bottom = bottom + near_ref[start : start + block, (2 * p + 1) * LANES : (2 * p + 2) * LANES]
            out_refs[p][start : start + block, :] = (top / bottom).astype(BF)
    spans = bounds_ref.shape[1]
    position = ids_ref[3] + lax.broadcasted_iota(jnp.int32, (rows, spans), 0)
    member = (position >= bounds_ref[0:1, :]) & (position < bounds_ref[1:2, :])
    outs = jnp.concatenate([ref[...] for ref in out_refs], axis=1)
    sums = dot(jnp.where(member, 1.0, 0.0).astype(BF), outs, ((0,), (0,)))
    count = spans // (2 * spread)
    even = jnp.concatenate([sums[2 * i * count : (2 * i + 1) * count] for i in range(spread)], axis=0)
    odd = jnp.concatenate([sums[(2 * i + 1) * count : (2 * i + 2) * count] for i in range(spread)], axis=0)
    lanes = slice(group * width, (group + 1) * width)
    if before:
        keep_ref[:, : group * width] = before[0][...]
        send_ref[:, : group * width] = before[1][...]
    keep_ref[:, lanes] = jnp.where(is_first, even, odd)
    send_ref[:, lanes] = jnp.where(is_first, odd, even).astype(BF)


def far(pairs, group, spread, ids, q, near_sums, mine, other, gains, bounds, before, arrived):
    rows = q.shape[0]
    width = pairs * LANES
    spans = bounds.shape[1]
    shape = (spans // 2, (group + 1) * width)
    return pl.pallas_call(
        functools.partial(far_kernel, pairs, group, 256, spread),
        in_specs=[smem()] + [vmem()] * (6 + len(before)) + [pl.BlockSpec(memory_space=pl.ANY)] * len(arrived),
        out_specs=[vmem()] * (2 + pairs) + [smem()],
        out_shape=[
            *[jax.ShapeDtypeStruct((rows, LANES), BF)] * pairs,
            jax.ShapeDtypeStruct(shape, F32),
            jax.ShapeDtypeStruct(shape, BF),
            TURN,
        ],
        compiler_params=pltpu.CompilerParams(vmem_limit_bytes=VMEM_LIMIT),
        cost_estimate=COST,
        name="far",
    )(ids, q, near_sums, mine, other, gains, bounds, *before, *arrived)


def out_kernel(count, pairs, spans, *refs):
    ids_ref, refs = refs[0], refs[1:]
    tokens, refs = [refs[j * pairs : (j + 1) * pairs] for j in range(count)], refs[count * pairs :]
    pooled, refs = refs[:spans], refs[spans:]
    *refs, turn_ref = refs
    turn_ref[0] = ids_ref[0]
    outs = refs[-2:] if spans else refs[-1:]
    weight_ref, *acc = refs[: -len(outs)]
    rows, width = tokens[0][0].shape[0], pairs * LANES

    def weight(j, size):
        return weight_ref[pl.ds(pl.multiple_of(ids_ref[j] * size, size), size), :]

    for start in range(0, rows, 256):
        at = slice(start, start + 256)
        total = acc[0][at, :] if acc else None
        for j in range(count):
            term = dot(jnp.concatenate([ref[at, :] for ref in tokens[j]], axis=1), weight(j, width))
            total = term if total is None else total + term
        outs[0][at, :] = total.astype(outs[0].dtype)
    if spans:
        outs[1][...] = sum(dot(ref[...], weight(count + k, ref.shape[1])) for k, ref in enumerate(pooled))


def out_part(parts, index, weight, acc, dtype, pooled=()):
    count = len(parts)
    pairs = len(parts[0])
    rows = parts[0][0].shape[0]
    columns = weight.shape[1]
    extra = [] if acc is None else [acc]
    shapes = [jax.ShapeDtypeStruct((rows, columns), dtype)]
    shapes += [jax.ShapeDtypeStruct((pooled[0].shape[0], columns), F32)] if pooled else []
    return pl.pallas_call(
        functools.partial(out_kernel, count, pairs, len(pooled)),
        in_specs=[smem()] + [vmem()] * (count * pairs + len(pooled) + 1 + len(extra)),
        out_specs=[vmem()] * len(shapes) + [smem()],
        out_shape=shapes + [jax.ShapeDtypeStruct((1,), jnp.int32)],
        compiler_params=pltpu.CompilerParams(vmem_limit_bytes=VMEM_LIMIT),
        cost_estimate=COST,
        name="out",
    )(index, *[piece for part in parts for piece in part], *pooled, weight, *extra)


def pieces_kernel(ids_ref, keep_ref, got_ref, *out_refs):
    spread = len(out_refs)
    count = keep_ref.shape[0] // spread
    for k, ref in enumerate(out_refs):
        at = pl.ds(pl.multiple_of(lax.rem(ids_ref[0] + k, spread) * count, count), count)
        ref[...] = (keep_ref[at, :] + got_ref[at, :].astype(F32)).astype(ref.dtype)


def pool_pieces(place, keep, got, spread):
    count = keep.shape[0] // spread
    shape = (count, keep.shape[1])
    return pl.pallas_call(
        pieces_kernel,
        in_specs=[smem(), vmem(), vmem()],
        out_specs=[vmem()] * spread,
        out_shape=[jax.ShapeDtypeStruct(shape, F32)] + [jax.ShapeDtypeStruct(shape, BF)] * (spread - 1),
        compiler_params=pltpu.CompilerParams(vmem_limit_bytes=VMEM_LIMIT),
        cost_estimate=COST,
        name="pool_pieces",
    )(place, keep, got)


def own_kernel(ids_ref, bounds_ref, own_ref, *refs):
    total = own_ref[...]
    for ref in refs[:-1]:
        total = total + ref[...].astype(F32)
    count = total.shape[0]
    rows = [
        total[i : i + 1] / (bounds_ref[1, ids_ref[0] + i] - bounds_ref[0, ids_ref[0] + i]).astype(F32)
        for i in range(count)
    ]
    refs[-1][...] = jnp.concatenate(rows, axis=0).astype(BF)


def pool_own(place, bounds, own, others):
    return pl.pallas_call(
        own_kernel,
        in_specs=[smem(), smem()] + [vmem()] * (1 + len(others)),
        out_specs=vmem(),
        out_shape=jax.ShapeDtypeStruct(own.shape, BF),
        compiler_params=pltpu.CompilerParams(vmem_limit_bytes=VMEM_LIMIT),
        cost_estimate=COST,
        name="pool_own",
    )(place, bounds, own, *others)


def swap(values, axis, step):
    count = lax.axis_size(axis)
    return lax.ppermute(values, axis, [(i, i ^ step) for i in range(count)])


def across_heads(values, step):
    count = lax.axis_size("head")
    return lax.ppermute(values, "head", [(i, (i + step) % count) for i in range(count)])


def add(a, b):
    return (a.astype(F32) + b.astype(F32)).astype(BF)


def add_kernel(a_ref, b_ref, out_ref):
    out_ref[...] = (a_ref[...].astype(F32) + b_ref[...].astype(F32)).astype(BF)


def add_call(a, b):
    return pl.pallas_call(
        add_kernel,
        in_specs=[vmem()] * 2,
        out_specs=vmem(),
        out_shape=jax.ShapeDtypeStruct(a.shape, BF),
        compiler_params=pltpu.CompilerParams(vmem_limit_bytes=VMEM_LIMIT),
        cost_estimate=COST,
        name="add",
    )(a, b)


def steps_of(axis):
    step = 1
    while step < lax.axis_size(axis):
        yield step
        step *= 2


def per_device(
    book_tokens,
    norm_gain,
    query_weight,
    key_weight,
    value_weight,
    proj_weight,
    dual_gains,
    out_weight,
    span_bounds,
):
    rows = book_tokens.shape[0]
    seq_devices = lax.axis_size(("seq", "rep"))
    seq_index = lax.axis_index(("seq", "rep"))
    head_devices = lax.axis_size("head")
    head_index = lax.axis_index("head")
    first_row = seq_index * rows
    all_pairs = query_weight.shape[1] // LANES
    groups = 2 if all_pairs % 2 == 0 else 1
    pairs = all_pairs // groups
    ids = jnp.stack(
        [lax.axis_index("rep"), (seq_index > 0).astype(jnp.int32), (seq_index < seq_devices - 1).astype(jnp.int32), first_row]
    ).astype(jnp.int32)
    gain = norm_gain[None, :]
    bounds = span_bounds.T

    both = ("seq", "rep")
    chips = [(i, i + 1) for i in range(1, seq_devices - 1, 2)]
    chips = chips + [(b, a) for a, b in chips]
    steps = list(steps_of("seq"))
    tie = lax.optimization_barrier

    fronts, mine, normed = [], [], book_tokens
    turn = ids
    for g in range(groups):
        last = g == groups - 1
        normed, *outs, turn = front(g == 0, last, g, pairs, turn, normed, gain, key_weight, value_weight, proj_weight,
                                    dual_gains, [f[3] for f in fronts])
        fronts.append(outs)
        send, edge = outs[2], outs[3]
        if last:
            for f in range(g):
                for step in steps[:-1]:
                    got, turn = tie((swap(mine[f], "seq", step), turn))
                    mine[f] = add(mine[f], got)
                mine[f], turn = tie((mine[f], turn))
        core = swap(send, "rep", 1)
        if last:
            chip = lax.ppermute(edge, both, chips)
        got, turn = tie((core[: outs[1].shape[0]], turn))
        mine.append(add(outs[1], got))
        mine[g], turn = tie((mine[g], turn))

    if groups == 1:
        for step in steps[:-1]:
            mine[0] = add_call(mine[0], swap(mine[0], "seq", step))

    spread = lax.axis_size("seq")
    outs, before, arrived, others, other_index = [], (), [], [], []
    for g in range(groups):
        normed, q, near_sums, turn = near(pairs, g, turn, normed, core, chip, query_weight, fronts[g][0])
        got, turn = tie((swap(mine[g], "seq", steps[-1]), turn))
        total = add_call(mine[g], got)
        other = swap(total, "rep", 1)
        if g == groups - 2:
            for step in steps[:-1]:
                got, turn = tie((swap(mine[-1], "seq", step), turn))
                mine[-1] = add_call(mine[-1], got)
            mine[-1], turn = tie((mine[-1], turn))
        *out, keep, send, turn = far(pairs, g, spread, turn, q, near_sums, total, other, dual_gains, bounds, before, arrived)
        before = [keep, send]
        outs.append(out)
        moved = [[across_heads(piece, k) for piece in out] for k in range(1, head_devices)]
        arrived = [moved[0][0]] if g < groups - 1 and moved else []
        others += moved
        other_index += [lax.rem(head_index - k + head_devices, head_devices) * groups + g for k in range(1, head_devices)]

    own_index = [head_index * groups + g for g in range(groups)]
    early = len(others) - (head_devices - 1)

    keep, send = before
    place = lax.axis_index("seq").astype(jnp.int32)[None]
    own, *pieces = pool_pieces(place, keep, swap(send, "rep", 1), spread)
    pieces = [
        lax.ppermute(piece, "seq", [(i, (i + k + 1) % spread) for i in range(spread)]) for k, piece in enumerate(pieces)
    ]
    parts = outs + others[:early]
    index = jnp.stack(own_index + other_index[:early]).astype(jnp.int32)
    acc, turn = out_part(parts, index, out_weight, None, F32)
    place = (seq_index * own.shape[0]).astype(jnp.int32)[None]
    place = place + (turn - index[:1])
    own = pool_own(place, bounds, own, pieces)
    pooled = [own] + [across_heads(own, k) for k in range(1, head_devices)]
    pooled_index = [lax.rem(head_index - k + head_devices, head_devices) for k in range(head_devices)]
    index = jnp.stack(other_index[early:] + pooled_index).astype(jnp.int32)
    return tuple(out_part(others[early:], index, out_weight, acc, BF, pooled)[:2])


def solution(mesh):
    placed = (
        P(("groups", "seq", "rep"), None),
        P(),
        P(None, "head"),
        P(None, "head"),
        P(None, "head"),
        P(None, "head"),
        P(None, "head"),
        P(None, "head"),
        P("groups", None),
    )
    return jax.shard_map(
        per_device,
        mesh=mesh,
        in_specs=placed,
        out_specs=(P(("groups", "seq", "rep"), "head"), P(("groups", "seq", "rep"), "head")),
        check_vma=False,
    )
```

```python
import functools

import jax
import jax.numpy as jnp
from jax import lax
from jax.experimental import pallas as pl
from jax.experimental.pallas import tpu as pltpu
from jax.sharding import PartitionSpec as P

DH = 64
R = 256
SEG = 128
HALF = SEG // 2
LANES = 2 * DH
SCORE_SCALE = DH ** (-0.5)
LOG2E = 1.4426950408889634

VMEM_LIMIT = 40 << 20
COST = pl.CostEstimate(flops=1 << 20, bytes_accessed=1 << 10, transcendentals=0)

LONG = pl.CostEstimate(flops=1 << 33, bytes_accessed=1 << 10, transcendentals=0)
TURN = jax.ShapeDtypeStruct((4,), jnp.int32)

softcap = 5.0
epsilon = 1e-05

BF = jnp.bfloat16
F32 = jnp.float32


def dot(a, b, dims=((1,), (0,))):
    return lax.dot_general(a, b, (dims, ((), ())), preferred_element_type=F32)


def exp_capped(values, scale):
    return jnp.exp2((softcap * LOG2E) * jnp.tanh(values * (scale / softcap)))


def pass_turn(ids_ref, turn_ref):
    for i in range(4):
        turn_ref[i] = ids_ref[i]


def vmem():
    return pl.BlockSpec(memory_space=pltpu.VMEM)


def smem():
    return pl.BlockSpec(memory_space=pltpu.SMEM)


def head_norm(values, gain):
    out = []
    for at in range(0, values.shape[1], LANES):
        x = values[:, at : at + LANES]
        first = lane_is_first(x.shape)

        def mean(y):
            low = jnp.sum(jnp.where(first, y, 0.0), axis=-1, keepdims=True)
            high = jnp.sum(jnp.where(first, 0.0, y), axis=-1, keepdims=True)
            return jnp.where(first, low, high) * (1.0 / DH)

        centred = x - mean(x)
        spread = mean(centred * centred)
        out.append((centred * lax.rsqrt(spread + epsilon) * gain[:, at : at + LANES]).astype(BF))
    return jnp.concatenate(out, axis=1)


def token_norm(x, gain):
    x = x.astype(F32)
    centred = x - jnp.mean(x, axis=-1, keepdims=True)
    spread = jnp.mean(centred * centred, axis=-1, keepdims=True)
    return (centred * lax.rsqrt(spread + epsilon) * gain).astype(BF)


def edge_rows(near_ref):
    rows = near_ref.shape[0]
    columns = [slice(at, at + 2 * LANES) for at in range(0, near_ref.shape[1], 2 * LANES)]
    return [jnp.concatenate([near_ref[at, c] for c in columns], axis=0) for at in (slice(0, HALF), slice(rows - HALF, rows))]


def front_kernel(first, last, group, pairs, tile, *refs):
    ids_ref, refs = refs[0], list(refs[1:])
    if first:
        x_hbm, gain_hbm, dual_hbm, wk_hbm, wv_hbm, wp_hbm = refs[:6]
        refs = refs[6:]
    else:
        given_ref, dual_ref, kv_ref, wp_ref = refs[:4]
        refs = refs[4:]
        if not last:
            wk_hbm, wv_hbm, wp_hbm = refs[:3]
            refs = refs[3:]
    earlier = [refs.pop(0) for _ in range(group)] if last else []
    normed_ref, near_ref, keep_ref, send_ref = refs[:4]
    edge_refs = refs[4 : 5 + len(earlier)]
    turn_ref = refs[5 + len(earlier)]
    refs = refs[6 + len(earlier) :]
    pass_turn(ids_ref, turn_ref)
    if not last:
        next_kv_ref, next_wp_ref = refs[:2]
        refs = refs[2:]
    raw_ref, p_ref, sem = refs[:3]
    if first:
        kv_ref, wp_ref, x_ref, gain_ref, dual_ref = refs[3:]
    rows = normed_ref.shape[0]
    width = pairs * LANES
    chunks = rows // tile
    used = 0

    def copy(source, target):
        nonlocal used
        made = pltpu.make_async_copy(source, target, sem.at[used])
        used += 1
        made.start()
        return made

    def weight_copies(g, kv, wp):
        own = pl.ds(g * width, width)
        heads = [
            copy(wk_hbm.at[:, own], kv.at[:, pl.ds(0, width)]),
            copy(wv_hbm.at[:, own], kv.at[:, pl.ds(width, width)]),
        ]
        return heads, [copy(wp_hbm.at[:, pl.ds(g * pairs * 2 * R, pairs * 2 * R)], wp)]

    def token_copy(i):
        at = pl.ds(i * tile, tile)
        return copy(x_hbm.at[at, :], x_ref.at[at, :])

    kv_copies, proj_copies, next_copies = [], [], []
    if first:
        token_copies = [token_copy(0)]
        small_copies = [copy(gain_hbm, gain_ref), copy(dual_hbm, dual_ref)]
        kv_copies, proj_copies = weight_copies(group, kv_ref, wp_ref)
        token_copies += [token_copy(i) for i in range(1, chunks)]
    if not last:
        next_copies = sum(weight_copies(group + 1, next_kv_ref, next_wp_ref), [])
    for i in range(chunks):
        at = pl.ds(i * tile, tile)
        if first:
            token_copies[i].wait()
            if i == 0:
                for made in small_copies:
                    made.wait()
            normed_ref[at, :] = token_norm(x_ref[at, :], gain_ref[...])
        normed = normed_ref[at, :]
        if i == 0:
            for made in kv_copies:
                made.wait()
        both = dot(normed, kv_ref[...])
        key, value = both[:, :width], both[:, width:]
        for p in range(pairs):
            cols = slice(p * LANES, (p + 1) * LANES)
            raw = jnp.concatenate([key[:, cols], value[:, cols]], axis=1).astype(BF)
            raw_ref[2 * p * LANES : 2 * (p + 1) * LANES, at] = raw.T
        if i == 0:
            for made in proj_copies:
                made.wait()
        p_ref[at, :] = exp_capped(dot(normed, wp_ref[...]), 1.0).astype(BF)
        near_ref[at, :width] = head_norm(key, dual_ref[0:1, group * width : (group + 1) * width])
        near_ref[at, width:] = head_norm(value, dual_ref[1:2, group * width : (group + 1) * width])
    total = []
    for p in range(pairs):
        full = dot(raw_ref[2 * p * LANES : 2 * (p + 1) * LANES, :], p_ref[:, 2 * p * R : 2 * (p + 1) * R])
        for part in range(4):
            head = part % 2
            total.append(full[part * DH : (part + 1) * DH, head * R : (head + 1) * R])
    for made in next_copies:
        made.wait()
    total = jnp.concatenate(total, axis=0).astype(BF)
    half = total.shape[0] // 2
    mine = ids_ref[0] == 0
    keep_ref[...] = jnp.where(mine, total[:half], total[half:])
    send_ref[:half, :] = jnp.where(mine, total[half:], total[:half])
    head, tail = edge_rows(near_ref)
    edge = head.shape[0]
    if last:
        for i, ref in enumerate(earlier):
            before = jnp.where(mine, ref[edge:, :], ref[:edge, :])
            send_ref[half + i * edge : half + (i + 1) * edge, :] = before
            edge_refs[i][...] = jnp.where(mine, ref[:edge, :], ref[edge:, :])
        send_ref[half + group * edge :, :] = jnp.where(mine, tail, head)
        edge_refs[group][...] = jnp.where(mine, head, tail)
    else:
        edge_refs[0][:edge, :] = head
        edge_refs[0][edge:, :] = tail


def in_hbm(values):
    return pltpu.with_memory_space_constraint(values, pltpu.HBM)


def front(first, last, group, pairs, ids, tokens, gain, wk, wv, wp, dual, earlier, fetched):
    rows, depth = tokens.shape
    width = pairs * LANES
    half = pairs * R // 2
    tile = min(512 if first else 256, rows)
    edge = (group + 1) * pairs * HALF if last else 0
    outs = [
        jax.ShapeDtypeStruct((rows, depth), BF),
        jax.ShapeDtypeStruct((rows, 2 * width), BF),
        jax.ShapeDtypeStruct((half, R), BF),
        jax.ShapeDtypeStruct((half + edge, R), BF),
        *[jax.ShapeDtypeStruct(((1 if last else 2) * pairs * HALF, R), BF)] * (group + 1 if last else 1),
        TURN,
    ]
    if not last:
        outs += [jax.ShapeDtypeStruct((depth, 2 * width), BF), jax.ShapeDtypeStruct((depth, 2 * pairs * R), BF)]
    hbm = pl.BlockSpec(memory_space=pltpu.HBM)
    earlier = earlier if last else []
    weights = [in_hbm(wk), in_hbm(wv), in_hbm(wp)]
    if first:
        ins = [hbm] * 6
        args = [in_hbm(tokens), in_hbm(gain), in_hbm(dual)] + weights
    else:
        ins = [vmem()] * 4 + ([] if last else [hbm] * 3)
        args = [tokens, dual, *fetched] + ([] if last else weights)
    ins = [smem()] + ins + [vmem()] * len(earlier)
    args = [ids] + args + earlier
    scratch = [
        pltpu.VMEM((2 * width, rows), BF),
        pltpu.VMEM((rows, 2 * pairs * R), BF),
        pltpu.SemaphoreType.DMA((rows // tile + 8,)),
    ]
    if first:
        scratch += [
            pltpu.VMEM((depth, 2 * width), BF),
            pltpu.VMEM((depth, 2 * pairs * R), BF),
            pltpu.VMEM((rows, depth), BF),
            pltpu.VMEM((1, depth), F32),
            pltpu.VMEM(dual.shape, F32),
        ]
    is_turn = [o is TURN for o in outs]
    return pl.pallas_call(
        functools.partial(front_kernel, first, last, group, pairs, tile),
        input_output_aliases={} if first else {1: 0},
        in_specs=ins,
        out_specs=[smem() if t else vmem() for t in is_turn],
        out_shape=outs,
        scratch_shapes=scratch,
        compiler_params=pltpu.CompilerParams(vmem_limit_bytes=VMEM_LIMIT),
        cost_estimate=pl.CostEstimate(
            flops=2 * rows * depth * (2 * width + 2 * pairs * R), bytes_accessed=4 << 20, transcendentals=0
        ),
        name="front",
    )(*args)


def lane_is_first(shape):
    return lax.broadcasted_iota(jnp.int32, shape, 1) < DH


def stacked(q):
    first = lane_is_first(q.shape)
    zero = jnp.zeros_like(q)
    return jnp.concatenate([jnp.where(first, q, zero), jnp.where(first, zero, q)], axis=0)


def unstack(both):
    rows = both.shape[0] // 2
    first = lane_is_first((rows, LANES))
    return (
        jnp.where(first, both[:rows, :LANES], both[rows:, :LANES]),
        jnp.where(first, both[:rows, LANES:], both[rows:, LANES:]),
    )


def near_kernel(pairs, group, groups, ids_ref, *refs):
    width = pairs * LANES
    if group == 0:
        normed_ref, wq_ref, core_ref, chip_ref, near_ref = refs[:5]
        q_refs, (out_ref, turn_ref, pad_ref) = refs[-3 - groups : -3], refs[-3:]
        q_ref, rows = q_refs[0], normed_ref.shape[0]
        for start in range(0, rows, 256):
            at = slice(start, start + 256)
            q = dot(normed_ref[at, :], wq_ref[...])
            for g in range(groups):
                q_refs[g][at, :] = q[:, g * width : (g + 1) * width].astype(BF)
    else:
        given_ref, core_ref, chip_ref, near_ref, q_ref, out_ref, turn_ref, pad_ref = refs
        rows = q_ref.shape[0]
    is_first = ids_ref[0] == 0
    row = lax.broadcasted_iota(jnp.int32, (2 * SEG, LANES), 0)
    ones = jnp.ones((2 * SEG, LANES), F32)
    has_prev = jnp.where(ids_ref[1] != 0, 1.0, 0.0)
    has_next = jnp.where(ids_ref[2] != 0, 1.0, 0.0)
    segments = rows // SEG
    offset = core_ref.shape[0] - (groups - group) * chip_ref.shape[0]
    pad_ref[HALF : HALF + rows, :] = near_ref[...]
    for c in range(pairs):
        at = c * HALF
        core = core_ref[offset + at : offset + at + HALF, :]
        chip = chip_ref[at : at + HALF, :]
        lanes = slice(2 * c * LANES, 2 * (c + 1) * LANES)
        pad_ref[0:HALF, lanes] = jnp.where(is_first, chip, core)
        pad_ref[HALF + rows :, lanes] = jnp.where(is_first, core, chip)
    for s in range(segments):
        count = ones
        if s == 0:
            count = jnp.where(row < HALF, has_prev, count)
        if s == segments - 1:
            count = jnp.where(row >= 3 * HALF, has_next, count)
        count = count.astype(BF)
        window = pl.ds(s * SEG, 2 * SEG)
        here = slice(s * SEG, (s + 1) * SEG)
        for p in range(pairs):
            cols = slice(p * LANES, (p + 1) * LANES)
            scores = dot(stacked(q_ref[here, cols]), pad_ref[window, cols], ((1,), (1,)))
            weights = exp_capped(scores, SCORE_SCALE).astype(BF)
            values = jnp.concatenate([pad_ref[window, width + p * LANES : width + (p + 1) * LANES], count], axis=1)
            top, bottom = unstack(dot(weights, values))
            out_ref[here, 2 * p * LANES : (2 * p + 1) * LANES] = top
            out_ref[here, (2 * p + 1) * LANES : (2 * p + 2) * LANES] = bottom
    pass_turn(ids_ref, turn_ref)


def near(pairs, group, groups, ids, source, wq, core, chips, near_pairs):
    rows = near_pairs.shape[0]
    width = pairs * LANES
    q = jax.ShapeDtypeStruct((rows, width), BF)
    count = groups if group == 0 else 1
    args = [source, wq] if group == 0 else [source]
    others = chips[1:] if group == 0 else []
    return pl.pallas_call(
        functools.partial(near_kernel, pairs, group, groups),
        in_specs=[smem()] + [vmem()] * (len(args) + 3) + [pl.BlockSpec(memory_space=pl.ANY)] * len(others),
        out_specs=[vmem()] * (count + 1) + [smem()],
        out_shape=[q] * count + [jax.ShapeDtypeStruct((rows, 2 * width), F32), TURN],
        input_output_aliases={} if group == 0 else {1: 0},
        scratch_shapes=[pltpu.VMEM((rows + SEG, 2 * width), BF)],
        compiler_params=pltpu.CompilerParams(vmem_limit_bytes=VMEM_LIMIT),
        cost_estimate=COST,
        name="near",
    )(ids, *args, core, chips[group], near_pairs, *others)


def far_kernel(pairs, group, block, spread, *refs):
    (ids_ref, q_ref, near_ref, mine_ref, other_ref, gains_ref, bounds_ref), refs = refs[:7], refs[7:]
    keep_ref, send_ref, turn_ref = refs[-3:]
    out_refs = refs[-3 - pairs : -3]
    before = refs[:2] if group else ()
    pass_turn(ids_ref, turn_ref)
    rows = q_ref.shape[0]
    width = pairs * LANES
    is_first = ids_ref[0] == 0
    top = jnp.where(is_first, mine_ref[...], other_ref[...])
    bottom = jnp.where(is_first, other_ref[...], mine_ref[...])
    total = jnp.concatenate([top, bottom], axis=0)
    ones = jnp.ones((LANES, R), BF)
    for p in range(pairs):
        cols = slice(p * LANES, (p + 1) * LANES)

        base = group * width + p * LANES
        gains = jnp.concatenate([gains_ref[:, base : base + LANES]] * 2, axis=0).T

        def land(kind):
            parts = []
            for h in range(2):
                at = p * R + kind * LANES + h * DH
                values = total[at : at + DH].astype(F32)
                centred = values - jnp.mean(values, axis=0, keepdims=True)
                spread = jnp.mean(centred * centred, axis=0, keepdims=True)
                gain = gains[h * DH : (h + 1) * DH, 2 + kind : 3 + kind]
                parts.append((centred * lax.rsqrt(spread + epsilon) * gain).astype(BF))
            return jnp.concatenate(parts, axis=0)

        keys = land(0)
        values = jnp.concatenate([land(1), ones], axis=0)
        for start in range(0, rows, block):
            q = stacked(q_ref[start : start + block, cols])
            weights = exp_capped(dot(q, keys), SCORE_SCALE).astype(BF)
            top, bottom = unstack(dot(weights, values, ((1,), (1,))))
            top = top + near_ref[start : start + block, 2 * p * LANES : (2 * p + 1) * LANES]
            bottom = bottom + near_ref[start : start + block, (2 * p + 1) * LANES : (2 * p + 2) * LANES]
            out_refs[p][start : start + block, :] = (top / bottom).astype(BF)
    spans = bounds_ref.shape[1]
    position = ids_ref[3] + lax.broadcasted_iota(jnp.int32, (rows, spans), 0)
    member = (position >= bounds_ref[0:1, :]) & (position < bounds_ref[1:2, :])
    outs = jnp.concatenate([ref[...] for ref in out_refs], axis=1)
    sums = dot(jnp.where(member, 1.0, 0.0).astype(BF), outs, ((0,), (0,)))
    count = spans // (2 * spread)
    even = jnp.concatenate([sums[2 * i * count : (2 * i + 1) * count] for i in range(spread)], axis=0)
    odd = jnp.concatenate([sums[(2 * i + 1) * count : (2 * i + 2) * count] for i in range(spread)], axis=0)
    lanes = slice(group * width, (group + 1) * width)
    if before:
        keep_ref[:, : group * width] = before[0][...]
        send_ref[:, : group * width] = before[1][...]
    keep_ref[:, lanes] = jnp.where(is_first, even, odd)
    send_ref[:, lanes] = jnp.where(is_first, odd, even).astype(BF)


def far(pairs, group, spread, ids, q, near_sums, mine, other, gains, bounds, before, arrived):
    rows = q.shape[0]
    width = pairs * LANES
    spans = bounds.shape[1]
    shape = (spans // 2, (group + 1) * width)
    return pl.pallas_call(
        functools.partial(far_kernel, pairs, group, 256, spread),
        in_specs=[smem()] + [vmem()] * (6 + len(before)) + [pl.BlockSpec(memory_space=pl.ANY)] * len(arrived),
        out_specs=[vmem()] * (2 + pairs) + [smem()],
        out_shape=[
            *[jax.ShapeDtypeStruct((rows, LANES), BF)] * pairs,
            jax.ShapeDtypeStruct(shape, F32),
            jax.ShapeDtypeStruct(shape, BF),
            TURN,
        ],
        compiler_params=pltpu.CompilerParams(vmem_limit_bytes=VMEM_LIMIT),
        cost_estimate=COST,
        name="far",
    )(ids, q, near_sums, mine, other, gains, bounds, *before, *arrived)


def out_kernel(count, pairs, spans, *refs):
    ids_ref, refs = refs[0], refs[1:]
    tokens, refs = [refs[j * pairs : (j + 1) * pairs] for j in range(count)], refs[count * pairs :]
    pooled, refs = refs[:spans], refs[spans:]
    if spans:
        *refs, stage_ref, sem = refs
    *refs, turn_ref = refs
    turn_ref[0] = ids_ref[0]
    outs = refs[-2:] if spans else refs[-1:]
    weight_ref, *acc = refs[: -len(outs)]
    rows, width = tokens[0][0].shape[0], pairs * LANES
    tile = min(256, rows)

    def weight(j, size):
        return weight_ref[pl.ds(pl.multiple_of(ids_ref[j] * size, size), size), :]

    made = []
    for start in range(0, rows, tile):
        at = slice(start, start + tile)
        total = acc[0][at, :] if acc else None
        for j in range(count):
            term = dot(jnp.concatenate([ref[at, :] for ref in tokens[j]], axis=1), weight(j, width))
            total = term if total is None else total + term
        if not spans:
            outs[0][at, :] = total.astype(outs[0].dtype)
            continue
        stage_ref[at, :] = total.astype(outs[0].dtype)
        here = pl.ds(start, tile)
        made.append(pltpu.make_async_copy(stage_ref.at[here, :], outs[0].at[here, :], sem.at[start // tile]))
        made[-1].start()
    if spans:
        outs[1][...] = sum(dot(ref[...], weight(count + k, ref.shape[1])) for k, ref in enumerate(pooled))
    for copy in made:
        copy.wait()


def out_part(parts, index, weight, acc, dtype, pooled=()):
    count = len(parts)
    pairs = len(parts[0])
    rows = parts[0][0].shape[0]
    columns = weight.shape[1]
    extra = [] if acc is None else [acc]
    shapes = [jax.ShapeDtypeStruct((rows, columns), dtype)]
    shapes += [jax.ShapeDtypeStruct((pooled[0].shape[0], columns), F32)] if pooled else []
    return pl.pallas_call(
        functools.partial(out_kernel, count, pairs, len(pooled)),
        in_specs=[smem()] + [vmem()] * (count * pairs + len(pooled) + 1 + len(extra)),
        out_specs=[pl.BlockSpec(memory_space=pltpu.HBM) if pooled else vmem()] + [vmem()] * (len(shapes) - 1) + [smem()],
        out_shape=shapes + [jax.ShapeDtypeStruct((1,), jnp.int32)],
        scratch_shapes=[pltpu.VMEM((rows, columns), dtype), pltpu.SemaphoreType.DMA((pl.cdiv(rows, 256),))] if pooled else [],
        compiler_params=pltpu.CompilerParams(vmem_limit_bytes=VMEM_LIMIT),
        cost_estimate=COST,
        name="out",
    )(index, *[piece for part in parts for piece in part], *pooled, weight, *extra)


def pieces_kernel(ids_ref, keep_ref, got_ref, *out_refs):
    spread = len(out_refs)
    count = keep_ref.shape[0] // spread
    for k, ref in enumerate(out_refs):
        at = pl.ds(pl.multiple_of(lax.rem(ids_ref[0] + k, spread) * count, count), count)
        ref[...] = (keep_ref[at, :] + got_ref[at, :].astype(F32)).astype(ref.dtype)


def pool_pieces(place, keep, got, spread):
    count = keep.shape[0] // spread
    shape = (count, keep.shape[1])
    return pl.pallas_call(
        pieces_kernel,
        in_specs=[smem(), vmem(), vmem()],
        out_specs=[vmem()] * spread,
        out_shape=[jax.ShapeDtypeStruct(shape, F32)] + [jax.ShapeDtypeStruct(shape, BF)] * (spread - 1),
        compiler_params=pltpu.CompilerParams(vmem_limit_bytes=VMEM_LIMIT),
        cost_estimate=COST,
        name="pool_pieces",
    )(place, keep, got)


def own_kernel(ids_ref, bounds_ref, own_ref, *refs):
    total = own_ref[...]
    for ref in refs[:-1]:
        total = total + ref[...].astype(F32)
    count = total.shape[0]
    rows = [
        total[i : i + 1] / (bounds_ref[1, ids_ref[0] + i] - bounds_ref[0, ids_ref[0] + i]).astype(F32)
        for i in range(count)
    ]
    refs[-1][...] = jnp.concatenate(rows, axis=0).astype(BF)


def pool_own(place, bounds, own, others):
    return pl.pallas_call(
        own_kernel,
        in_specs=[smem(), smem()] + [vmem()] * (1 + len(others)),
        out_specs=vmem(),
        out_shape=jax.ShapeDtypeStruct(own.shape, BF),
        compiler_params=pltpu.CompilerParams(vmem_limit_bytes=VMEM_LIMIT),
        cost_estimate=COST,
        name="pool_own",
    )(place, bounds, own, *others)


def swap(values, axis, step):
    count = lax.axis_size(axis)
    return lax.ppermute(values, axis, [(i, i ^ step) for i in range(count)])


def across_heads(values, step):
    count = lax.axis_size("head")
    return lax.ppermute(values, "head", [(i, (i + step) % count) for i in range(count)])


def add_kernel(a_ref, b_ref, out_ref):
    count = a_ref.shape[0]
    out_ref[...] = (a_ref[...].astype(F32) + b_ref[:count, :].astype(F32)).astype(BF)


def add_call(a, b, cost=COST):
    return pl.pallas_call(
        add_kernel,
        in_specs=[vmem()] * 2,
        out_specs=vmem(),
        out_shape=jax.ShapeDtypeStruct(a.shape, BF),
        compiler_params=pltpu.CompilerParams(vmem_limit_bytes=VMEM_LIMIT),
        cost_estimate=cost,
        name="add",
    )(a, b)


def steps_of(axis):
    step = 1
    while step < lax.axis_size(axis):
        yield step
        step *= 2


def per_device(
    book_tokens,
    norm_gain,
    query_weight,
    key_weight,
    value_weight,
    proj_weight,
    dual_gains,
    out_weight,
    span_bounds,
):
    rows = book_tokens.shape[0]
    seq_devices = lax.axis_size(("seq", "rep"))
    seq_index = lax.axis_index(("seq", "rep"))
    head_devices = lax.axis_size("head")
    head_index = lax.axis_index("head")
    first_row = seq_index * rows
    all_pairs = query_weight.shape[1] // LANES
    groups = 2 if all_pairs % 2 == 0 else 1
    pairs = all_pairs // groups
    ids = jnp.stack(
        [lax.axis_index("rep"), (seq_index > 0).astype(jnp.int32), (seq_index < seq_devices - 1).astype(jnp.int32), first_row]
    ).astype(jnp.int32)
    gain = norm_gain[None, :]
    bounds = span_bounds.T

    both = ("seq", "rep")
    chips = [(i, i + 1) for i in range(1, seq_devices - 1, 2)]
    chips = chips + [(b, a) for a, b in chips]
    steps = list(steps_of("seq"))
    tie = lax.optimization_barrier

    fronts, mine, normed = [], [], book_tokens
    turn = ids
    fetched = []
    for g in range(groups):
        last = g == groups - 1
        normed, *outs = front(g == 0, last, g, pairs, turn, normed, gain, key_weight, value_weight, proj_weight,
                              dual_gains, [f[3] for f in fronts], fetched)
        edges = outs[3 : 4 + g if last else 4]
        outs, turn, fetched = outs[:4], outs[3 + len(edges)], outs[4 + len(edges) :]
        fronts.append(outs)
        send = outs[2]
        if last:
            for f in range(g):
                for step in steps[:-1]:
                    got, turn = tie((swap(mine[f], "seq", step), turn))
                    mine[f] = add_call(mine[f], got, LONG)
                mine[f], turn = tie((mine[f], turn))
        core = swap(send, "rep", 1)
        if last:
            chip = [lax.ppermute(edge, both, chips) for edge in edges]
        mine.append(add_call(outs[1], core))
        mine[g], turn = tie((mine[g], turn))

    if groups == 1:
        for step in steps[:-1]:
            mine[0] = add_call(mine[0], swap(mine[0], "seq", step))

    spread = lax.axis_size("seq")
    outs, before, arrived, others, other_index, queries = [], (), [], [], [], []
    for g in range(groups):
        source = queries[g] if g else normed
        *made, near_sums, turn = near(pairs, g, groups, turn, source, query_weight, core, chip, fronts[g][0])
        queries = queries if g else made
        q = made[0]
        got, turn = tie((swap(mine[g], "seq", steps[-1]), turn))
        total = add_call(mine[g], got)
        other = swap(total, "rep", 1)
        if g == groups - 2:
            for step in steps[:-1]:
                got, turn = tie((swap(mine[-1], "seq", step), turn))
                mine[-1] = add_call(mine[-1], got)
            mine[-1], turn = tie((mine[-1], turn))
        *out, keep, send, turn = far(pairs, g, spread, turn, q, near_sums, total, other, dual_gains, bounds, before, arrived)
        before = [keep, send]
        outs.append(out)
        moved = [[across_heads(piece, k) for piece in out] for k in range(1, head_devices)]
        arrived = [moved[0][0]] if g < groups - 1 and moved else []
        others += moved
        other_index += [lax.rem(head_index - k + head_devices, head_devices) * groups + g for k in range(1, head_devices)]

    own_index = [head_index * groups + g for g in range(groups)]
    early = len(others) - (head_devices - 1)

    keep, send = before
    place = lax.axis_index("seq").astype(jnp.int32)[None]
    own, *pieces = pool_pieces(place, keep, swap(send, "rep", 1), spread)
    pieces = [
        lax.ppermute(piece, "seq", [(i, (i + k + 1) % spread) for i in range(spread)]) for k, piece in enumerate(pieces)
    ]
    parts = outs + others[:early]
    index = jnp.stack(own_index + other_index[:early]).astype(jnp.int32)
    acc, turn = out_part(parts, index, out_weight, None, F32)
    place = (seq_index * own.shape[0]).astype(jnp.int32)[None]
    place = place + (turn - index[:1])
    own = pool_own(place, bounds, own, pieces)
    pooled = [own] + [across_heads(own, k) for k in range(1, head_devices)]
    pooled_index = [lax.rem(head_index - k + head_devices, head_devices) for k in range(head_devices)]
    index = jnp.stack(other_index[early:] + pooled_index).astype(jnp.int32)
    return tuple(out_part(others[early:], index, out_weight, acc, BF, pooled)[:2])


def solution(mesh):
    placed = (
        P(("groups", "seq", "rep"), None),
        P(),
        P(None, "head"),
        P(None, "head"),
        P(None, "head"),
        P(None, "head"),
        P(None, "head"),
        P(None, "head"),
        P("groups", None),
    )
    return jax.shard_map(
        per_device,
        mesh=mesh,
        in_specs=placed,
        out_specs=(P(("groups", "seq", "rep"), "head"), P(("groups", "seq", "rep"), "head")),
        check_vma=False,
    )
```

```python
import functools

import jax
import jax.numpy as jnp
from jax import lax
from jax.experimental import pallas as pl
from jax.experimental.pallas import tpu as pltpu
from jax.sharding import PartitionSpec as P

DH = 64
R = 256
SEG = 128
HALF = SEG // 2
LANES = 2 * DH
SCORE_SCALE = DH ** (-0.5)
LOG2E = 1.4426950408889634

VMEM_LIMIT = 40 << 20
COST = pl.CostEstimate(flops=1 << 20, bytes_accessed=1 << 10, transcendentals=0)

LONG = pl.CostEstimate(flops=1 << 33, bytes_accessed=1 << 10, transcendentals=0)
TURN = jax.ShapeDtypeStruct((4,), jnp.int32)

softcap = 5.0
epsilon = 1e-05

BF = jnp.bfloat16
F32 = jnp.float32


def dot(a, b, dims=((1,), (0,))):
    return lax.dot_general(a, b, (dims, ((), ())), preferred_element_type=F32)


def exp_capped(values, scale):
    return jnp.exp2((softcap * LOG2E) * jnp.tanh(values * (scale / softcap)))


def pass_turn(ids_ref, turn_ref):
    for i in range(4):
        turn_ref[i] = ids_ref[i]


def vmem():
    return pl.BlockSpec(memory_space=pltpu.VMEM)


def smem():
    return pl.BlockSpec(memory_space=pltpu.SMEM)


def head_norm(values, gain):
    out = []
    for at in range(0, values.shape[1], LANES):
        x = values[:, at : at + LANES]
        first = lane_is_first(x.shape)

        def mean(y):
            low = jnp.sum(jnp.where(first, y, 0.0), axis=-1, keepdims=True)
            high = jnp.sum(jnp.where(first, 0.0, y), axis=-1, keepdims=True)
            return jnp.where(first, low, high) * (1.0 / DH)

        centred = x - mean(x)
        spread = mean(centred * centred)
        out.append((centred * lax.rsqrt(spread + epsilon) * gain[:, at : at + LANES]).astype(BF))
    return jnp.concatenate(out, axis=1)


def token_norm(x, gain):
    x = x.astype(F32)
    centred = x - jnp.mean(x, axis=-1, keepdims=True)
    spread = jnp.mean(centred * centred, axis=-1, keepdims=True)
    return (centred * lax.rsqrt(spread + epsilon) * gain).astype(BF)


def edge_rows(near_ref):
    rows = near_ref.shape[0]
    columns = [slice(at, at + 2 * LANES) for at in range(0, near_ref.shape[1], 2 * LANES)]
    return [jnp.concatenate([near_ref[at, c] for c in columns], axis=0) for at in (slice(0, HALF), slice(rows - HALF, rows))]


def front_kernel(first, last, group, pairs, tile, *refs):
    ids_ref, refs = refs[0], list(refs[1:])
    if first:
        x_hbm, gain_hbm, dual_hbm, wk_hbm, wv_hbm, wp_hbm = refs[:6]
        refs = refs[6:]
    else:
        given_ref, dual_ref, kv_ref, wp_ref = refs[:4]
        refs = refs[4:]
        if not last:
            wk_hbm, wv_hbm, wp_hbm = refs[:3]
            refs = refs[3:]
    earlier = [refs.pop(0) for _ in range(group)] if last else []
    normed_ref, near_ref, keep_ref, send_ref, edge_ref, turn_ref = refs[:6]
    refs = refs[6:]
    pass_turn(ids_ref, turn_ref)
    if not last:
        next_kv_ref, next_wp_ref = refs[:2]
        refs = refs[2:]
    raw_ref, p_ref, sem = refs[:3]
    if first:
        kv_ref, wp_ref, x_ref, gain_ref, dual_ref = refs[3:]
    rows = normed_ref.shape[0]
    width = pairs * LANES
    chunks = rows // tile
    used = 0

    def copy(source, target):
        nonlocal used
        made = pltpu.make_async_copy(source, target, sem.at[used])
        used += 1
        made.start()
        return made

    def weight_copies(g, kv, wp):
        own = pl.ds(g * width, width)
        heads = [
            copy(wk_hbm.at[:, own], kv.at[:, pl.ds(0, width)]),
            copy(wv_hbm.at[:, own], kv.at[:, pl.ds(width, width)]),
        ]
        return heads, [copy(wp_hbm.at[:, pl.ds(g * pairs * 2 * R, pairs * 2 * R)], wp)]

    def token_copy(i):
        at = pl.ds(i * tile, tile)
        return copy(x_hbm.at[at, :], x_ref.at[at, :])

    kv_copies, proj_copies, next_copies = [], [], []
    if first:
        token_copies = [token_copy(0)]
        small_copies = [copy(gain_hbm, gain_ref), copy(dual_hbm, dual_ref)]
        kv_copies, proj_copies = weight_copies(group, kv_ref, wp_ref)
        token_copies += [token_copy(i) for i in range(1, chunks)]
    if not last:
        next_copies = sum(weight_copies(group + 1, next_kv_ref, next_wp_ref), [])
    for i in range(chunks):
        at = pl.ds(i * tile, tile)
        if first:
            token_copies[i].wait()
            if i == 0:
                for made in small_copies:
                    made.wait()
            normed_ref[at, :] = token_norm(x_ref[at, :], gain_ref[...])
        normed = normed_ref[at, :]
        if i == 0:
            for made in kv_copies:
                made.wait()
        both = dot(normed, kv_ref[...])
        key, value = both[:, :width], both[:, width:]
        for p in range(pairs):
            cols = slice(p * LANES, (p + 1) * LANES)
            raw = jnp.concatenate([key[:, cols], value[:, cols]], axis=1).astype(BF)
            raw_ref[2 * p * LANES : 2 * (p + 1) * LANES, at] = raw.T
        if i == 0:
            for made in proj_copies:
                made.wait()
        p_ref[at, :] = exp_capped(dot(normed, wp_ref[...]), 1.0).astype(BF)
        near_ref[at, :width] = head_norm(key, dual_ref[0:1, group * width : (group + 1) * width])
        near_ref[at, width:] = head_norm(value, dual_ref[1:2, group * width : (group + 1) * width])
    total = []
    for p in range(pairs):
        full = dot(raw_ref[2 * p * LANES : 2 * (p + 1) * LANES, :], p_ref[:, 2 * p * R : 2 * (p + 1) * R])
        for part in range(4):
            head = part % 2
            total.append(full[part * DH : (part + 1) * DH, head * R : (head + 1) * R])
    for made in next_copies:
        made.wait()
    total = jnp.concatenate(total, axis=0).astype(BF)
    half = total.shape[0] // 2
    mine = ids_ref[0] == 0
    keep_ref[...] = jnp.where(mine, total[:half], total[half:])
    send_ref[:half, :] = jnp.where(mine, total[half:], total[:half])
    head, tail = edge_rows(near_ref)
    edge = head.shape[0]
    if last:
        for i, ref in enumerate(earlier):
            before = jnp.where(mine, ref[edge:, :], ref[:edge, :])
            send_ref[half + i * edge : half + (i + 1) * edge, :] = before
            edge_ref[i * edge : (i + 1) * edge, :] = jnp.where(mine, ref[:edge, :], ref[edge:, :])
        send_ref[half + group * edge :, :] = jnp.where(mine, tail, head)
        edge_ref[group * edge :, :] = jnp.where(mine, head, tail)
    else:
        edge_ref[:edge, :] = head
        edge_ref[edge:, :] = tail


def in_hbm(values):
    return pltpu.with_memory_space_constraint(values, pltpu.HBM)


def front(first, last, group, pairs, ids, tokens, gain, wk, wv, wp, dual, earlier, fetched):
    rows, depth = tokens.shape
    width = pairs * LANES
    half = pairs * R // 2
    tile = min(512 if first else 256, rows)
    edge = (group + 1) * pairs * HALF if last else 0
    outs = [
        jax.ShapeDtypeStruct((rows, depth), BF),
        jax.ShapeDtypeStruct((rows, 2 * width), BF),
        jax.ShapeDtypeStruct((half, R), BF),
        jax.ShapeDtypeStruct((half + edge, R), BF),
        jax.ShapeDtypeStruct((edge if last else 2 * pairs * HALF, R), BF),
        TURN,
    ]
    if not last:
        outs += [jax.ShapeDtypeStruct((depth, 2 * width), BF), jax.ShapeDtypeStruct((depth, 2 * pairs * R), BF)]
    hbm = pl.BlockSpec(memory_space=pltpu.HBM)
    earlier = earlier if last else []
    weights = [in_hbm(wk), in_hbm(wv), in_hbm(wp)]
    if first:
        ins = [hbm] * 6
        args = [in_hbm(tokens), in_hbm(gain), in_hbm(dual)] + weights
    else:
        ins = [vmem()] * 4 + ([] if last else [hbm] * 3)
        args = [tokens, dual, *fetched] + ([] if last else weights)
    ins = [smem()] + ins + [vmem()] * len(earlier)
    args = [ids] + args + earlier
    scratch = [
        pltpu.VMEM((2 * width, rows), BF),
        pltpu.VMEM((rows, 2 * pairs * R), BF),
        pltpu.SemaphoreType.DMA((rows // tile + 8,)),
    ]
    if first:
        scratch += [
            pltpu.VMEM((depth, 2 * width), BF),
            pltpu.VMEM((depth, 2 * pairs * R), BF),
            pltpu.VMEM((rows, depth), BF),
            pltpu.VMEM((1, depth), F32),
            pltpu.VMEM(dual.shape, F32),
        ]
    is_turn = [o is TURN for o in outs]
    return pl.pallas_call(
        functools.partial(front_kernel, first, last, group, pairs, tile),
        input_output_aliases={} if first else {1: 0},
        in_specs=ins,
        out_specs=[smem() if t else vmem() for t in is_turn],
        out_shape=outs,
        scratch_shapes=scratch,
        compiler_params=pltpu.CompilerParams(vmem_limit_bytes=VMEM_LIMIT),
        cost_estimate=pl.CostEstimate(
            flops=2 * rows * depth * (2 * width + 2 * pairs * R), bytes_accessed=4 << 20, transcendentals=0
        ),
        name="front",
    )(*args)


def lane_is_first(shape):
    return lax.broadcasted_iota(jnp.int32, shape, 1) < DH


def stacked(q):
    first = lane_is_first(q.shape)
    zero = jnp.zeros_like(q)
    return jnp.concatenate([jnp.where(first, q, zero), jnp.where(first, zero, q)], axis=0)


def unstack(both):
    rows = both.shape[0] // 2
    first = lane_is_first((rows, LANES))
    return (
        jnp.where(first, both[:rows, :LANES], both[rows:, :LANES]),
        jnp.where(first, both[:rows, LANES:], both[rows:, LANES:]),
    )


def near_kernel(pairs, group, groups, ids_ref, *refs):
    width = pairs * LANES
    if group == 0:
        normed_ref, wq_ref, core_ref, chip_ref, near_ref = refs[:5]
        q_refs, (out_ref, turn_ref, pad_ref) = refs[5:-3], refs[-3:]
        q_ref, rows = q_refs[0], normed_ref.shape[0]
        for start in range(0, rows, 256):
            at = slice(start, start + 256)
            q = dot(normed_ref[at, :], wq_ref[...])
            for g in range(groups):
                q_refs[g][at, :] = q[:, g * width : (g + 1) * width].astype(BF)
    else:
        given_ref, core_ref, chip_ref, near_ref, q_ref, out_ref, turn_ref, pad_ref = refs
        rows = q_ref.shape[0]
    is_first = ids_ref[0] == 0
    row = lax.broadcasted_iota(jnp.int32, (2 * SEG, LANES), 0)
    ones = jnp.ones((2 * SEG, LANES), F32)
    has_prev = jnp.where(ids_ref[1] != 0, 1.0, 0.0)
    has_next = jnp.where(ids_ref[2] != 0, 1.0, 0.0)
    segments = rows // SEG
    offset = core_ref.shape[0] - chip_ref.shape[0]
    pad_ref[HALF : HALF + rows, :] = near_ref[...]
    for c in range(pairs):
        at = (group * pairs + c) * HALF
        core = core_ref[offset + at : offset + at + HALF, :]
        chip = chip_ref[at : at + HALF, :]
        lanes = slice(2 * c * LANES, 2 * (c + 1) * LANES)
        pad_ref[0:HALF, lanes] = jnp.where(is_first, chip, core)
        pad_ref[HALF + rows :, lanes] = jnp.where(is_first, core, chip)
    for s in range(segments):
        count = ones
        if s == 0:
            count = jnp.where(row < HALF, has_prev, count)
        if s == segments - 1:
            count = jnp.where(row >= 3 * HALF, has_next, count)
        count = count.astype(BF)
        window = pl.ds(s * SEG, 2 * SEG)
        here = slice(s * SEG, (s + 1) * SEG)
        for p in range(pairs):
            cols = slice(p * LANES, (p + 1) * LANES)
            scores = dot(stacked(q_ref[here, cols]), pad_ref[window, cols], ((1,), (1,)))
            weights = exp_capped(scores, SCORE_SCALE).astype(BF)
            values = jnp.concatenate([pad_ref[window, width + p * LANES : width + (p + 1) * LANES], count], axis=1)
            top, bottom = unstack(dot(weights, values))
            out_ref[here, 2 * p * LANES : (2 * p + 1) * LANES] = top
            out_ref[here, (2 * p + 1) * LANES : (2 * p + 2) * LANES] = bottom
    pass_turn(ids_ref, turn_ref)


def near(pairs, group, groups, ids, source, wq, core, chip, near_pairs):
    rows = near_pairs.shape[0]
    width = pairs * LANES
    q = jax.ShapeDtypeStruct((rows, width), BF)
    count = groups if group == 0 else 1
    args = [source, wq] if group == 0 else [source]
    return pl.pallas_call(
        functools.partial(near_kernel, pairs, group, groups),
        in_specs=[smem()] + [vmem()] * (len(args) + 3),
        out_specs=[vmem()] * (count + 1) + [smem()],
        out_shape=[q] * count + [jax.ShapeDtypeStruct((rows, 2 * width), F32), TURN],
        input_output_aliases={} if group == 0 else {1: 0},
        scratch_shapes=[pltpu.VMEM((rows + SEG, 2 * width), BF)],
        compiler_params=pltpu.CompilerParams(vmem_limit_bytes=VMEM_LIMIT),
        cost_estimate=COST,
        name="near",
    )(ids, *args, core, chip, near_pairs)


def far_kernel(pairs, group, which, block, spread, *refs):
    (ids_ref, q_ref, near_ref, mine_ref, other_ref, gains_ref, bounds_ref), refs = refs[:7], refs[7:]
    keep_ref, send_ref, turn_ref = refs[-3:]
    out_refs = refs[-3 - len(which) : -3]
    done = (group * pairs + which[0]) * LANES
    before = refs[:2] if done else ()
    pass_turn(ids_ref, turn_ref)
    rows = q_ref.shape[0]
    width = pairs * LANES
    is_first = ids_ref[0] == 0
    top = jnp.where(is_first, mine_ref[...], other_ref[...])
    bottom = jnp.where(is_first, other_ref[...], mine_ref[...])
    total = jnp.concatenate([top, bottom], axis=0)
    ones = jnp.ones((LANES, R), BF)
    for out_ref, p in zip(out_refs, which):
        cols = slice(p * LANES, (p + 1) * LANES)

        base = group * width + p * LANES
        gains = jnp.concatenate([gains_ref[:, base : base + LANES]] * 2, axis=0).T

        def land(kind):
            parts = []
            for h in range(2):
                at = p * R + kind * LANES + h * DH
                values = total[at : at + DH].astype(F32)
                centred = values - jnp.mean(values, axis=0, keepdims=True)
                spread = jnp.mean(centred * centred, axis=0, keepdims=True)
                gain = gains[h * DH : (h + 1) * DH, 2 + kind : 3 + kind]
                parts.append((centred * lax.rsqrt(spread + epsilon) * gain).astype(BF))
            return jnp.concatenate(parts, axis=0)

        keys = land(0)
        values = jnp.concatenate([land(1), ones], axis=0)
        for start in range(0, rows, block):
            q = stacked(q_ref[start : start + block, cols])
            weights = exp_capped(dot(q, keys), SCORE_SCALE).astype(BF)
            top, bottom = unstack(dot(weights, values, ((1,), (1,))))
            top = top + near_ref[start : start + block, 2 * p * LANES : (2 * p + 1) * LANES]
            bottom = bottom + near_ref[start : start + block, (2 * p + 1) * LANES : (2 * p + 2) * LANES]
            out_ref[start : start + block, :] = (top / bottom).astype(BF)
    spans = bounds_ref.shape[1]
    position = ids_ref[3] + lax.broadcasted_iota(jnp.int32, (rows, spans), 0)
    member = (position >= bounds_ref[0:1, :]) & (position < bounds_ref[1:2, :])
    outs = jnp.concatenate([ref[...] for ref in out_refs], axis=1)
    sums = dot(jnp.where(member, 1.0, 0.0).astype(BF), outs, ((0,), (0,)))
    count = spans // (2 * spread)
    even = jnp.concatenate([sums[2 * i * count : (2 * i + 1) * count] for i in range(spread)], axis=0)
    odd = jnp.concatenate([sums[(2 * i + 1) * count : (2 * i + 2) * count] for i in range(spread)], axis=0)
    lanes = slice(done, done + len(which) * LANES)
    if before:
        keep_ref[:, :done] = before[0][...]
        send_ref[:, :done] = before[1][...]
    keep_ref[:, lanes] = jnp.where(is_first, even, odd)
    send_ref[:, lanes] = jnp.where(is_first, odd, even).astype(BF)


def far(pairs, group, which, spread, ids, q, near_sums, mine, other, gains, bounds, before, arrived):
    rows = q.shape[0]
    width = pairs * LANES
    spans = bounds.shape[1]
    shape = (spans // 2, (group * pairs + which[-1] + 1) * LANES)
    return pl.pallas_call(
        functools.partial(far_kernel, pairs, group, which, 256, spread),
        in_specs=[smem()] + [vmem()] * (6 + len(before)) + [pl.BlockSpec(memory_space=pl.ANY)] * len(arrived),
        out_specs=[vmem()] * (2 + len(which)) + [smem()],
        out_shape=[
            *[jax.ShapeDtypeStruct((rows, LANES), BF)] * len(which),
            jax.ShapeDtypeStruct(shape, F32),
            jax.ShapeDtypeStruct(shape, BF),
            TURN,
        ],
        compiler_params=pltpu.CompilerParams(vmem_limit_bytes=VMEM_LIMIT),
        cost_estimate=COST,
        name="far",
    )(ids, q, near_sums, mine, other, gains, bounds, *before, *arrived)


def out_kernel(count, pairs, spans, *refs):
    ids_ref, refs = refs[0], refs[1:]
    tokens, refs = [refs[j * pairs : (j + 1) * pairs] for j in range(count)], refs[count * pairs :]
    pooled, refs = refs[:spans], refs[spans:]
    *refs, turn_ref = refs
    turn_ref[0] = ids_ref[0]
    outs = refs[-2:] if spans else refs[-1:]
    weight_ref, *acc = refs[: -len(outs)]
    rows, width = tokens[0][0].shape[0], pairs * LANES
    tile = min(256, rows)

    def weight(j, size):
        return weight_ref[pl.ds(pl.multiple_of(ids_ref[j] * size, size), size), :]

    for start in range(0, rows, tile):
        at = slice(start, start + tile)
        total = acc[0][at, :] if acc else None
        for j in range(count):
            term = dot(jnp.concatenate([ref[at, :] for ref in tokens[j]], axis=1), weight(j, width))
            total = term if total is None else total + term
        outs[0][at, :] = total.astype(outs[0].dtype)
    if spans:
        outs[1][...] = sum(dot(ref[...], weight(count + k, ref.shape[1])) for k, ref in enumerate(pooled))


def out_part(parts, index, weight, acc, dtype, pooled=()):
    count = len(parts)
    pairs = len(parts[0])
    rows = parts[0][0].shape[0]
    columns = weight.shape[1]
    extra = [] if acc is None else [acc]
    shapes = [jax.ShapeDtypeStruct((rows, columns), dtype)]
    shapes += [jax.ShapeDtypeStruct((pooled[0].shape[0], columns), F32)] if pooled else []
    return pl.pallas_call(
        functools.partial(out_kernel, count, pairs, len(pooled)),
        in_specs=[smem()] + [vmem()] * (count * pairs + len(pooled) + 1 + len(extra)),
        out_specs=[vmem()] * len(shapes) + [smem()],
        out_shape=shapes + [jax.ShapeDtypeStruct((1,), jnp.int32)],
        compiler_params=pltpu.CompilerParams(vmem_limit_bytes=VMEM_LIMIT),
        cost_estimate=COST,
        name="out",
    )(index, *[piece for part in parts for piece in part], *pooled, weight, *extra)


def pieces_kernel(ids_ref, keep_ref, got_ref, *out_refs):
    spread = len(out_refs)
    count = keep_ref.shape[0] // spread
    for k, ref in enumerate(out_refs):
        at = pl.ds(pl.multiple_of(lax.rem(ids_ref[0] + k, spread) * count, count), count)
        ref[...] = (keep_ref[at, :] + got_ref[at, :].astype(F32)).astype(ref.dtype)


def pool_pieces(place, keep, got, spread):
    count = keep.shape[0] // spread
    shape = (count, keep.shape[1])
    return pl.pallas_call(
        pieces_kernel,
        in_specs=[smem(), vmem(), vmem()],
        out_specs=[vmem()] * spread,
        out_shape=[jax.ShapeDtypeStruct(shape, F32)] + [jax.ShapeDtypeStruct(shape, BF)] * (spread - 1),
        compiler_params=pltpu.CompilerParams(vmem_limit_bytes=VMEM_LIMIT),
        cost_estimate=COST,
        name="pool_pieces",
    )(place, keep, got)


def own_kernel(ids_ref, bounds_ref, own_ref, *refs):
    total = own_ref[...]
    for ref in refs[:-1]:
        total = total + ref[...].astype(F32)
    count = total.shape[0]
    rows = [
        total[i : i + 1] / (bounds_ref[1, ids_ref[0] + i] - bounds_ref[0, ids_ref[0] + i]).astype(F32)
        for i in range(count)
    ]
    refs[-1][...] = jnp.concatenate(rows, axis=0).astype(BF)


def pool_own(place, bounds, own, others):
    return pl.pallas_call(
        own_kernel,
        in_specs=[smem(), smem()] + [vmem()] * (1 + len(others)),
        out_specs=vmem(),
        out_shape=jax.ShapeDtypeStruct(own.shape, BF),
        compiler_params=pltpu.CompilerParams(vmem_limit_bytes=VMEM_LIMIT),
        cost_estimate=COST,
        name="pool_own",
    )(place, bounds, own, *others)


def swap(values, axis, step):
    count = lax.axis_size(axis)
    return lax.ppermute(values, axis, [(i, i ^ step) for i in range(count)])


def across_heads(values, step):
    count = lax.axis_size("head")
    return lax.ppermute(values, "head", [(i, (i + step) % count) for i in range(count)])


def add_kernel(a_ref, b_ref, out_ref):
    count = a_ref.shape[0]
    out_ref[...] = (a_ref[...].astype(F32) + b_ref[:count, :].astype(F32)).astype(BF)


def add_call(a, b, cost=COST):
    return pl.pallas_call(
        add_kernel,
        in_specs=[vmem()] * 2,
        out_specs=vmem(),
        out_shape=jax.ShapeDtypeStruct(a.shape, BF),
        compiler_params=pltpu.CompilerParams(vmem_limit_bytes=VMEM_LIMIT),
        cost_estimate=cost,
        name="add",
    )(a, b)


def steps_of(axis):
    step = 1
    while step < lax.axis_size(axis):
        yield step
        step *= 2


def per_device(
    book_tokens,
    norm_gain,
    query_weight,
    key_weight,
    value_weight,
    proj_weight,
    dual_gains,
    out_weight,
    span_bounds,
):
    rows = book_tokens.shape[0]
    seq_devices = lax.axis_size(("seq", "rep"))
    seq_index = lax.axis_index(("seq", "rep"))
    head_devices = lax.axis_size("head")
    head_index = lax.axis_index("head")
    first_row = seq_index * rows
    all_pairs = query_weight.shape[1] // LANES
    groups = 2 if all_pairs % 2 == 0 else 1
    pairs = all_pairs // groups
    ids = jnp.stack(
        [lax.axis_index("rep"), (seq_index > 0).astype(jnp.int32), (seq_index < seq_devices - 1).astype(jnp.int32), first_row]
    ).astype(jnp.int32)
    gain = norm_gain[None, :]
    bounds = span_bounds.T

    both = ("seq", "rep")
    chips = [(i, i + 1) for i in range(1, seq_devices - 1, 2)]
    chips = chips + [(b, a) for a, b in chips]
    steps = list(steps_of("seq"))
    tie = lax.optimization_barrier

    fronts, mine, normed = [], [], book_tokens
    turn = ids
    fetched = []
    for g in range(groups):
        last = g == groups - 1
        normed, *outs = front(g == 0, last, g, pairs, turn, normed, gain, key_weight, value_weight, proj_weight,
                              dual_gains, [f[3] for f in fronts], fetched)
        outs, turn, fetched = outs[:4], outs[4], outs[5:]
        fronts.append(outs)
        send, edge = outs[2], outs[3]
        if last:
            for f in range(g):
                for step in steps[:-1]:
                    got, turn = tie((swap(mine[f], "seq", step), turn))
                    mine[f] = add_call(mine[f], got, LONG)
                mine[f], turn = tie((mine[f], turn))
        core = swap(send, "rep", 1)
        if last:
            chip = lax.ppermute(edge, both, chips)
        mine.append(add_call(outs[1], core))
        mine[g], turn = tie((mine[g], turn))

    if groups == 1:
        for step in steps[:-1]:
            mine[0] = add_call(mine[0], swap(mine[0], "seq", step))

    spread = lax.axis_size("seq")
    outs, before, arrived, others, other_index, queries = [], (), [], [], [], []
    for g in range(groups):
        source = queries[g] if g else normed
        *made, near_sums, turn = near(pairs, g, groups, turn, source, query_weight, core, chip, fronts[g][0])
        queries = queries if g else made
        q = made[0]
        got, turn = tie((swap(mine[g], "seq", steps[-1]), turn))
        total = add_call(mine[g], got)
        other = swap(total, "rep", 1)
        if g == groups - 2:
            for step in steps[:-1]:
                got, turn = tie((swap(mine[-1], "seq", step), turn))
                mine[-1] = add_call(mine[-1], got)
            mine[-1], turn = tie((mine[-1], turn))
        out = []
        for which in [[p] for p in range(pairs)] if g < groups - 1 else [list(range(pairs))]:
            *made, keep, send, turn = far(pairs, g, which, spread, turn, q, near_sums, total, other, dual_gains, bounds,
                                          before, arrived)
            before = [keep, send]
            out += made
        outs.append(out)
        moved = [[across_heads(piece, k) for piece in out] for k in range(1, head_devices)]
        arrived = [moved[0][0]] if g < groups - 1 and moved else []
        others += moved
        other_index += [lax.rem(head_index - k + head_devices, head_devices) * groups + g for k in range(1, head_devices)]

    own_index = [head_index * groups + g for g in range(groups)]
    early = len(others) - (head_devices - 1)

    keep, send = before
    place = lax.axis_index("seq").astype(jnp.int32)[None]
    own, *pieces = pool_pieces(place, keep, swap(send, "rep", 1), spread)
    pieces = [
        lax.ppermute(piece, "seq", [(i, (i + k + 1) % spread) for i in range(spread)]) for k, piece in enumerate(pieces)
    ]
    parts = outs + others[:early]
    index = jnp.stack(own_index + other_index[:early]).astype(jnp.int32)
    acc, turn = out_part(parts, index, out_weight, None, F32)
    place = (seq_index * own.shape[0]).astype(jnp.int32)[None]
    place = place + (turn - index[:1])
    own = pool_own(place, bounds, own, pieces)
    pooled = [own] + [across_heads(own, k) for k in range(1, head_devices)]
    pooled_index = [lax.rem(head_index - k + head_devices, head_devices) for k in range(head_devices)]
    index = jnp.stack(other_index[early:] + pooled_index).astype(jnp.int32)
    return tuple(out_part(others[early:], index, out_weight, acc, BF, pooled)[:2])


def solution(mesh):
    placed = (
        P(("groups", "seq", "rep"), None),
        P(),
        P(None, "head"),
        P(None, "head"),
        P(None, "head"),
        P(None, "head"),
        P(None, "head"),
        P(None, "head"),
        P("groups", None),
    )
    return jax.shard_map(
        per_device,
        mesh=mesh,
        in_specs=placed,
        out_specs=(P(("groups", "seq", "rep"), "head"), P(("groups", "seq", "rep"), "head")),
        check_vma=False,
    )
```

```python
import functools

import jax
import jax.numpy as jnp
from jax import lax
from jax.experimental import pallas as pl
from jax.experimental.pallas import tpu as pltpu
from jax.sharding import PartitionSpec as P

DH = 64
R = 256
SEG = 128
HALF = SEG // 2
LANES = 2 * DH
SCORE_SCALE = DH ** (-0.5)
LOG2E = 1.4426950408889634

VMEM_LIMIT = 40 << 20
COST = pl.CostEstimate(flops=1 << 20, bytes_accessed=1 << 10, transcendentals=0)

LONG = pl.CostEstimate(flops=1 << 33, bytes_accessed=1 << 10, transcendentals=0)
TURN = jax.ShapeDtypeStruct((4,), jnp.int32)

softcap = 5.0
epsilon = 1e-05

BF = jnp.bfloat16
F32 = jnp.float32


def dot(a, b, dims=((1,), (0,))):
    return lax.dot_general(a, b, (dims, ((), ())), preferred_element_type=F32)


def exp_capped(values, scale):
    return jnp.exp2((softcap * LOG2E) * jnp.tanh(values * (scale / softcap)))


def pass_turn(ids_ref, turn_ref):
    for i in range(4):
        turn_ref[i] = ids_ref[i]


def vmem():
    return pl.BlockSpec(memory_space=pltpu.VMEM)


def smem():
    return pl.BlockSpec(memory_space=pltpu.SMEM)


def head_norm(values, gain):
    out = []
    for at in range(0, values.shape[1], LANES):
        x = values[:, at : at + LANES]
        first = lane_is_first(x.shape)

        def mean(y):
            low = jnp.sum(jnp.where(first, y, 0.0), axis=-1, keepdims=True)
            high = jnp.sum(jnp.where(first, 0.0, y), axis=-1, keepdims=True)
            return jnp.where(first, low, high) * (1.0 / DH)

        centred = x - mean(x)
        spread = mean(centred * centred)
        out.append((centred * lax.rsqrt(spread + epsilon) * gain[:, at : at + LANES]).astype(BF))
    return jnp.concatenate(out, axis=1)


def token_norm(x, gain):
    x = x.astype(F32)
    centred = x - jnp.mean(x, axis=-1, keepdims=True)
    spread = jnp.mean(centred * centred, axis=-1, keepdims=True)
    return (centred * lax.rsqrt(spread + epsilon) * gain).astype(BF)


def edge_rows(near_ref):
    rows = near_ref.shape[0]
    columns = [slice(at, at + 2 * LANES) for at in range(0, near_ref.shape[1], 2 * LANES)]
    return [jnp.concatenate([near_ref[at, c] for c in columns], axis=0) for at in (slice(0, HALF), slice(rows - HALF, rows))]


def front_kernel(first, last, group, pairs, tile, *refs):
    ids_ref, refs = refs[0], list(refs[1:])
    if first:
        x_hbm, gain_hbm, dual_hbm, wk_hbm, wv_hbm, wp_hbm = refs[:6]
        refs = refs[6:]
    else:
        given_ref, dual_ref, kv_ref, wp_ref = refs[:4]
        refs = refs[4:]
        if not last:
            wk_hbm, wv_hbm, wp_hbm = refs[:3]
            refs = refs[3:]
    earlier = [refs.pop(0) for _ in range(group)] if last else []
    normed_ref, near_ref, keep_ref, send_ref, edge_ref, turn_ref = refs[:6]
    refs = refs[6:]
    pass_turn(ids_ref, turn_ref)
    if not last:
        next_kv_ref, next_wp_ref = refs[:2]
        refs = refs[2:]
    raw_ref, p_ref, sem = refs[:3]
    if first:
        kv_ref, wp_ref, x_ref, gain_ref, dual_ref = refs[3:]
    rows = normed_ref.shape[0]
    width = pairs * LANES
    chunks = rows // tile
    used = 0

    def copy(source, target):
        nonlocal used
        made = pltpu.make_async_copy(source, target, sem.at[used])
        used += 1
        made.start()
        return made

    def weight_copies(g, kv, wp):
        own = pl.ds(g * width, width)
        heads = [
            copy(wk_hbm.at[:, own], kv.at[:, pl.ds(0, width)]),
            copy(wv_hbm.at[:, own], kv.at[:, pl.ds(width, width)]),
        ]
        return heads, [copy(wp_hbm.at[:, pl.ds(g * pairs * 2 * R, pairs * 2 * R)], wp)]

    def token_copy(i):
        at = pl.ds(i * tile, tile)
        return copy(x_hbm.at[at, :], x_ref.at[at, :])

    kv_copies, proj_copies, next_copies = [], [], []
    if first:
        token_copies = [token_copy(0)]
        small_copies = [copy(gain_hbm, gain_ref), copy(dual_hbm, dual_ref)]
        kv_copies, proj_copies = weight_copies(group, kv_ref, wp_ref)
        token_copies += [token_copy(i) for i in range(1, chunks)]
    for i in range(chunks):
        at = pl.ds(i * tile, tile)
        if first:
            token_copies[i].wait()
            if i == 0:
                for made in small_copies:
                    made.wait()
            normed_ref[at, :] = token_norm(x_ref[at, :], gain_ref[...])
        normed = normed_ref[at, :]
        if i == 0:
            for made in kv_copies:
                made.wait()
        both = dot(normed, kv_ref[...])
        key, value = both[:, :width], both[:, width:]
        for p in range(pairs):
            cols = slice(p * LANES, (p + 1) * LANES)
            raw = jnp.concatenate([key[:, cols], value[:, cols]], axis=1).astype(BF)
            raw_ref[2 * p * LANES : 2 * (p + 1) * LANES, at] = raw.T
        if i == 0:
            for made in proj_copies:
                made.wait()
        if i == 0 and not last:
            next_copies = sum(weight_copies(group + 1, next_kv_ref, next_wp_ref), [])
        p_ref[at, :] = exp_capped(dot(normed, wp_ref[...]), 1.0).astype(BF)
        near_ref[at, :width] = head_norm(key, dual_ref[0:1, group * width : (group + 1) * width])
        near_ref[at, width:] = head_norm(value, dual_ref[1:2, group * width : (group + 1) * width])
    total = []
    for p in range(pairs):
        full = dot(raw_ref[2 * p * LANES : 2 * (p + 1) * LANES, :], p_ref[:, 2 * p * R : 2 * (p + 1) * R])
        for part in range(4):
            head = part % 2
            total.append(full[part * DH : (part + 1) * DH, head * R : (head + 1) * R])
    for made in next_copies:
        made.wait()
    total = jnp.concatenate(total, axis=0).astype(BF)
    half = total.shape[0] // 2
    mine = ids_ref[0] == 0
    keep_ref[...] = jnp.where(mine, total[:half], total[half:])
    send_ref[:half, :] = jnp.where(mine, total[half:], total[:half])
    head, tail = edge_rows(near_ref)
    edge = head.shape[0]
    if last:
        for i, ref in enumerate(earlier):
            before = jnp.where(mine, ref[edge:, :], ref[:edge, :])
            send_ref[half + i * edge : half + (i + 1) * edge, :] = before
            edge_ref[i * edge : (i + 1) * edge, :] = jnp.where(mine, ref[:edge, :], ref[edge:, :])
        send_ref[half + group * edge :, :] = jnp.where(mine, tail, head)
        edge_ref[group * edge :, :] = jnp.where(mine, head, tail)
    else:
        edge_ref[:edge, :] = head
        edge_ref[edge:, :] = tail


def in_hbm(values):
    return pltpu.with_memory_space_constraint(values, pltpu.HBM)


def front(first, last, group, pairs, ids, tokens, gain, wk, wv, wp, dual, earlier, fetched):
    rows, depth = tokens.shape
    width = pairs * LANES
    half = pairs * R // 2
    tile = min(512 if first else 256, rows)
    edge = (group + 1) * pairs * HALF if last else 0
    outs = [
        jax.ShapeDtypeStruct((rows, depth), BF),
        jax.ShapeDtypeStruct((rows, 2 * width), BF),
        jax.ShapeDtypeStruct((half, R), BF),
        jax.ShapeDtypeStruct((half + edge, R), BF),
        jax.ShapeDtypeStruct((edge if last else 2 * pairs * HALF, R), BF),
        TURN,
    ]
    if not last:
        outs += [jax.ShapeDtypeStruct((depth, 2 * width), BF), jax.ShapeDtypeStruct((depth, 2 * pairs * R), BF)]
    hbm = pl.BlockSpec(memory_space=pltpu.HBM)
    earlier = earlier if last else []
    weights = [in_hbm(wk), in_hbm(wv), in_hbm(wp)]
    if first:
        ins = [hbm] * 6
        args = [in_hbm(tokens), in_hbm(gain), in_hbm(dual)] + weights
    else:
        ins = [vmem()] * 4 + ([] if last else [hbm] * 3)
        args = [tokens, dual, *fetched] + ([] if last else weights)
    ins = [smem()] + ins + [vmem()] * len(earlier)
    args = [ids] + args + earlier
    scratch = [
        pltpu.VMEM((2 * width, rows), BF),
        pltpu.VMEM((rows, 2 * pairs * R), BF),
        pltpu.SemaphoreType.DMA((rows // tile + 8,)),
    ]
    if first:
        scratch += [
            pltpu.VMEM((depth, 2 * width), BF),
            pltpu.VMEM((depth, 2 * pairs * R), BF),
            pltpu.VMEM((rows, depth), BF),
            pltpu.VMEM((1, depth), F32),
            pltpu.VMEM(dual.shape, F32),
        ]
    is_turn = [o is TURN for o in outs]
    return pl.pallas_call(
        functools.partial(front_kernel, first, last, group, pairs, tile),
        input_output_aliases={} if first else {1: 0},
        in_specs=ins,
        out_specs=[smem() if t else vmem() for t in is_turn],
        out_shape=outs,
        scratch_shapes=scratch,
        compiler_params=pltpu.CompilerParams(vmem_limit_bytes=VMEM_LIMIT),
        cost_estimate=pl.CostEstimate(
            flops=2 * rows * depth * (2 * width + 2 * pairs * R), bytes_accessed=4 << 20, transcendentals=0
        ),
        name="front",
    )(*args)


def lane_is_first(shape):
    return lax.broadcasted_iota(jnp.int32, shape, 1) < DH


def stacked(q):
    first = lane_is_first(q.shape)
    zero = jnp.zeros_like(q)
    return jnp.concatenate([jnp.where(first, q, zero), jnp.where(first, zero, q)], axis=0)


def unstack(both):
    rows = both.shape[0] // 2
    first = lane_is_first((rows, LANES))
    return (
        jnp.where(first, both[:rows, :LANES], both[rows:, :LANES]),
        jnp.where(first, both[:rows, LANES:], both[rows:, LANES:]),
    )


def near_kernel(pairs, group, groups, ids_ref, *refs):
    width = pairs * LANES
    if group == 0:
        normed_ref, wq_ref, core_ref, chip_ref, near_ref = refs[:5]
        q_refs, (out_ref, turn_ref, pad_ref) = refs[5:-3], refs[-3:]
        q_ref, rows = q_refs[0], normed_ref.shape[0]
        for start in range(0, rows, 256):
            at = slice(start, start + 256)
            q = dot(normed_ref[at, :], wq_ref[...])
            for g in range(groups):
                q_refs[g][at, :] = q[:, g * width : (g + 1) * width].astype(BF)
    else:
        given_ref, core_ref, chip_ref, near_ref, q_ref, out_ref, turn_ref, pad_ref = refs
        rows = q_ref.shape[0]
    is_first = ids_ref[0] == 0
    row = lax.broadcasted_iota(jnp.int32, (2 * SEG, LANES), 0)
    ones = jnp.ones((2 * SEG, LANES), F32)
    has_prev = jnp.where(ids_ref[1] != 0, 1.0, 0.0)
    has_next = jnp.where(ids_ref[2] != 0, 1.0, 0.0)
    segments = rows // SEG
    offset = core_ref.shape[0] - chip_ref.shape[0]
    pad_ref[HALF : HALF + rows, :] = near_ref[...]
    for c in range(pairs):
        at = (group * pairs + c) * HALF
        core = core_ref[offset + at : offset + at + HALF, :]
        chip = chip_ref[at : at + HALF, :]
        lanes = slice(2 * c * LANES, 2 * (c + 1) * LANES)
        pad_ref[0:HALF, lanes] = jnp.where(is_first, chip, core)
        pad_ref[HALF + rows :, lanes] = jnp.where(is_first, core, chip)
    for s in range(segments):
        count = ones
        if s == 0:
            count = jnp.where(row < HALF, has_prev, count)
        if s == segments - 1:
            count = jnp.where(row >= 3 * HALF, has_next, count)
        count = count.astype(BF)
        window = pl.ds(s * SEG, 2 * SEG)
        here = slice(s * SEG, (s + 1) * SEG)
        for p in range(pairs):
            cols = slice(p * LANES, (p + 1) * LANES)
            scores = dot(stacked(q_ref[here, cols]), pad_ref[window, cols], ((1,), (1,)))
            weights = exp_capped(scores, SCORE_SCALE).astype(BF)
            values = jnp.concatenate([pad_ref[window, width + p * LANES : width + (p + 1) * LANES], count], axis=1)
            top, bottom = unstack(dot(weights, values))
            out_ref[here, 2 * p * LANES : (2 * p + 1) * LANES] = top
            out_ref[here, (2 * p + 1) * LANES : (2 * p + 2) * LANES] = bottom
    pass_turn(ids_ref, turn_ref)


def near(pairs, group, groups, ids, source, wq, core, chip, near_pairs):
    rows = near_pairs.shape[0]
    width = pairs * LANES
    q = jax.ShapeDtypeStruct((rows, width), BF)
    count = groups if group == 0 else 1
    args = [source, wq] if group == 0 else [source]
    return pl.pallas_call(
        functools.partial(near_kernel, pairs, group, groups),
        in_specs=[smem()] + [vmem()] * (len(args) + 3),
        out_specs=[vmem()] * (count + 1) + [smem()],
        out_shape=[q] * count + [jax.ShapeDtypeStruct((rows, 2 * width), F32), TURN],
        input_output_aliases={} if group == 0 else {1: 0},
        scratch_shapes=[pltpu.VMEM((rows + SEG, 2 * width), BF)],
        compiler_params=pltpu.CompilerParams(vmem_limit_bytes=VMEM_LIMIT),
        cost_estimate=COST,
        name="near",
    )(ids, *args, core, chip, near_pairs)


def far_kernel(pairs, group, part, block, spread, waits, final, *refs):
    ids_ref, q_ref, near_ref, gains_ref = refs[:4]
    refs = refs[4:]
    is_first = ids_ref[0] == 0
    if part == "all":
        mine, other = refs[0][...], refs[1][...]
        total = jnp.concatenate([jnp.where(is_first, mine, other), jnp.where(is_first, other, mine)], axis=0)
        p, refs = 0, refs[2:]
    else:
        total = refs[0][...]
        p, refs = ids_ref[0] if part == "own" else 1 - ids_ref[0], refs[1:]
    refs = refs[waits:]
    if final:
        bounds_ref, *earlier = refs[:-4]
        out_ref, keep_ref, send_ref, turn_ref = refs[-4:]
    else:
        out_ref, turn_ref = refs
    pass_turn(ids_ref, turn_ref)
    rows = q_ref.shape[0]

    def lanes(offset, scale=1):
        start = (offset + p) * scale * LANES
        return pl.ds(start if part == "all" else pl.multiple_of(start, LANES), scale * LANES)

    gains = jnp.concatenate([gains_ref[:, lanes(group * pairs)]] * 2, axis=0).T

    def land(kind):
        parts = []
        for h in range(2):
            at = kind * LANES + h * DH
            values = total[at : at + DH].astype(F32)
            centred = values - jnp.mean(values, axis=0, keepdims=True)
            spread = jnp.mean(centred * centred, axis=0, keepdims=True)
            gain = gains[h * DH : (h + 1) * DH, 2 + kind : 3 + kind]
            parts.append((centred * lax.rsqrt(spread + epsilon) * gain).astype(BF))
        return jnp.concatenate(parts, axis=0)

    keys = land(0)
    values = jnp.concatenate([land(1), jnp.ones((LANES, R), BF)], axis=0)
    for start in range(0, rows, block):
        at = slice(start, start + block)
        weights = exp_capped(dot(stacked(q_ref[at, lanes(0)]), keys), SCORE_SCALE).astype(BF)
        top, bottom = unstack(dot(weights, values, ((1,), (1,))))
        near_sums = near_ref[at, lanes(0, 2)]
        out_ref[at, :] = ((top + near_sums[:, :LANES]) / (bottom + near_sums[:, LANES:])).astype(BF)
    if not final:
        return
    spans = bounds_ref.shape[1]
    position = ids_ref[3] + lax.broadcasted_iota(jnp.int32, (rows, spans), 0)
    member = (position >= bounds_ref[0:1, :]) & (position < bounds_ref[1:2, :])
    pieces = jnp.concatenate([ref[...] for ref in earlier + [out_ref]], axis=1)
    sums = dot(jnp.where(member, 1.0, 0.0).astype(BF), pieces, ((0,), (0,)))
    if part != "all":
        ordered = []
        for at in range(0, sums.shape[1], 2 * LANES):
            low, high = sums[:, at : at + LANES], sums[:, at + LANES : at + 2 * LANES]
            ordered += [jnp.where(is_first, low, high), jnp.where(is_first, high, low)]
        sums = jnp.concatenate(ordered, axis=1)
    count = spans // (2 * spread)
    even = jnp.concatenate([sums[2 * i * count : (2 * i + 1) * count] for i in range(spread)], axis=0)
    odd = jnp.concatenate([sums[(2 * i + 1) * count : (2 * i + 2) * count] for i in range(spread)], axis=0)
    keep_ref[...] = jnp.where(is_first, even, odd)
    send_ref[...] = jnp.where(is_first, odd, even).astype(BF)


def far(pairs, group, part, spread, ids, q, near_sums, gains, halves, arrived, final):
    rows = q.shape[0]
    shapes = [jax.ShapeDtypeStruct((rows, LANES), BF)]
    if final:
        shape = (final[0].shape[1] // 2, len(final) * LANES)
        shapes += [jax.ShapeDtypeStruct(shape, F32), jax.ShapeDtypeStruct(shape, BF)]
    return pl.pallas_call(
        functools.partial(far_kernel, pairs, group, part, 256, spread, len(arrived), bool(final)),
        in_specs=[smem()]
        + [vmem()] * (3 + len(halves))
        + [pl.BlockSpec(memory_space=pl.ANY)] * len(arrived)
        + [vmem()] * len(final),
        out_specs=[vmem()] * len(shapes) + [smem()],
        out_shape=shapes + [TURN],
        compiler_params=pltpu.CompilerParams(vmem_limit_bytes=VMEM_LIMIT),
        cost_estimate=COST,
        name="far",
    )(ids, q, near_sums, gains, *halves, *arrived, *final)


def out_kernel(count, pairs, spans, *refs):
    ids_ref, refs = refs[0], refs[1:]
    tokens, refs = [refs[j * pairs : (j + 1) * pairs] for j in range(count)], refs[count * pairs :]
    pooled, refs = refs[:spans], refs[spans:]
    *refs, turn_ref = refs
    turn_ref[0] = ids_ref[0]
    outs = refs[-2:] if spans else refs[-1:]
    weight_ref, *acc = refs[: -len(outs)]
    rows, width = tokens[0][0].shape[0], pairs * LANES
    tile = min(256, rows)

    def weight(j, size):
        return weight_ref[pl.ds(pl.multiple_of(ids_ref[j] * size, size), size), :]

    def head_weight(j):
        if pairs == 1:
            return weight(j, width)
        first = ids_ref[count + spans]
        blocks = [weight_ref[pl.ds(pl.multiple_of(ids_ref[j] * width + p * LANES, LANES), LANES), :] for p in (first, 1 - first)]
        return jnp.concatenate(blocks, axis=0)

    weights = [head_weight(j) for j in range(count)]

    for start in range(0, rows, tile):
        at = slice(start, start + tile)
        total = acc[0][at, :] if acc else None
        for j in range(count):
            term = dot(jnp.concatenate([ref[at, :] for ref in tokens[j]], axis=1), weights[j])
            total = term if total is None else total + term
        outs[0][at, :] = total.astype(outs[0].dtype)
    if spans:
        outs[1][...] = sum(dot(ref[...], weight(count + k, ref.shape[1])) for k, ref in enumerate(pooled))


def out_part(parts, index, weight, acc, dtype, pooled=()):
    count = len(parts)
    pairs = len(parts[0])
    rows = parts[0][0].shape[0]
    columns = weight.shape[1]
    extra = [] if acc is None else [acc]
    shapes = [jax.ShapeDtypeStruct((rows, columns), dtype)]
    shapes += [jax.ShapeDtypeStruct((pooled[0].shape[0], columns), F32)] if pooled else []
    return pl.pallas_call(
        functools.partial(out_kernel, count, pairs, len(pooled)),
        in_specs=[smem()] + [vmem()] * (count * pairs + len(pooled) + 1 + len(extra)),
        out_specs=[vmem()] * len(shapes) + [smem()],
        out_shape=shapes + [jax.ShapeDtypeStruct((1,), jnp.int32)],
        compiler_params=pltpu.CompilerParams(vmem_limit_bytes=VMEM_LIMIT),
        cost_estimate=COST,
        name="out",
    )(index, *[piece for part in parts for piece in part], *pooled, weight, *extra)


def pieces_kernel(ids_ref, keep_ref, got_ref, *out_refs):
    spread = len(out_refs)
    count = keep_ref.shape[0] // spread
    for k, ref in enumerate(out_refs):
        at = pl.ds(pl.multiple_of(lax.rem(ids_ref[0] + k, spread) * count, count), count)
        ref[...] = (keep_ref[at, :] + got_ref[at, :].astype(F32)).astype(ref.dtype)


def pool_pieces(place, keep, got, spread):
    count = keep.shape[0] // spread
    shape = (count, keep.shape[1])
    return pl.pallas_call(
        pieces_kernel,
        in_specs=[smem(), vmem(), vmem()],
        out_specs=[vmem()] * spread,
        out_shape=[jax.ShapeDtypeStruct(shape, F32)] + [jax.ShapeDtypeStruct(shape, BF)] * (spread - 1),
        compiler_params=pltpu.CompilerParams(vmem_limit_bytes=VMEM_LIMIT),
        cost_estimate=COST,
        name="pool_pieces",
    )(place, keep, got)


def own_kernel(ids_ref, bounds_ref, own_ref, *refs):
    total = own_ref[...]
    for ref in refs[:-1]:
        total = total + ref[...].astype(F32)
    count = total.shape[0]
    rows = [
        total[i : i + 1] / (bounds_ref[1, ids_ref[0] + i] - bounds_ref[0, ids_ref[0] + i]).astype(F32)
        for i in range(count)
    ]
    refs[-1][...] = jnp.concatenate(rows, axis=0).astype(BF)


def pool_own(place, bounds, own, others):
    return pl.pallas_call(
        own_kernel,
        in_specs=[smem(), smem()] + [vmem()] * (1 + len(others)),
        out_specs=vmem(),
        out_shape=jax.ShapeDtypeStruct(own.shape, BF),
        compiler_params=pltpu.CompilerParams(vmem_limit_bytes=VMEM_LIMIT),
        cost_estimate=COST,
        name="pool_own",
    )(place, bounds, own, *others)


def swap(values, axis, step):
    count = lax.axis_size(axis)
    return lax.ppermute(values, axis, [(i, i ^ step) for i in range(count)])


def across_heads(values, step):
    count = lax.axis_size("head")
    return lax.ppermute(values, "head", [(i, (i + step) % count) for i in range(count)])


def add_kernel(a_ref, b_ref, out_ref):
    count = a_ref.shape[0]
    out_ref[...] = (a_ref[...].astype(F32) + b_ref[:count, :].astype(F32)).astype(BF)


def add_call(a, b, cost=COST):
    return pl.pallas_call(
        add_kernel,
        in_specs=[vmem()] * 2,
        out_specs=vmem(),
        out_shape=jax.ShapeDtypeStruct(a.shape, BF),
        compiler_params=pltpu.CompilerParams(vmem_limit_bytes=VMEM_LIMIT),
        cost_estimate=cost,
        name="add",
    )(a, b)


def steps_of(axis):
    step = 1
    while step < lax.axis_size(axis):
        yield step
        step *= 2


def per_device(
    book_tokens,
    norm_gain,
    query_weight,
    key_weight,
    value_weight,
    proj_weight,
    dual_gains,
    out_weight,
    span_bounds,
):
    rows = book_tokens.shape[0]
    seq_devices = lax.axis_size(("seq", "rep"))
    seq_index = lax.axis_index(("seq", "rep"))
    head_devices = lax.axis_size("head")
    head_index = lax.axis_index("head")
    first_row = seq_index * rows
    all_pairs = query_weight.shape[1] // LANES
    groups = 2 if all_pairs == 4 else all_pairs
    pairs = all_pairs // groups
    ids = jnp.stack(
        [lax.axis_index("rep"), (seq_index > 0).astype(jnp.int32), (seq_index < seq_devices - 1).astype(jnp.int32), first_row]
    ).astype(jnp.int32)
    gain = norm_gain[None, :]
    bounds = span_bounds.T

    both = ("seq", "rep")
    chips = [(i, i + 1) for i in range(1, seq_devices - 1, 2)]
    chips = chips + [(b, a) for a, b in chips]
    steps = list(steps_of("seq"))
    tie = lax.optimization_barrier

    fronts, mine, normed = [], [], book_tokens
    turn = ids
    fetched = []
    for g in range(groups):
        last = g == groups - 1
        normed, *outs = front(g == 0, last, g, pairs, turn, normed, gain, key_weight, value_weight, proj_weight,
                              dual_gains, [f[3] for f in fronts], fetched)
        outs, turn, fetched = outs[:4], outs[4], outs[5:]
        fronts.append(outs)
        send, edge = outs[2], outs[3]
        if last:
            for f in range(g):
                for step in steps[:-1]:
                    got, turn = tie((swap(mine[f], "seq", step), turn))
                    mine[f] = add_call(mine[f], got, LONG)
                mine[f], turn = tie((mine[f], turn))
        core = swap(send, "rep", 1)
        if last:
            chip = lax.ppermute(edge, both, chips)
        mine.append(add_call(outs[1], core))
        mine[g], turn = tie((mine[g], turn))

    if groups == 1:
        for step in steps[:-1]:
            mine[0] = add_call(mine[0], swap(mine[0], "seq", step))

    spread = lax.axis_size("seq")
    outs, arrived, others, other_index, queries = [], [], [], [], []
    for g in range(groups):
        source = queries[g] if g else normed
        *made, near_sums, turn = near(pairs, g, groups, turn, source, query_weight, core, chip, fronts[g][0])
        queries = queries if g else made
        q = made[0]
        got, turn = tie((swap(mine[g], "seq", steps[-1]), turn))
        total = add_call(mine[g], got)
        other = swap(total, "rep", 1)
        if g == groups - 2:
            for step in steps[:-1]:
                got, turn = tie((swap(mine[-1], "seq", step), turn))
                mine[-1] = add_call(mine[-1], got)
            mine[-1], turn = tie((mine[-1], turn))
        out = []
        calls = [("own", [total]), ("other", [other])] if pairs == 2 else [("all", [total, other])]
        for part, halves in calls:
            final = []
            if g == groups - 1 and part != "own":
                final = [bounds] + [piece for o in outs for piece in o] + out
            made, *sums, turn = far(pairs, g, part, spread, turn, q, near_sums, dual_gains, halves, arrived, final)
            arrived = []
            out.append(made)
        outs.append(out)
        moved = [[across_heads(piece, k) for piece in out] for k in range(1, head_devices)]
        arrived = [moved[0][0]] if g < groups - 1 and moved else []
        others += moved
        other_index += [lax.rem(head_index - k + head_devices, head_devices) * groups + g for k in range(1, head_devices)]

    own_index = [head_index * groups + g for g in range(groups)]
    early = len(others) - (head_devices - 1)

    keep, send = sums
    place = lax.axis_index("seq").astype(jnp.int32)[None]
    own, *pieces = pool_pieces(place, keep, swap(send, "rep", 1), spread)
    pieces = [
        lax.ppermute(piece, "seq", [(i, (i + k + 1) % spread) for i in range(spread)]) for k, piece in enumerate(pieces)
    ]
    parts = outs + others[:early]
    index = jnp.stack(own_index + other_index[:early] + [lax.axis_index("rep")]).astype(jnp.int32)
    acc, turn = out_part(parts, index, out_weight, None, F32)
    place = (seq_index * own.shape[0]).astype(jnp.int32)[None]
    place = place + (turn - index[:1])
    own = pool_own(place, bounds, own, pieces)
    pooled = [own] + [across_heads(own, k) for k in range(1, head_devices)]
    pooled_index = [lax.rem(head_index - k + head_devices, head_devices) for k in range(head_devices)]
    index = jnp.stack(other_index[early:] + pooled_index + [lax.axis_index("rep")]).astype(jnp.int32)
    return tuple(out_part(others[early:], index, out_weight, acc, BF, pooled)[:2])


def solution(mesh):
    placed = (
        P(("groups", "seq", "rep"), None),
        P(),
        P(None, "head"),
        P(None, "head"),
        P(None, "head"),
        P(None, "head"),
        P(None, "head"),
        P(None, "head"),
        P("groups", None),
    )
    return jax.shard_map(
        per_device,
        mesh=mesh,
        in_specs=placed,
        out_specs=(P(("groups", "seq", "rep"), "head"), P(("groups", "seq", "rep"), "head")),
        check_vma=False,
    )
```

```python
import functools

import jax
import jax.numpy as jnp
from jax import lax
from jax.experimental import pallas as pl
from jax.experimental.pallas import tpu as pltpu
from jax.sharding import PartitionSpec as P

DH = 64
R = 256
SEG = 128
HALF = SEG // 2
LANES = 2 * DH
SCORE_SCALE = DH ** (-0.5)
LOG2E = 1.4426950408889634

VMEM_LIMIT = 40 << 20
COST = pl.CostEstimate(flops=1 << 20, bytes_accessed=1 << 10, transcendentals=0)

LONG = pl.CostEstimate(flops=1 << 33, bytes_accessed=1 << 10, transcendentals=0)
TURN = jax.ShapeDtypeStruct((4,), jnp.int32)

softcap = 5.0
epsilon = 1e-05

BF = jnp.bfloat16
F32 = jnp.float32


def dot(a, b, dims=((1,), (0,))):
    return lax.dot_general(a, b, (dims, ((), ())), preferred_element_type=F32)


def exp_capped(values, scale):
    return jnp.exp2((softcap * LOG2E) * jnp.tanh(values * (scale / softcap)))


def pass_turn(ids_ref, turn_ref):
    for i in range(4):
        turn_ref[i] = ids_ref[i]


def vmem():
    return pl.BlockSpec(memory_space=pltpu.VMEM)


def smem():
    return pl.BlockSpec(memory_space=pltpu.SMEM)


def head_norm(values, gain):
    out = []
    for at in range(0, values.shape[1], LANES):
        x = values[:, at : at + LANES]
        first = lane_is_first(x.shape)

        def mean(y):
            low = jnp.sum(jnp.where(first, y, 0.0), axis=-1, keepdims=True)
            high = jnp.sum(jnp.where(first, 0.0, y), axis=-1, keepdims=True)
            return jnp.where(first, low, high) * (1.0 / DH)

        centred = x - mean(x)
        spread = mean(centred * centred)
        out.append((centred * lax.rsqrt(spread + epsilon) * gain[:, at : at + LANES]).astype(BF))
    return jnp.concatenate(out, axis=1)


def token_norm(x, gain):
    x = x.astype(F32)
    centred = x - jnp.mean(x, axis=-1, keepdims=True)
    spread = jnp.mean(centred * centred, axis=-1, keepdims=True)
    return (centred * lax.rsqrt(spread + epsilon) * gain).astype(BF)


def edge_rows(near_ref):
    rows = near_ref.shape[0]
    columns = [slice(at, at + 2 * LANES) for at in range(0, near_ref.shape[1], 2 * LANES)]
    return [jnp.concatenate([near_ref[at, c] for c in columns], axis=0) for at in (slice(0, HALF), slice(rows - HALF, rows))]


def front_kernel(first, last, group, pairs, tile, *refs):
    ids_ref, refs = refs[0], list(refs[1:])
    if first:
        x_hbm, gain_hbm, dual_hbm, wk_hbm, wv_hbm, wp_hbm = refs[:6]
        refs = refs[6:]
    else:
        given_ref, dual_ref, kv_ref, wp_ref = refs[:4]
        refs = refs[4:]
        if not last:
            wk_hbm, wv_hbm, wp_hbm = refs[:3]
            refs = refs[3:]
    earlier = [refs.pop(0) for _ in range(group)] if last else []
    normed_ref, near_ref, keep_ref, send_ref, edge_ref, turn_ref = refs[:6]
    refs = refs[6:]
    pass_turn(ids_ref, turn_ref)
    if not last:
        next_kv_ref, next_wp_ref = refs[:2]
        refs = refs[2:]
    raw_ref, p_ref, sem = refs[:3]
    if first:
        kv_ref, wp_ref, x_ref, gain_ref, dual_ref = refs[3:]
    rows = normed_ref.shape[0]
    width = pairs * LANES
    chunks = rows // tile
    used = 0

    def copy(source, target):
        nonlocal used
        made = pltpu.make_async_copy(source, target, sem.at[used])
        used += 1
        made.start()
        return made

    def weight_copies(g, kv, wp):
        own = pl.ds(g * width, width)
        heads = [
            copy(wk_hbm.at[:, own], kv.at[:, pl.ds(0, width)]),
            copy(wv_hbm.at[:, own], kv.at[:, pl.ds(width, width)]),
        ]
        return heads, [copy(wp_hbm.at[:, pl.ds(g * pairs * 2 * R, pairs * 2 * R)], wp)]

    def token_copy(i):
        at = pl.ds(i * tile, tile)
        return copy(x_hbm.at[at, :], x_ref.at[at, :])

    kv_copies, proj_copies, next_copies = [], [], []
    if first:
        token_copies = [token_copy(0)]
        small_copies = [copy(gain_hbm, gain_ref), copy(dual_hbm, dual_ref)]
        kv_copies, proj_copies = weight_copies(group, kv_ref, wp_ref)
        token_copies += [token_copy(i) for i in range(1, chunks)]
    for i in range(chunks):
        at = pl.ds(i * tile, tile)
        if first:
            token_copies[i].wait()
            if i == 0:
                for made in small_copies:
                    made.wait()
            normed_ref[at, :] = token_norm(x_ref[at, :], gain_ref[...])
        normed = normed_ref[at, :]
        if i == 0:
            for made in kv_copies:
                made.wait()
        both = dot(normed, kv_ref[...])
        key, value = both[:, :width], both[:, width:]
        for p in range(pairs):
            cols = slice(p * LANES, (p + 1) * LANES)
            raw = jnp.concatenate([key[:, cols], value[:, cols]], axis=1).astype(BF)
            raw_ref[2 * p * LANES : 2 * (p + 1) * LANES, at] = raw.T
        if i == 0:
            for made in proj_copies:
                made.wait()
        if i == 0 and not last:
            next_copies = sum(weight_copies(group + 1, next_kv_ref, next_wp_ref), [])
        p_ref[at, :] = exp_capped(dot(normed, wp_ref[...]), 1.0).astype(BF)
        near_ref[at, :width] = head_norm(key, dual_ref[0:1, group * width : (group + 1) * width])
        near_ref[at, width:] = head_norm(value, dual_ref[1:2, group * width : (group + 1) * width])
    total = []
    for p in range(pairs):
        full = dot(raw_ref[2 * p * LANES : 2 * (p + 1) * LANES, :], p_ref[:, 2 * p * R : 2 * (p + 1) * R])
        for part in range(4):
            head = part % 2
            total.append(full[part * DH : (part + 1) * DH, head * R : (head + 1) * R])
    for made in next_copies:
        made.wait()
    total = jnp.concatenate(total, axis=0).astype(BF)
    half = total.shape[0] // 2
    mine = ids_ref[0] == 0
    keep_ref[...] = jnp.where(mine, total[:half], total[half:])
    send_ref[:half, :] = jnp.where(mine, total[half:], total[:half])
    head, tail = edge_rows(near_ref)
    edge = head.shape[0]
    if last:
        for i, ref in enumerate(earlier):
            before = jnp.where(mine, ref[edge:, :], ref[:edge, :])
            send_ref[half + i * edge : half + (i + 1) * edge, :] = before
            edge_ref[i * edge : (i + 1) * edge, :] = jnp.where(mine, ref[:edge, :], ref[edge:, :])
        send_ref[half + group * edge :, :] = jnp.where(mine, tail, head)
        edge_ref[group * edge :, :] = jnp.where(mine, head, tail)
    else:
        edge_ref[:edge, :] = head
        edge_ref[edge:, :] = tail


def in_hbm(values):
    return pltpu.with_memory_space_constraint(values, pltpu.HBM)


def front(first, last, group, pairs, ids, tokens, gain, wk, wv, wp, dual, earlier, fetched):
    rows, depth = tokens.shape
    width = pairs * LANES
    half = pairs * R // 2
    tile = min(512 if first else 256, rows)
    edge = (group + 1) * pairs * HALF if last else 0
    outs = [
        jax.ShapeDtypeStruct((rows, depth), BF),
        jax.ShapeDtypeStruct((rows, 2 * width), BF),
        jax.ShapeDtypeStruct((half, R), BF),
        jax.ShapeDtypeStruct((half + edge, R), BF),
        jax.ShapeDtypeStruct((edge if last else 2 * pairs * HALF, R), BF),
        TURN,
    ]
    if not last:
        outs += [jax.ShapeDtypeStruct((depth, 2 * width), BF), jax.ShapeDtypeStruct((depth, 2 * pairs * R), BF)]
    hbm = pl.BlockSpec(memory_space=pltpu.HBM)
    earlier = earlier if last else []
    weights = [in_hbm(wk), in_hbm(wv), in_hbm(wp)]
    if first:
        ins = [hbm] * 6
        args = [in_hbm(tokens), in_hbm(gain), in_hbm(dual)] + weights
    else:
        ins = [vmem()] * 4 + ([] if last else [hbm] * 3)
        args = [tokens, dual, *fetched] + ([] if last else weights)
    ins = [smem()] + ins + [vmem()] * len(earlier)
    args = [ids] + args + earlier
    scratch = [
        pltpu.VMEM((2 * width, rows), BF),
        pltpu.VMEM((rows, 2 * pairs * R), BF),
        pltpu.SemaphoreType.DMA((rows // tile + 8,)),
    ]
    if first:
        scratch += [
            pltpu.VMEM((depth, 2 * width), BF),
            pltpu.VMEM((depth, 2 * pairs * R), BF),
            pltpu.VMEM((rows, depth), BF),
            pltpu.VMEM((1, depth), F32),
            pltpu.VMEM(dual.shape, F32),
        ]
    is_turn = [o is TURN for o in outs]
    return pl.pallas_call(
        functools.partial(front_kernel, first, last, group, pairs, tile),
        input_output_aliases={} if first else {1: 0},
        in_specs=ins,
        out_specs=[smem() if t else vmem() for t in is_turn],
        out_shape=outs,
        scratch_shapes=scratch,
        compiler_params=pltpu.CompilerParams(vmem_limit_bytes=VMEM_LIMIT),
        cost_estimate=pl.CostEstimate(
            flops=2 * rows * depth * (2 * width + 2 * pairs * R), bytes_accessed=4 << 20, transcendentals=0
        ),
        name="front",
    )(*args)


def lane_is_first(shape):
    return lax.broadcasted_iota(jnp.int32, shape, 1) < DH


def stacked(q):
    first = lane_is_first(q.shape)
    zero = jnp.zeros_like(q)
    return jnp.concatenate([jnp.where(first, q, zero), jnp.where(first, zero, q)], axis=0)


def unstack(both):
    rows = both.shape[0] // 2
    first = lane_is_first((rows, LANES))
    return (
        jnp.where(first, both[:rows, :LANES], both[rows:, :LANES]),
        jnp.where(first, both[:rows, LANES:], both[rows:, LANES:]),
    )


def near_kernel(pairs, group, groups, ids_ref, *refs):
    width = pairs * LANES
    if group == 0:
        normed_ref, wq_ref, core_ref, chip_ref, near_ref = refs[:5]
        q_refs, (out_ref, turn_ref, pad_ref) = refs[5:-3], refs[-3:]
        q_ref, rows = q_refs[0], normed_ref.shape[0]
        for start in range(0, rows, 256):
            at = slice(start, start + 256)
            q = dot(normed_ref[at, :], wq_ref[...])
            for g in range(groups):
                q_refs[g][at, :] = q[:, g * width : (g + 1) * width].astype(BF)
    else:
        given_ref, core_ref, chip_ref, near_ref, q_ref, out_ref, turn_ref, pad_ref = refs
        rows = q_ref.shape[0]
    is_first = ids_ref[0] == 0
    row = lax.broadcasted_iota(jnp.int32, (2 * SEG, LANES), 0)
    ones = jnp.ones((2 * SEG, LANES), F32)
    has_prev = jnp.where(ids_ref[1] != 0, 1.0, 0.0)
    has_next = jnp.where(ids_ref[2] != 0, 1.0, 0.0)
    segments = rows // SEG
    offset = core_ref.shape[0] - chip_ref.shape[0]
    pad_ref[HALF : HALF + rows, :] = near_ref[...]
    for c in range(pairs):
        at = (group * pairs + c) * HALF
        core = core_ref[offset + at : offset + at + HALF, :]
        chip = chip_ref[at : at + HALF, :]
        lanes = slice(2 * c * LANES, 2 * (c + 1) * LANES)
        pad_ref[0:HALF, lanes] = jnp.where(is_first, chip, core)
        pad_ref[HALF + rows :, lanes] = jnp.where(is_first, core, chip)
    for s in range(segments):
        count = ones
        if s == 0:
            count = jnp.where(row < HALF, has_prev, count)
        if s == segments - 1:
            count = jnp.where(row >= 3 * HALF, has_next, count)
        count = count.astype(BF)
        window = pl.ds(s * SEG, 2 * SEG)
        here = slice(s * SEG, (s + 1) * SEG)
        for p in range(pairs):
            cols = slice(p * LANES, (p + 1) * LANES)
            scores = dot(stacked(q_ref[here, cols]), pad_ref[window, cols], ((1,), (1,)))
            weights = exp_capped(scores, SCORE_SCALE).astype(BF)
            values = jnp.concatenate([pad_ref[window, width + p * LANES : width + (p + 1) * LANES], count], axis=1)
            top, bottom = unstack(dot(weights, values))
            out_ref[here, 2 * p * LANES : (2 * p + 1) * LANES] = top
            out_ref[here, (2 * p + 1) * LANES : (2 * p + 2) * LANES] = bottom
    pass_turn(ids_ref, turn_ref)


def near(pairs, group, groups, ids, source, wq, core, chip, near_pairs):
    rows = near_pairs.shape[0]
    width = pairs * LANES
    q = jax.ShapeDtypeStruct((rows, width), BF)
    count = groups if group == 0 else 1
    args = [source, wq] if group == 0 else [source]
    return pl.pallas_call(
        functools.partial(near_kernel, pairs, group, groups),
        in_specs=[smem()] + [vmem()] * (len(args) + 3),
        out_specs=[vmem()] * (count + 1) + [smem()],
        out_shape=[q] * count + [jax.ShapeDtypeStruct((rows, 2 * width), F32), TURN],
        input_output_aliases={} if group == 0 else {1: 0},
        scratch_shapes=[pltpu.VMEM((rows + SEG, 2 * width), BF)],
        compiler_params=pltpu.CompilerParams(vmem_limit_bytes=VMEM_LIMIT),
        cost_estimate=COST,
        name="near",
    )(ids, *args, core, chip, near_pairs)


def far_kernel(pairs, group, part, block, spread, waits, final, *refs):
    ids_ref, q_ref, near_ref, gains_ref = refs[:4]
    refs = refs[4:]
    is_first = ids_ref[0] == 0
    if part == "all":
        mine, other = refs[0][...], refs[1][...]
        total = jnp.concatenate([jnp.where(is_first, mine, other), jnp.where(is_first, other, mine)], axis=0)
        p, refs = 0, refs[2:]
    else:
        total = refs[0][...]
        p, refs = ids_ref[0] if part == "own" else 1 - ids_ref[0], refs[1:]
    refs = refs[waits:]
    if final:
        bounds_ref, *earlier = refs[:-4]
        out_ref, keep_ref, send_ref, turn_ref = refs[-4:]
    else:
        out_ref, turn_ref = refs
    pass_turn(ids_ref, turn_ref)
    rows = q_ref.shape[0]

    def lanes(offset, scale=1):
        start = (offset + p) * scale * LANES
        return pl.ds(start if part == "all" else pl.multiple_of(start, LANES), scale * LANES)

    gains = jnp.concatenate([gains_ref[:, lanes(group * pairs)]] * 2, axis=0).T

    def land(kind):
        parts = []
        for h in range(2):
            at = kind * LANES + h * DH
            values = total[at : at + DH].astype(F32)
            centred = values - jnp.mean(values, axis=0, keepdims=True)
            spread = jnp.mean(centred * centred, axis=0, keepdims=True)
            gain = gains[h * DH : (h + 1) * DH, 2 + kind : 3 + kind]
            parts.append((centred * lax.rsqrt(spread + epsilon) * gain).astype(BF))
        return jnp.concatenate(parts, axis=0)

    keys = land(0)
    values = jnp.concatenate([land(1), jnp.ones((LANES, R), BF)], axis=0)
    for start in range(0, rows, block):
        at = slice(start, start + block)
        weights = exp_capped(dot(stacked(q_ref[at, lanes(0)]), keys), SCORE_SCALE).astype(BF)
        top, bottom = unstack(dot(weights, values, ((1,), (1,))))
        near_sums = near_ref[at, lanes(0, 2)]
        out_ref[at, :] = ((top + near_sums[:, :LANES]) / (bottom + near_sums[:, LANES:])).astype(BF)
    if not final:
        return
    spans = bounds_ref.shape[1]
    position = ids_ref[3] + lax.broadcasted_iota(jnp.int32, (rows, spans), 0)
    member = (position >= bounds_ref[0:1, :]) & (position < bounds_ref[1:2, :])
    pieces = jnp.concatenate([ref[...] for ref in earlier + [out_ref]], axis=1)
    sums = dot(jnp.where(member, 1.0, 0.0).astype(BF), pieces, ((0,), (0,)))
    if part != "all":
        ordered = []
        for at in range(0, sums.shape[1], 2 * LANES):
            low, high = sums[:, at : at + LANES], sums[:, at + LANES : at + 2 * LANES]
            ordered += [jnp.where(is_first, low, high), jnp.where(is_first, high, low)]
        sums = jnp.concatenate(ordered, axis=1)
    count = spans // (2 * spread)
    even = jnp.concatenate([sums[2 * i * count : (2 * i + 1) * count] for i in range(spread)], axis=0)
    odd = jnp.concatenate([sums[(2 * i + 1) * count : (2 * i + 2) * count] for i in range(spread)], axis=0)
    keep_ref[...] = jnp.where(is_first, even, odd)
    send_ref[...] = jnp.where(is_first, odd, even).astype(BF)


def far(pairs, group, part, spread, ids, q, near_sums, gains, halves, arrived, final):
    rows = q.shape[0]
    shapes = [jax.ShapeDtypeStruct((rows, LANES), BF)]
    if final:
        shape = (final[0].shape[1] // 2, len(final) * LANES)
        shapes += [jax.ShapeDtypeStruct(shape, F32), jax.ShapeDtypeStruct(shape, BF)]
    return pl.pallas_call(
        functools.partial(far_kernel, pairs, group, part, 256, spread, len(arrived), bool(final)),
        in_specs=[smem()]
        + [vmem()] * (3 + len(halves))
        + [pl.BlockSpec(memory_space=pl.ANY)] * len(arrived)
        + [vmem()] * len(final),
        out_specs=[vmem()] * len(shapes) + [smem()],
        out_shape=shapes + [TURN],
        compiler_params=pltpu.CompilerParams(vmem_limit_bytes=VMEM_LIMIT),
        cost_estimate=COST,
        name="far",
    )(ids, q, near_sums, gains, *halves, *arrived, *final)


def out_kernel(count, pairs, spans, *refs):
    ids_ref, refs = refs[0], refs[1:]
    tokens, refs = [refs[j * pairs : (j + 1) * pairs] for j in range(count)], refs[count * pairs :]
    pooled, refs = refs[:spans], refs[spans:]
    *refs, turn_ref = refs
    turn_ref[0] = ids_ref[0]
    outs = refs[-2:] if spans else refs[-1:]
    weight_ref, *acc = refs[: -len(outs)]
    rows, width = tokens[0][0].shape[0], pairs * LANES
    tile = min(256, rows)

    def weight(j, size):
        return weight_ref[pl.ds(pl.multiple_of(ids_ref[j] * size, size), size), :]

    def head_weight(j):
        if pairs == 1:
            return weight(j, width)
        first = ids_ref[count + spans]
        blocks = [weight_ref[pl.ds(pl.multiple_of(ids_ref[j] * width + p * LANES, LANES), LANES), :] for p in (first, 1 - first)]
        return jnp.concatenate(blocks, axis=0)

    weights = [head_weight(j) for j in range(count)]

    for start in range(0, rows, tile):
        at = slice(start, start + tile)
        total = acc[0][at, :] if acc else None
        for j in range(count):
            term = dot(jnp.concatenate([ref[at, :] for ref in tokens[j]], axis=1), weights[j])
            total = term if total is None else total + term
        outs[0][at, :] = total.astype(outs[0].dtype)
    if spans:
        outs[1][...] = sum(dot(ref[...], weight(count + k, ref.shape[1])) for k, ref in enumerate(pooled))


def out_part(parts, index, weight, acc, dtype, pooled=()):
    count = len(parts)
    pairs = len(parts[0])
    rows = parts[0][0].shape[0]
    columns = weight.shape[1]
    extra = [] if acc is None else [acc]
    shapes = [jax.ShapeDtypeStruct((rows, columns), dtype)]
    shapes += [jax.ShapeDtypeStruct((pooled[0].shape[0], columns), F32)] if pooled else []
    return pl.pallas_call(
        functools.partial(out_kernel, count, pairs, len(pooled)),
        in_specs=[smem()] + [vmem()] * (count * pairs + len(pooled) + 1 + len(extra)),
        out_specs=[vmem()] * len(shapes) + [smem()],
        out_shape=shapes + [jax.ShapeDtypeStruct((1,), jnp.int32)],
        compiler_params=pltpu.CompilerParams(vmem_limit_bytes=VMEM_LIMIT),
        cost_estimate=COST,
        name="out",
    )(index, *[piece for part in parts for piece in part], *pooled, weight, *extra)


def pieces_kernel(ids_ref, keep_ref, got_ref, *out_refs):
    spread = len(out_refs)
    count = keep_ref.shape[0] // spread
    for k, ref in enumerate(out_refs):
        at = pl.ds(pl.multiple_of(lax.rem(ids_ref[0] + k, spread) * count, count), count)
        ref[...] = (keep_ref[at, :] + got_ref[at, :].astype(F32)).astype(ref.dtype)


def pool_pieces(place, keep, got, spread):
    count = keep.shape[0] // spread
    shape = (count, keep.shape[1])
    return pl.pallas_call(
        pieces_kernel,
        in_specs=[smem(), vmem(), vmem()],
        out_specs=[vmem()] * spread,
        out_shape=[jax.ShapeDtypeStruct(shape, F32)] + [jax.ShapeDtypeStruct(shape, BF)] * (spread - 1),
        compiler_params=pltpu.CompilerParams(vmem_limit_bytes=VMEM_LIMIT),
        cost_estimate=COST,
        name="pool_pieces",
    )(place, keep, got)


def own_kernel(ids_ref, bounds_ref, own_ref, *refs):
    total = own_ref[...]
    for ref in refs[:-1]:
        total = total + ref[...].astype(F32)
    count = total.shape[0]
    rows = [
        total[i : i + 1] / (bounds_ref[1, ids_ref[0] + i] - bounds_ref[0, ids_ref[0] + i]).astype(F32)
        for i in range(count)
    ]
    refs[-1][...] = jnp.concatenate(rows, axis=0).astype(BF)


def pool_own(place, bounds, own, others):
    return pl.pallas_call(
        own_kernel,
        in_specs=[smem(), smem()] + [vmem()] * (1 + len(others)),
        out_specs=vmem(),
        out_shape=jax.ShapeDtypeStruct(own.shape, BF),
        compiler_params=pltpu.CompilerParams(vmem_limit_bytes=VMEM_LIMIT),
        cost_estimate=COST,
        name="pool_own",
    )(place, bounds, own, *others)


def swap(values, axis, step):
    count = lax.axis_size(axis)
    return lax.ppermute(values, axis, [(i, i ^ step) for i in range(count)])


def across_heads(values, step):
    count = lax.axis_size("head")
    return lax.ppermute(values, "head", [(i, (i + step) % count) for i in range(count)])


def add_kernel(a_ref, b_ref, out_ref):
    count = a_ref.shape[0]
    out_ref[...] = (a_ref[...].astype(F32) + b_ref[:count, :].astype(F32)).astype(BF)


def add_call(a, b, cost=COST):
    return pl.pallas_call(
        add_kernel,
        in_specs=[vmem()] * 2,
        out_specs=vmem(),
        out_shape=jax.ShapeDtypeStruct(a.shape, BF),
        compiler_params=pltpu.CompilerParams(vmem_limit_bytes=VMEM_LIMIT),
        cost_estimate=cost,
        name="add",
    )(a, b)


def steps_of(axis):
    step = 1
    while step < lax.axis_size(axis):
        yield step
        step *= 2


def per_device(
    book_tokens,
    norm_gain,
    query_weight,
    key_weight,
    value_weight,
    proj_weight,
    dual_gains,
    out_weight,
    span_bounds,
):
    rows = book_tokens.shape[0]
    seq_devices = lax.axis_size(("seq", "rep"))
    seq_index = lax.axis_index(("seq", "rep"))
    head_devices = lax.axis_size("head")
    head_index = lax.axis_index("head")
    first_row = seq_index * rows
    all_pairs = query_weight.shape[1] // LANES
    groups = 2 if all_pairs == 4 else all_pairs
    pairs = all_pairs // groups
    ids = jnp.stack(
        [lax.axis_index("rep"), (seq_index > 0).astype(jnp.int32), (seq_index < seq_devices - 1).astype(jnp.int32), first_row]
    ).astype(jnp.int32)
    gain = norm_gain[None, :]
    bounds = span_bounds.T

    both = ("seq", "rep")
    chips = [(i, i + 1) for i in range(1, seq_devices - 1, 2)]
    chips = chips + [(b, a) for a, b in chips]
    steps = list(steps_of("seq"))
    tie = lax.optimization_barrier

    fronts, mine, normed = [], [], book_tokens
    turn = ids
    fetched = []
    for g in range(groups):
        last = g == groups - 1
        normed, *outs = front(g == 0, last, g, pairs, turn, normed, gain, key_weight, value_weight, proj_weight,
                              dual_gains, [f[3] for f in fronts], fetched)
        outs, turn, fetched = outs[:4], outs[4], outs[5:]
        fronts.append(outs)
        send, edge = outs[2], outs[3]
        if last:
            for f in range(g):
                for step in steps[:-1]:
                    got, turn = tie((swap(mine[f], "seq", step), turn))
                    mine[f] = add_call(mine[f], got, LONG)
                mine[f], turn = tie((mine[f], turn))
        core = swap(send, "rep", 1)
        if last:
            chip = lax.ppermute(edge, both, chips)
        mine.append(add_call(outs[1], core))
        mine[g], turn = tie((mine[g], turn))

    if groups == 1:
        for step in steps[:-1]:
            mine[0] = add_call(mine[0], swap(mine[0], "seq", step))

    spread = lax.axis_size("seq")
    outs, arrived, others, other_index, queries = [], [], [], [], []
    for g in range(groups):
        source = queries[g] if g else normed
        *made, near_sums, turn = near(pairs, g, groups, turn, source, query_weight, core, chip, fronts[g][0])
        queries = queries if g else made
        q = made[0]
        got, turn = tie((swap(mine[g], "seq", steps[-1]), turn))
        total = add_call(mine[g], got)
        out = []
        for part in ("own", "other") if pairs == 2 else ("all",):
            halves, final = [total], []
            if part != "own":
                if part == "other" and g < groups - 1:
                    total, turn = tie((total, turn))
                other = swap(total, "rep", 1)
                halves = [other] if part == "other" else [total, other]
                if g == groups - 2:
                    for step in steps[:-1]:
                        got, turn = tie((swap(mine[-1], "seq", step), turn))
                        mine[-1] = add_call(mine[-1], got)
                    mine[-1], turn = tie((mine[-1], turn))
                if g == groups - 1:
                    final = [bounds] + [piece for o in outs for piece in o] + out
            made, *sums, turn = far(pairs, g, part, spread, turn, q, near_sums, dual_gains, halves, arrived, final)
            arrived = []
            out.append(made)
        outs.append(out)
        moved = [[across_heads(piece, k) for piece in out] for k in range(1, head_devices)]
        arrived = [moved[0][0]] if g < groups - 1 and moved else []
        others += moved
        other_index += [lax.rem(head_index - k + head_devices, head_devices) * groups + g for k in range(1, head_devices)]

    own_index = [head_index * groups + g for g in range(groups)]
    early = len(others) - (head_devices - 1)

    keep, send = sums
    place = lax.axis_index("seq").astype(jnp.int32)[None]
    own, *pieces = pool_pieces(place, keep, swap(send, "rep", 1), spread)
    pieces = [
        lax.ppermute(piece, "seq", [(i, (i + k + 1) % spread) for i in range(spread)]) for k, piece in enumerate(pieces)
    ]
    parts = outs + others[:early]
    index = jnp.stack(own_index + other_index[:early] + [lax.axis_index("rep")]).astype(jnp.int32)
    acc, turn = out_part(parts, index, out_weight, None, F32)
    place = (seq_index * own.shape[0]).astype(jnp.int32)[None]
    place = place + (turn - index[:1])
    own = pool_own(place, bounds, own, pieces)
    pooled = [own] + [across_heads(own, k) for k in range(1, head_devices)]
    pooled_index = [lax.rem(head_index - k + head_devices, head_devices) for k in range(head_devices)]
    index = jnp.stack(other_index[early:] + pooled_index + [lax.axis_index("rep")]).astype(jnp.int32)
    return tuple(out_part(others[early:], index, out_weight, acc, BF, pooled)[:2])


def solution(mesh):
    placed = (
        P(("groups", "seq", "rep"), None),
        P(),
        P(None, "head"),
        P(None, "head"),
        P(None, "head"),
        P(None, "head"),
        P(None, "head"),
        P(None, "head"),
        P("groups", None),
    )
    return jax.shard_map(
        per_device,
        mesh=mesh,
        in_specs=placed,
        out_specs=(P(("groups", "seq", "rep"), "head"), P(("groups", "seq", "rep"), "head")),
        check_vma=False,
    )
```

```python
import functools

import jax
import jax.numpy as jnp
from jax import lax
from jax.experimental import pallas as pl
from jax.experimental.pallas import tpu as pltpu
from jax.sharding import PartitionSpec as P

DH = 64
R = 256
SEG = 128
HALF = SEG // 2
LANES = 2 * DH
SCORE_SCALE = DH ** (-0.5)
LOG2E = 1.4426950408889634

VMEM_LIMIT = 40 << 20
COST = pl.CostEstimate(flops=1 << 20, bytes_accessed=1 << 10, transcendentals=0)

LONG = pl.CostEstimate(flops=1 << 33, bytes_accessed=1 << 10, transcendentals=0)
TURN = jax.ShapeDtypeStruct((4,), jnp.int32)

softcap = 5.0
epsilon = 1e-05

BF = jnp.bfloat16
F32 = jnp.float32


def dot(a, b, dims=((1,), (0,))):
    return lax.dot_general(a, b, (dims, ((), ())), preferred_element_type=F32)


def exp_capped(values, scale):
    return jnp.exp2((softcap * LOG2E) * jnp.tanh(values * (scale / softcap)))


def pass_turn(ids_ref, turn_ref):
    for i in range(4):
        turn_ref[i] = ids_ref[i]


def vmem():
    return pl.BlockSpec(memory_space=pltpu.VMEM)


def smem():
    return pl.BlockSpec(memory_space=pltpu.SMEM)


def head_norm(values, gain):
    out = []
    for at in range(0, values.shape[1], LANES):
        x = values[:, at : at + LANES]
        first = lane_is_first(x.shape)

        def mean(y):
            low = jnp.sum(jnp.where(first, y, 0.0), axis=-1, keepdims=True)
            high = jnp.sum(jnp.where(first, 0.0, y), axis=-1, keepdims=True)
            return jnp.where(first, low, high) * (1.0 / DH)

        centred = x - mean(x)
        spread = mean(centred * centred)
        out.append((centred * lax.rsqrt(spread + epsilon) * gain[:, at : at + LANES]).astype(BF))
    return jnp.concatenate(out, axis=1)


def token_norm(x, gain):
    x = x.astype(F32)
    centred = x - jnp.mean(x, axis=-1, keepdims=True)
    spread = jnp.mean(centred * centred, axis=-1, keepdims=True)
    return (centred * lax.rsqrt(spread + epsilon) * gain).astype(BF)


def edge_rows(near_ref):
    rows = near_ref.shape[0]
    columns = [slice(at, at + 2 * LANES) for at in range(0, near_ref.shape[1], 2 * LANES)]
    return [jnp.concatenate([near_ref[at, c] for c in columns], axis=0) for at in (slice(0, HALF), slice(rows - HALF, rows))]


def front_kernel(first, last, group, pairs, tile, *refs):
    ids_ref, refs = refs[0], list(refs[1:])
    if first:
        x_hbm, gain_hbm, dual_hbm, wk_hbm, wv_hbm, wp_hbm = refs[:6]
        refs = refs[6:]
    else:
        given_ref, dual_ref, kv_ref, wp_ref = refs[:4]
        refs = refs[4:]
        if not last:
            wk_hbm, wv_hbm, wp_hbm = refs[:3]
            refs = refs[3:]
    earlier = [refs.pop(0) for _ in range(group)] if last else []
    normed_ref, near_ref, keep_ref, send_ref, edge_ref, turn_ref = refs[:6]
    refs = refs[6:]
    pass_turn(ids_ref, turn_ref)
    if not last:
        next_kv_ref, next_wp_ref = refs[:2]
        refs = refs[2:]
    raw_ref, p_ref, sem = refs[:3]
    if first:
        kv_ref, wp_ref, x_ref, gain_ref, dual_ref = refs[3:]
    rows = normed_ref.shape[0]
    width = pairs * LANES
    chunks = rows // tile
    used = 0

    def copy(source, target):
        nonlocal used
        made = pltpu.make_async_copy(source, target, sem.at[used])
        used += 1
        made.start()
        return made

    def weight_copies(g, kv, wp):
        own = pl.ds(g * width, width)
        heads = [
            copy(wk_hbm.at[:, own], kv.at[:, pl.ds(0, width)]),
            copy(wv_hbm.at[:, own], kv.at[:, pl.ds(width, width)]),
        ]
        return heads, [copy(wp_hbm.at[:, pl.ds(g * pairs * 2 * R, pairs * 2 * R)], wp)]

    def token_copy(i):
        at = pl.ds(i * tile, tile)
        return copy(x_hbm.at[at, :], x_ref.at[at, :])

    kv_copies, proj_copies, next_copies = [], [], []
    if first:
        token_copies = [token_copy(0)]
        small_copies = [copy(gain_hbm, gain_ref), copy(dual_hbm, dual_ref)]
        kv_copies, proj_copies = weight_copies(group, kv_ref, wp_ref)
        token_copies += [token_copy(i) for i in range(1, chunks)]
    for i in range(chunks):
        at = pl.ds(i * tile, tile)
        if first:
            token_copies[i].wait()
            if i == 0:
                for made in small_copies:
                    made.wait()
            normed_ref[at, :] = token_norm(x_ref[at, :], gain_ref[...])
        normed = normed_ref[at, :]
        if i == 0:
            for made in kv_copies:
                made.wait()
        both = dot(normed, kv_ref[...])
        key, value = both[:, :width], both[:, width:]
        for p in range(pairs):
            cols = slice(p * LANES, (p + 1) * LANES)
            raw = jnp.concatenate([key[:, cols], value[:, cols]], axis=1).astype(BF)
            raw_ref[2 * p * LANES : 2 * (p + 1) * LANES, at] = raw.T
        if i == 0:
            for made in proj_copies:
                made.wait()
        if i == 0 and not last:
            next_copies = sum(weight_copies(group + 1, next_kv_ref, next_wp_ref), [])
        p_ref[at, :] = exp_capped(dot(normed, wp_ref[...]), 1.0).astype(BF)
        near_ref[at, :width] = head_norm(key, dual_ref[0:1, group * width : (group + 1) * width])
        near_ref[at, width:] = head_norm(value, dual_ref[1:2, group * width : (group + 1) * width])
    total = []
    for p in range(pairs):
        full = dot(raw_ref[2 * p * LANES : 2 * (p + 1) * LANES, :], p_ref[:, 2 * p * R : 2 * (p + 1) * R])
        for part in range(4):
            head = part % 2
            total.append(full[part * DH : (part + 1) * DH, head * R : (head + 1) * R])
    for made in next_copies:
        made.wait()
    total = jnp.concatenate(total, axis=0).astype(BF)
    half = total.shape[0] // 2
    mine = ids_ref[0] == 0
    keep_ref[...] = jnp.where(mine, total[:half], total[half:])
    send_ref[:half, :] = jnp.where(mine, total[half:], total[:half])
    head, tail = edge_rows(near_ref)
    edge = head.shape[0]
    if last:
        for i, ref in enumerate(earlier):
            before = jnp.where(mine, ref[edge:, :], ref[:edge, :])
            send_ref[half + i * edge : half + (i + 1) * edge, :] = before
            edge_ref[i * edge : (i + 1) * edge, :] = jnp.where(mine, ref[:edge, :], ref[edge:, :])
        send_ref[half + group * edge :, :] = jnp.where(mine, tail, head)
        edge_ref[group * edge :, :] = jnp.where(mine, head, tail)
    else:
        edge_ref[:edge, :] = head
        edge_ref[edge:, :] = tail


def in_hbm(values):
    return pltpu.with_memory_space_constraint(values, pltpu.HBM)


def front(first, last, group, pairs, ids, tokens, gain, wk, wv, wp, dual, earlier, fetched):
    rows, depth = tokens.shape
    width = pairs * LANES
    half = pairs * R // 2
    tile = min(512 if first else 256, rows)
    edge = (group + 1) * pairs * HALF if last else 0
    outs = [
        jax.ShapeDtypeStruct((rows, depth), BF),
        jax.ShapeDtypeStruct((rows, 2 * width), BF),
        jax.ShapeDtypeStruct((half, R), BF),
        jax.ShapeDtypeStruct((half + edge, R), BF),
        jax.ShapeDtypeStruct((edge if last else 2 * pairs * HALF, R), BF),
        TURN,
    ]
    if not last:
        outs += [jax.ShapeDtypeStruct((depth, 2 * width), BF), jax.ShapeDtypeStruct((depth, 2 * pairs * R), BF)]
    hbm = pl.BlockSpec(memory_space=pltpu.HBM)
    earlier = earlier if last else []
    weights = [in_hbm(wk), in_hbm(wv), in_hbm(wp)]
    if first:
        ins = [hbm] * 6
        args = [in_hbm(tokens), in_hbm(gain), in_hbm(dual)] + weights
    else:
        ins = [vmem()] * 4 + ([] if last else [hbm] * 3)
        args = [tokens, dual, *fetched] + ([] if last else weights)
    ins = [smem()] + ins + [vmem()] * len(earlier)
    args = [ids] + args + earlier
    scratch = [
        pltpu.VMEM((2 * width, rows), BF),
        pltpu.VMEM((rows, 2 * pairs * R), BF),
        pltpu.SemaphoreType.DMA((rows // tile + 8,)),
    ]
    if first:
        scratch += [
            pltpu.VMEM((depth, 2 * width), BF),
            pltpu.VMEM((depth, 2 * pairs * R), BF),
            pltpu.VMEM((rows, depth), BF),
            pltpu.VMEM((1, depth), F32),
            pltpu.VMEM(dual.shape, F32),
        ]
    is_turn = [o is TURN for o in outs]
    return pl.pallas_call(
        functools.partial(front_kernel, first, last, group, pairs, tile),
        input_output_aliases={} if first else {1: 0},
        in_specs=ins,
        out_specs=[smem() if t else vmem() for t in is_turn],
        out_shape=outs,
        scratch_shapes=scratch,
        compiler_params=pltpu.CompilerParams(vmem_limit_bytes=VMEM_LIMIT),
        cost_estimate=pl.CostEstimate(
            flops=2 * rows * depth * (2 * width + 2 * pairs * R), bytes_accessed=4 << 20, transcendentals=0
        ),
        name="front",
    )(*args)


def lane_is_first(shape):
    return lax.broadcasted_iota(jnp.int32, shape, 1) < DH


def stacked(q):
    first = lane_is_first(q.shape)
    zero = jnp.zeros_like(q)
    return jnp.concatenate([jnp.where(first, q, zero), jnp.where(first, zero, q)], axis=0)


def unstack(both):
    rows = both.shape[0] // 2
    first = lane_is_first((rows, LANES))
    return (
        jnp.where(first, both[:rows, :LANES], both[rows:, :LANES]),
        jnp.where(first, both[:rows, LANES:], both[rows:, LANES:]),
    )


def near_kernel(pairs, group, groups, ids_ref, *refs):
    width = pairs * LANES
    if group == 0:
        normed_ref, wq_ref, core_ref, chip_ref, near_ref = refs[:5]
        q_refs, (out_ref, turn_ref, pad_ref) = refs[5:-3], refs[-3:]
        q_ref, rows = q_refs[0], normed_ref.shape[0]
        for start in range(0, rows, 256):
            at = slice(start, start + 256)
            q = dot(normed_ref[at, :], wq_ref[...])
            for g in range(groups):
                q_refs[g][at, :] = q[:, g * width : (g + 1) * width].astype(BF)
    else:
        given_ref, core_ref, chip_ref, near_ref, q_ref, out_ref, turn_ref, pad_ref = refs
        rows = q_ref.shape[0]
    is_first = ids_ref[0] == 0
    row = lax.broadcasted_iota(jnp.int32, (2 * SEG, LANES), 0)
    ones = jnp.ones((2 * SEG, LANES), F32)
    has_prev = jnp.where(ids_ref[1] != 0, 1.0, 0.0)
    has_next = jnp.where(ids_ref[2] != 0, 1.0, 0.0)
    segments = rows // SEG
    offset = core_ref.shape[0] - chip_ref.shape[0]
    pad_ref[HALF : HALF + rows, :] = near_ref[...]
    for c in range(pairs):
        at = (group * pairs + c) * HALF
        core = core_ref[offset + at : offset + at + HALF, :]
        chip = chip_ref[at : at + HALF, :]
        lanes = slice(2 * c * LANES, 2 * (c + 1) * LANES)
        pad_ref[0:HALF, lanes] = jnp.where(is_first, chip, core)
        pad_ref[HALF + rows :, lanes] = jnp.where(is_first, core, chip)
    for s in range(segments):
        count = ones
        if s == 0:
            count = jnp.where(row < HALF, has_prev, count)
        if s == segments - 1:
            count = jnp.where(row >= 3 * HALF, has_next, count)
        count = count.astype(BF)
        window = pl.ds(s * SEG, 2 * SEG)
        here = slice(s * SEG, (s + 1) * SEG)
        for p in range(pairs):
            cols = slice(p * LANES, (p + 1) * LANES)
            scores = dot(stacked(q_ref[here, cols]), pad_ref[window, cols], ((1,), (1,)))
            weights = exp_capped(scores, SCORE_SCALE).astype(BF)
            values = jnp.concatenate([pad_ref[window, width + p * LANES : width + (p + 1) * LANES], count], axis=1)
            top, bottom = unstack(dot(weights, values))
            out_ref[here, 2 * p * LANES : (2 * p + 1) * LANES] = top
            out_ref[here, (2 * p + 1) * LANES : (2 * p + 2) * LANES] = bottom
    pass_turn(ids_ref, turn_ref)


def near(pairs, group, groups, ids, source, wq, core, chip, near_pairs):
    rows = near_pairs.shape[0]
    width = pairs * LANES
    q = jax.ShapeDtypeStruct((rows, width), BF)
    count = groups if group == 0 else 1
    args = [source, wq] if group == 0 else [source]
    return pl.pallas_call(
        functools.partial(near_kernel, pairs, group, groups),
        in_specs=[smem()] + [vmem()] * (len(args) + 3),
        out_specs=[vmem()] * (count + 1) + [smem()],
        out_shape=[q] * count + [jax.ShapeDtypeStruct((rows, 2 * width), F32), TURN],
        input_output_aliases={} if group == 0 else {1: 0},
        scratch_shapes=[pltpu.VMEM((rows + SEG, 2 * width), BF)],
        compiler_params=pltpu.CompilerParams(vmem_limit_bytes=VMEM_LIMIT),
        cost_estimate=COST,
        name="near",
    )(ids, *args, core, chip, near_pairs)


def far_kernel(pairs, group, part, block, spread, waits, final, *refs):
    ids_ref, q_ref, near_ref, gains_ref = refs[:4]
    refs = refs[4:]
    is_first = ids_ref[0] == 0
    if part == "all":
        mine, other = refs[0][...], refs[1][...]
        total = jnp.concatenate([jnp.where(is_first, mine, other), jnp.where(is_first, other, mine)], axis=0)
        p, refs = 0, refs[2:]
    else:
        total = refs[0][...]
        p, refs = ids_ref[0] if part == "own" else 1 - ids_ref[0], refs[1:]
    refs = refs[waits:]
    if final:
        bounds_ref, *earlier = refs[:-4]
        out_ref, keep_ref, send_ref, turn_ref = refs[-4:]
    else:
        out_ref, turn_ref = refs
    pass_turn(ids_ref, turn_ref)
    rows = q_ref.shape[0]

    def lanes(offset, scale=1):
        start = (offset + p) * scale * LANES
        return pl.ds(start if part == "all" else pl.multiple_of(start, LANES), scale * LANES)

    gains = jnp.concatenate([gains_ref[:, lanes(group * pairs)]] * 2, axis=0).T

    def land(kind):
        parts = []
        for h in range(2):
            at = kind * LANES + h * DH
            values = total[at : at + DH].astype(F32)
            centred = values - jnp.mean(values, axis=0, keepdims=True)
            spread = jnp.mean(centred * centred, axis=0, keepdims=True)
            gain = gains[h * DH : (h + 1) * DH, 2 + kind : 3 + kind]
            parts.append((centred * lax.rsqrt(spread + epsilon) * gain).astype(BF))
        return jnp.concatenate(parts, axis=0)

    keys = land(0)
    values = jnp.concatenate([land(1), jnp.ones((LANES, R), BF)], axis=0)
    for start in range(0, rows, block):
        at = slice(start, start + block)
        weights = exp_capped(dot(stacked(q_ref[at, lanes(0)]), keys), SCORE_SCALE).astype(BF)
        top, bottom = unstack(dot(weights, values, ((1,), (1,))))
        near_sums = near_ref[at, lanes(0, 2)]
        out_ref[at, :] = ((top + near_sums[:, :LANES]) / (bottom + near_sums[:, LANES:])).astype(BF)
    if not final:
        return
    spans = bounds_ref.shape[1]
    position = ids_ref[3] + lax.broadcasted_iota(jnp.int32, (rows, spans), 0)
    member = (position >= bounds_ref[0:1, :]) & (position < bounds_ref[1:2, :])
    pieces = jnp.concatenate([ref[...] for ref in earlier + [out_ref]], axis=1)
    sums = dot(jnp.where(member, 1.0, 0.0).astype(BF), pieces, ((0,), (0,)))
    if part != "all":
        ordered = []
        for at in range(0, sums.shape[1], 2 * LANES):
            low, high = sums[:, at : at + LANES], sums[:, at + LANES : at + 2 * LANES]
            ordered += [jnp.where(is_first, low, high), jnp.where(is_first, high, low)]
        sums = jnp.concatenate(ordered, axis=1)
    count = spans // (2 * spread)
    even = jnp.concatenate([sums[2 * i * count : (2 * i + 1) * count] for i in range(spread)], axis=0)
    odd = jnp.concatenate([sums[(2 * i + 1) * count : (2 * i + 2) * count] for i in range(spread)], axis=0)
    keep_ref[...] = jnp.where(is_first, even, odd)
    send_ref[...] = jnp.where(is_first, odd, even).astype(BF)


def far(pairs, group, part, spread, ids, q, near_sums, gains, halves, arrived, final):
    rows = q.shape[0]
    shapes = [jax.ShapeDtypeStruct((rows, LANES), BF)]
    if final:
        shape = (final[0].shape[1] // 2, len(final) * LANES)
        shapes += [jax.ShapeDtypeStruct(shape, F32), jax.ShapeDtypeStruct(shape, BF)]
    return pl.pallas_call(
        functools.partial(far_kernel, pairs, group, part, 256, spread, len(arrived), bool(final)),
        in_specs=[smem()]
        + [vmem()] * (3 + len(halves))
        + [pl.BlockSpec(memory_space=pl.ANY)] * len(arrived)
        + [vmem()] * len(final),
        out_specs=[vmem()] * len(shapes) + [smem()],
        out_shape=shapes + [TURN],
        compiler_params=pltpu.CompilerParams(vmem_limit_bytes=VMEM_LIMIT),
        cost_estimate=COST,
        name="far",
    )(ids, q, near_sums, gains, *halves, *arrived, *final)


def out_kernel(count, pairs, spans, *refs):
    ids_ref, refs = refs[0], refs[1:]
    tokens, refs = [refs[j * pairs : (j + 1) * pairs] for j in range(count)], refs[count * pairs :]
    pooled, refs = refs[:spans], refs[spans:]
    *refs, turn_ref = refs
    turn_ref[0] = ids_ref[0]
    outs = refs[-2:] if spans else refs[-1:]
    weight_ref, *acc = refs[: -len(outs)]
    rows, width = tokens[0][0].shape[0], pairs * LANES
    tile = min(256, rows)

    def weight(j, size):
        return weight_ref[pl.ds(pl.multiple_of(ids_ref[j] * size, size), size), :]

    def head_weight(j):
        if pairs == 1:
            return weight(j, width)
        first = ids_ref[count + spans]
        blocks = [weight_ref[pl.ds(pl.multiple_of(ids_ref[j] * width + p * LANES, LANES), LANES), :] for p in (first, 1 - first)]
        return jnp.concatenate(blocks, axis=0)

    weights = [head_weight(j) for j in range(count)]

    for start in range(0, rows, tile):
        at = slice(start, start + tile)
        total = acc[0][at, :] if acc else None
        for j in range(count):
            term = dot(jnp.concatenate([ref[at, :] for ref in tokens[j]], axis=1), weights[j])
            total = term if total is None else total + term
        outs[0][at, :] = total.astype(outs[0].dtype)
    if spans:
        outs[1][...] = sum(dot(ref[...], weight(count + k, ref.shape[1])) for k, ref in enumerate(pooled))


def out_part(parts, index, weight, acc, dtype, pooled=()):
    count = len(parts)
    pairs = len(parts[0])
    rows = parts[0][0].shape[0]
    columns = weight.shape[1]
    extra = [] if acc is None else [acc]
    shapes = [jax.ShapeDtypeStruct((rows, columns), dtype)]
    shapes += [jax.ShapeDtypeStruct((pooled[0].shape[0], columns), F32)] if pooled else []
    return pl.pallas_call(
        functools.partial(out_kernel, count, pairs, len(pooled)),
        in_specs=[smem()] + [vmem()] * (count * pairs + len(pooled) + 1 + len(extra)),
        out_specs=[vmem()] * len(shapes) + [smem()],
        out_shape=shapes + [jax.ShapeDtypeStruct((1,), jnp.int32)],
        compiler_params=pltpu.CompilerParams(vmem_limit_bytes=VMEM_LIMIT),
        cost_estimate=COST,
        name="out",
    )(index, *[piece for part in parts for piece in part], *pooled, weight, *extra)


def pieces_kernel(ids_ref, keep_ref, got_ref, *out_refs):
    spread = len(out_refs)
    count = keep_ref.shape[0] // spread
    for k, ref in enumerate(out_refs):
        at = pl.ds(pl.multiple_of(lax.rem(ids_ref[0] + k, spread) * count, count), count)
        ref[...] = (keep_ref[at, :] + got_ref[at, :].astype(F32)).astype(ref.dtype)


def pool_pieces(place, keep, got, spread):
    count = keep.shape[0] // spread
    shape = (count, keep.shape[1])
    return pl.pallas_call(
        pieces_kernel,
        in_specs=[smem(), vmem(), vmem()],
        out_specs=[vmem()] * spread,
        out_shape=[jax.ShapeDtypeStruct(shape, F32)] + [jax.ShapeDtypeStruct(shape, BF)] * (spread - 1),
        compiler_params=pltpu.CompilerParams(vmem_limit_bytes=VMEM_LIMIT),
        cost_estimate=COST,
        name="pool_pieces",
    )(place, keep, got)


def own_kernel(ids_ref, bounds_ref, own_ref, *refs):
    total = own_ref[...]
    for ref in refs[:-1]:
        total = total + ref[...].astype(F32)
    count = total.shape[0]
    rows = [
        total[i : i + 1] / (bounds_ref[1, ids_ref[0] + i] - bounds_ref[0, ids_ref[0] + i]).astype(F32)
        for i in range(count)
    ]
    refs[-1][...] = jnp.concatenate(rows, axis=0).astype(BF)


def pool_own(place, bounds, own, others):
    return pl.pallas_call(
        own_kernel,
        in_specs=[smem(), smem()] + [vmem()] * (1 + len(others)),
        out_specs=vmem(),
        out_shape=jax.ShapeDtypeStruct(own.shape, BF),
        compiler_params=pltpu.CompilerParams(vmem_limit_bytes=VMEM_LIMIT),
        cost_estimate=COST,
        name="pool_own",
    )(place, bounds, own, *others)


def swap(values, axis, step):
    count = lax.axis_size(axis)
    return lax.ppermute(values, axis, [(i, i ^ step) for i in range(count)])


def across_heads(values, step):
    count = lax.axis_size("head")
    return lax.ppermute(values, "head", [(i, (i + step) % count) for i in range(count)])


def add_kernel(a_ref, b_ref, out_ref):
    count = a_ref.shape[0]
    out_ref[...] = (a_ref[...].astype(F32) + b_ref[:count, :].astype(F32)).astype(BF)


def add_call(a, b, cost=COST):
    return pl.pallas_call(
        add_kernel,
        in_specs=[vmem()] * 2,
        out_specs=vmem(),
        out_shape=jax.ShapeDtypeStruct(a.shape, BF),
        compiler_params=pltpu.CompilerParams(vmem_limit_bytes=VMEM_LIMIT),
        cost_estimate=cost,
        name="add",
    )(a, b)


def steps_of(axis):
    step = 1
    while step < lax.axis_size(axis):
        yield step
        step *= 2


def per_device(
    book_tokens,
    norm_gain,
    query_weight,
    key_weight,
    value_weight,
    proj_weight,
    dual_gains,
    out_weight,
    span_bounds,
):
    rows = book_tokens.shape[0]
    seq_devices = lax.axis_size(("seq", "rep"))
    seq_index = lax.axis_index(("seq", "rep"))
    head_devices = lax.axis_size("head")
    head_index = lax.axis_index("head")
    first_row = seq_index * rows
    all_pairs = query_weight.shape[1] // LANES
    groups = 2 if all_pairs == 4 else all_pairs
    pairs = all_pairs // groups
    ids = jnp.stack(
        [lax.axis_index("rep"), (seq_index > 0).astype(jnp.int32), (seq_index < seq_devices - 1).astype(jnp.int32), first_row]
    ).astype(jnp.int32)
    gain = norm_gain[None, :]
    bounds = span_bounds.T

    both = ("seq", "rep")
    chips = [(i, i + 1) for i in range(1, seq_devices - 1, 2)]
    chips = chips + [(b, a) for a, b in chips]
    steps = list(steps_of("seq"))
    tie = lax.optimization_barrier

    fronts, mine, normed = [], [], book_tokens
    turn = ids
    fetched = []
    for g in range(groups):
        last = g == groups - 1
        normed, *outs = front(g == 0, last, g, pairs, turn, normed, gain, key_weight, value_weight, proj_weight,
                              dual_gains, [f[3] for f in fronts], fetched)
        outs, turn, fetched = outs[:4], outs[4], outs[5:]
        fronts.append(outs)
        send, edge = outs[2], outs[3]
        if last:
            for f in range(g):
                for step in steps[:-1]:
                    got, turn = tie((swap(mine[f], "seq", step), turn))
                    mine[f] = add_call(mine[f], got, LONG)
                mine[f], turn = tie((mine[f], turn))
        core = swap(send, "rep", 1)
        if last:
            chip = lax.ppermute(edge, both, chips)
        mine.append(add_call(outs[1], core))
        mine[g], turn = tie((mine[g], turn))

    if groups == 1:
        for step in steps[:-1]:
            mine[0] = add_call(mine[0], swap(mine[0], "seq", step))

    spread = lax.axis_size("seq")
    outs, arrived, others, other_index, queries = [], [], [], [], []
    for g in range(groups):
        source = queries[g] if g else normed
        *made, near_sums, turn = near(pairs, g, groups, turn, source, query_weight, core, chip, fronts[g][0])
        queries = queries if g else made
        q = made[0]
        got, turn = tie((swap(mine[g], "seq", steps[-1]), turn))
        total = add_call(mine[g], got)
        out = []
        for part in ("own", "other") if pairs == 2 else ("all",):
            halves, final = [total], []
            if part != "own":
                if part == "other":
                    total, turn = tie((total, turn))
                other = swap(total, "rep", 1)
                halves = [other] if part == "other" else [total, other]
                if g == groups - 2:
                    for step in steps[:-1]:
                        got, turn = tie((swap(mine[-1], "seq", step), turn))
                        mine[-1] = add_call(mine[-1], got)
                    mine[-1], turn = tie((mine[-1], turn))
                if g == groups - 1:
                    final = [bounds] + [piece for o in outs for piece in o] + out
            made, *sums, turn = far(pairs, g, part, spread, turn, q, near_sums, dual_gains, halves, arrived, final)
            arrived = []
            out.append(made)
        outs.append(out)
        moved = [[across_heads(piece, k) for piece in out] for k in range(1, head_devices)]
        arrived = [moved[0][0]] if g < groups - 1 and moved else []
        others += moved
        other_index += [lax.rem(head_index - k + head_devices, head_devices) * groups + g for k in range(1, head_devices)]

    own_index = [head_index * groups + g for g in range(groups)]
    early = len(others) - (head_devices - 1)

    keep, send = sums
    place = lax.axis_index("seq").astype(jnp.int32)[None]
    own, *pieces = pool_pieces(place, keep, swap(send, "rep", 1), spread)
    pieces = [
        lax.ppermute(piece, "seq", [(i, (i + k + 1) % spread) for i in range(spread)]) for k, piece in enumerate(pieces)
    ]
    parts = outs + others[:early]
    index = jnp.stack(own_index + other_index[:early] + [lax.axis_index("rep")]).astype(jnp.int32)
    acc, turn = out_part(parts, index, out_weight, None, F32)
    place = (seq_index * own.shape[0]).astype(jnp.int32)[None]
    place = place + (turn - index[:1])
    own = pool_own(place, bounds, own, pieces)
    pooled = [own] + [across_heads(own, k) for k in range(1, head_devices)]
    pooled_index = [lax.rem(head_index - k + head_devices, head_devices) for k in range(head_devices)]
    index = jnp.stack(other_index[early:] + pooled_index + [lax.axis_index("rep")]).astype(jnp.int32)
    return tuple(out_part(others[early:], index, out_weight, acc, BF, pooled)[:2])


def solution(mesh):
    placed = (
        P(("groups", "seq", "rep"), None),
        P(),
        P(None, "head"),
        P(None, "head"),
        P(None, "head"),
        P(None, "head"),
        P(None, "head"),
        P(None, "head"),
        P("groups", None),
    )
    return jax.shard_map(
        per_device,
        mesh=mesh,
        in_specs=placed,
        out_specs=(P(("groups", "seq", "rep"), "head"), P(("groups", "seq", "rep"), "head")),
        check_vma=False,
    )
```

```python
import functools

import jax
import jax.numpy as jnp
from jax import lax
from jax.experimental import pallas as pl
from jax.experimental.pallas import tpu as pltpu
from jax.sharding import PartitionSpec as P

DH = 64
R = 256
SEG = 128
HALF = SEG // 2
LANES = 2 * DH
SCORE_SCALE = DH ** (-0.5)
LOG2E = 1.4426950408889634

VMEM_LIMIT = 40 << 20
COST = pl.CostEstimate(flops=1 << 20, bytes_accessed=1 << 10, transcendentals=0)

LONG = pl.CostEstimate(flops=1 << 33, bytes_accessed=1 << 10, transcendentals=0)
TURN = jax.ShapeDtypeStruct((4,), jnp.int32)

softcap = 5.0
epsilon = 1e-05

BF = jnp.bfloat16
F32 = jnp.float32


def dot(a, b, dims=((1,), (0,))):
    return lax.dot_general(a, b, (dims, ((), ())), preferred_element_type=F32)


def exp_capped(values, scale):
    return jnp.exp2((softcap * LOG2E) * jnp.tanh(values * (scale / softcap)))


def pass_turn(ids_ref, turn_ref):
    for i in range(4):
        turn_ref[i] = ids_ref[i]


def vmem():
    return pl.BlockSpec(memory_space=pltpu.VMEM)


def smem():
    return pl.BlockSpec(memory_space=pltpu.SMEM)


def head_norm(values, gain):
    out = []
    for at in range(0, values.shape[1], LANES):
        x = values[:, at : at + LANES]
        first = lane_is_first(x.shape)

        def mean(y):
            low = jnp.sum(jnp.where(first, y, 0.0), axis=-1, keepdims=True)
            high = jnp.sum(jnp.where(first, 0.0, y), axis=-1, keepdims=True)
            return jnp.where(first, low, high) * (1.0 / DH)

        centred = x - mean(x)
        spread = mean(centred * centred)
        out.append((centred * lax.rsqrt(spread + epsilon) * gain[:, at : at + LANES]).astype(BF))
    return jnp.concatenate(out, axis=1)


def token_norm(x, gain):
    x = x.astype(F32)
    centred = x - jnp.mean(x, axis=-1, keepdims=True)
    spread = jnp.mean(centred * centred, axis=-1, keepdims=True)
    return (centred * lax.rsqrt(spread + epsilon) * gain).astype(BF)


def edge_rows(near_ref):
    rows = near_ref.shape[0]
    columns = [slice(at, at + 2 * LANES) for at in range(0, near_ref.shape[1], 2 * LANES)]
    return [jnp.concatenate([near_ref[at, c] for c in columns], axis=0) for at in (slice(0, HALF), slice(rows - HALF, rows))]


def front_kernel(first, last, group, pairs, tile, *refs):
    ids_ref, refs = refs[0], list(refs[1:])
    if first:
        x_hbm, gain_hbm, dual_hbm, wk_hbm, wv_hbm, wp_hbm = refs[:6]
        refs = refs[6:]
    else:
        given_ref, dual_ref, kv_ref, wp_ref = refs[:4]
        refs = refs[4:]
        if not last:
            wk_hbm, wv_hbm, wp_hbm = refs[:3]
            refs = refs[3:]
    earlier = [refs.pop(0) for _ in range(group)] if last else []
    normed_ref, near_ref, keep_ref, send_ref, edge_ref, turn_ref = refs[:6]
    refs = refs[6:]
    pass_turn(ids_ref, turn_ref)
    if not last:
        next_kv_ref, next_wp_ref = refs[:2]
        refs = refs[2:]
    raw_ref, p_ref, sem = refs[:3]
    if first:
        kv_ref, wp_ref, x_ref, gain_ref, dual_ref = refs[3:]
    rows = normed_ref.shape[0]
    width = pairs * LANES
    chunks = rows // tile
    used = 0

    def copy(source, target):
        nonlocal used
        made = pltpu.make_async_copy(source, target, sem.at[used])
        used += 1
        made.start()
        return made

    def weight_copies(g, kv, wp):
        own = pl.ds(g * width, width)
        heads = [
            copy(wk_hbm.at[:, own], kv.at[:, pl.ds(0, width)]),
            copy(wv_hbm.at[:, own], kv.at[:, pl.ds(width, width)]),
        ]
        return heads, [copy(wp_hbm.at[:, pl.ds(g * pairs * 2 * R, pairs * 2 * R)], wp)]

    def token_copy(i):
        at = pl.ds(i * tile, tile)
        return copy(x_hbm.at[at, :], x_ref.at[at, :])

    kv_copies, proj_copies, next_copies = [], [], []
    if first:
        token_copies = [token_copy(0)]
        small_copies = [copy(gain_hbm, gain_ref), copy(dual_hbm, dual_ref)]
        kv_copies, proj_copies = weight_copies(group, kv_ref, wp_ref)
        token_copies += [token_copy(i) for i in range(1, chunks)]
    for i in range(chunks):
        at = pl.ds(i * tile, tile)
        if first:
            token_copies[i].wait()
            if i == 0:
                for made in small_copies:
                    made.wait()
            normed_ref[at, :] = token_norm(x_ref[at, :], gain_ref[...])
        normed = normed_ref[at, :]
        if i == 0:
            for made in kv_copies:
                made.wait()
        both = dot(normed, kv_ref[...])
        key, value = both[:, :width], both[:, width:]
        for p in range(pairs):
            cols = slice(p * LANES, (p + 1) * LANES)
            raw = jnp.concatenate([key[:, cols], value[:, cols]], axis=1).astype(BF)
            raw_ref[2 * p * LANES : 2 * (p + 1) * LANES, at] = raw.T
        if i == 0:
            for made in proj_copies:
                made.wait()
        if i == 0 and not last:
            next_copies = sum(weight_copies(group + 1, next_kv_ref, next_wp_ref), [])
        p_ref[at, :] = exp_capped(dot(normed, wp_ref[...]), 1.0).astype(BF)
        near_ref[at, :width] = head_norm(key, dual_ref[0:1, group * width : (group + 1) * width])
        near_ref[at, width:] = head_norm(value, dual_ref[1:2, group * width : (group + 1) * width])
    total = []
    for p in range(pairs):
        full = dot(raw_ref[2 * p * LANES : 2 * (p + 1) * LANES, :], p_ref[:, 2 * p * R : 2 * (p + 1) * R])
        for part in range(4):
            head = part % 2
            total.append(full[part * DH : (part + 1) * DH, head * R : (head + 1) * R])
    for made in next_copies:
        made.wait()
    total = jnp.concatenate(total, axis=0).astype(BF)
    half = total.shape[0] // 2
    mine = ids_ref[0] == 0
    keep_ref[...] = jnp.where(mine, total[:half], total[half:])
    send_ref[:half, :] = jnp.where(mine, total[half:], total[:half])
    head, tail = edge_rows(near_ref)
    edge = head.shape[0]
    if last:
        for i, ref in enumerate(earlier):
            before = jnp.where(mine, ref[edge:, :], ref[:edge, :])
            send_ref[half + i * edge : half + (i + 1) * edge, :] = before
            edge_ref[i * edge : (i + 1) * edge, :] = jnp.where(mine, ref[:edge, :], ref[edge:, :])
        send_ref[half + group * edge :, :] = jnp.where(mine, tail, head)
        edge_ref[group * edge :, :] = jnp.where(mine, head, tail)
    else:
        edge_ref[:edge, :] = head
        edge_ref[edge:, :] = tail


def in_hbm(values):
    return pltpu.with_memory_space_constraint(values, pltpu.HBM)


def front(first, last, group, pairs, ids, tokens, gain, wk, wv, wp, dual, earlier, fetched):
    rows, depth = tokens.shape
    width = pairs * LANES
    half = pairs * R // 2
    tile = min(512 if first else 256, rows)
    edge = (group + 1) * pairs * HALF if last else 0
    outs = [
        jax.ShapeDtypeStruct((rows, depth), BF),
        jax.ShapeDtypeStruct((rows, 2 * width), BF),
        jax.ShapeDtypeStruct((half, R), BF),
        jax.ShapeDtypeStruct((half + edge, R), BF),
        jax.ShapeDtypeStruct((edge if last else 2 * pairs * HALF, R), BF),
        TURN,
    ]
    if not last:
        outs += [jax.ShapeDtypeStruct((depth, 2 * width), BF), jax.ShapeDtypeStruct((depth, 2 * pairs * R), BF)]
    hbm = pl.BlockSpec(memory_space=pltpu.HBM)
    earlier = earlier if last else []
    weights = [in_hbm(wk), in_hbm(wv), in_hbm(wp)]
    if first:
        ins = [hbm] * 6
        args = [in_hbm(tokens), in_hbm(gain), in_hbm(dual)] + weights
    else:
        ins = [vmem()] * 4 + ([] if last else [hbm] * 3)
        args = [tokens, dual, *fetched] + ([] if last else weights)
    ins = [smem()] + ins + [vmem()] * len(earlier)
    args = [ids] + args + earlier
    scratch = [
        pltpu.VMEM((2 * width, rows), BF),
        pltpu.VMEM((rows, 2 * pairs * R), BF),
        pltpu.SemaphoreType.DMA((rows // tile + 8,)),
    ]
    if first:
        scratch += [
            pltpu.VMEM((depth, 2 * width), BF),
            pltpu.VMEM((depth, 2 * pairs * R), BF),
            pltpu.VMEM((rows, depth), BF),
            pltpu.VMEM((1, depth), F32),
            pltpu.VMEM(dual.shape, F32),
        ]
    is_turn = [o is TURN for o in outs]
    return pl.pallas_call(
        functools.partial(front_kernel, first, last, group, pairs, tile),
        input_output_aliases={} if first else {1: 0},
        in_specs=ins,
        out_specs=[smem() if t else vmem() for t in is_turn],
        out_shape=outs,
        scratch_shapes=scratch,
        compiler_params=pltpu.CompilerParams(vmem_limit_bytes=VMEM_LIMIT),
        cost_estimate=pl.CostEstimate(
            flops=2 * rows * depth * (2 * width + 2 * pairs * R), bytes_accessed=4 << 20, transcendentals=0
        ),
        name="front",
    )(*args)


def lane_is_first(shape):
    return lax.broadcasted_iota(jnp.int32, shape, 1) < DH


def stacked(q):
    first = lane_is_first(q.shape)
    zero = jnp.zeros_like(q)
    return jnp.concatenate([jnp.where(first, q, zero), jnp.where(first, zero, q)], axis=0)


def unstack(both):
    rows = both.shape[0] // 2
    first = lane_is_first((rows, LANES))
    return (
        jnp.where(first, both[:rows, :LANES], both[rows:, :LANES]),
        jnp.where(first, both[:rows, LANES:], both[rows:, LANES:]),
    )


def near_kernel(pairs, group, groups, ids_ref, *refs):
    width = pairs * LANES
    if group == 0:
        normed_ref, wq_ref, core_ref, chip_ref, near_ref = refs[:5]
        q_refs, (out_ref, turn_ref, pad_ref) = refs[5:-3], refs[-3:]
        q_ref, rows = q_refs[0], normed_ref.shape[0]
        for start in range(0, rows, 256):
            at = slice(start, start + 256)
            q = dot(normed_ref[at, :], wq_ref[...])
            for g in range(groups):
                q_refs[g][at, :] = q[:, g * width : (g + 1) * width].astype(BF)
    else:
        given_ref, core_ref, chip_ref, near_ref, q_ref, out_ref, turn_ref, pad_ref = refs
        rows = q_ref.shape[0]
    is_first = ids_ref[0] == 0
    row = lax.broadcasted_iota(jnp.int32, (2 * SEG, LANES), 0)
    ones = jnp.ones((2 * SEG, LANES), F32)
    has_prev = jnp.where(ids_ref[1] != 0, 1.0, 0.0)
    has_next = jnp.where(ids_ref[2] != 0, 1.0, 0.0)
    segments = rows // SEG
    offset = core_ref.shape[0] - chip_ref.shape[0]
    pad_ref[HALF : HALF + rows, :] = near_ref[...]
    for c in range(pairs):
        at = (group * pairs + c) * HALF
        core = core_ref[offset + at : offset + at + HALF, :]
        chip = chip_ref[at : at + HALF, :]
        lanes = slice(2 * c * LANES, 2 * (c + 1) * LANES)
        pad_ref[0:HALF, lanes] = jnp.where(is_first, chip, core)
        pad_ref[HALF + rows :, lanes] = jnp.where(is_first, core, chip)
    for s in range(segments):
        count = ones
        if s == 0:
            count = jnp.where(row < HALF, has_prev, count)
        if s == segments - 1:
            count = jnp.where(row >= 3 * HALF, has_next, count)
        count = count.astype(BF)
        window = pl.ds(s * SEG, 2 * SEG)
        here = slice(s * SEG, (s + 1) * SEG)
        for p in range(pairs):
            cols = slice(p * LANES, (p + 1) * LANES)
            scores = dot(stacked(q_ref[here, cols]), pad_ref[window, cols], ((1,), (1,)))
            weights = exp_capped(scores, SCORE_SCALE).astype(BF)
            values = jnp.concatenate([pad_ref[window, width + p * LANES : width + (p + 1) * LANES], count], axis=1)
            top, bottom = unstack(dot(weights, values))
            out_ref[here, 2 * p * LANES : (2 * p + 1) * LANES] = top
            out_ref[here, (2 * p + 1) * LANES : (2 * p + 2) * LANES] = bottom
    pass_turn(ids_ref, turn_ref)


def near(pairs, group, groups, ids, source, wq, core, chip, near_pairs):
    rows = near_pairs.shape[0]
    width = pairs * LANES
    q = jax.ShapeDtypeStruct((rows, width), BF)
    count = groups if group == 0 else 1
    args = [source, wq] if group == 0 else [source]
    return pl.pallas_call(
        functools.partial(near_kernel, pairs, group, groups),
        in_specs=[smem()] + [vmem()] * (len(args) + 3),
        out_specs=[vmem()] * (count + 1) + [smem()],
        out_shape=[q] * count + [jax.ShapeDtypeStruct((rows, 2 * width), F32), TURN],
        input_output_aliases={} if group == 0 else {1: 0},
        scratch_shapes=[pltpu.VMEM((rows + SEG, 2 * width), BF)],
        compiler_params=pltpu.CompilerParams(vmem_limit_bytes=VMEM_LIMIT),
        cost_estimate=COST,
        name="near",
    )(ids, *args, core, chip, near_pairs)


def far_kernel(pairs, group, p, block, spread, waits, final, *refs):
    ids_ref, q_ref, near_ref, gains_ref = refs[:4]
    refs = refs[4:]
    is_first = ids_ref[0] == 0
    mine, other = refs[0][...], refs[1][...]
    total = jnp.concatenate([jnp.where(is_first, mine, other), jnp.where(is_first, other, mine)], axis=0)
    total = total[p * R : (p + 1) * R]
    refs = refs[2 + waits :]
    if final:
        bounds_ref, *earlier = refs[:-4]
        out_ref, keep_ref, send_ref, turn_ref = refs[-4:]
    else:
        out_ref, turn_ref = refs
    pass_turn(ids_ref, turn_ref)
    rows = q_ref.shape[0]

    def lanes(offset, scale=1):
        return pl.ds((offset + p) * scale * LANES, scale * LANES)

    gains = jnp.concatenate([gains_ref[:, lanes(group * pairs)]] * 2, axis=0).T

    def land(kind):
        parts = []
        for h in range(2):
            at = kind * LANES + h * DH
            values = total[at : at + DH].astype(F32)
            centred = values - jnp.mean(values, axis=0, keepdims=True)
            spread = jnp.mean(centred * centred, axis=0, keepdims=True)
            gain = gains[h * DH : (h + 1) * DH, 2 + kind : 3 + kind]
            parts.append((centred * lax.rsqrt(spread + epsilon) * gain).astype(BF))
        return jnp.concatenate(parts, axis=0)

    keys = land(0)
    values = jnp.concatenate([land(1), jnp.ones((LANES, R), BF)], axis=0)
    for start in range(0, rows, block):
        at = slice(start, start + block)
        weights = exp_capped(dot(stacked(q_ref[at, lanes(0)]), keys), SCORE_SCALE).astype(BF)
        top, bottom = unstack(dot(weights, values, ((1,), (1,))))
        near_sums = near_ref[at, lanes(0, 2)]
        out_ref[at, :] = ((top + near_sums[:, :LANES]) / (bottom + near_sums[:, LANES:])).astype(BF)
    if not final:
        return
    spans = bounds_ref.shape[1]
    position = ids_ref[3] + lax.broadcasted_iota(jnp.int32, (rows, spans), 0)
    member = (position >= bounds_ref[0:1, :]) & (position < bounds_ref[1:2, :])
    pieces = jnp.concatenate([ref[...] for ref in earlier + [out_ref]], axis=1)
    sums = dot(jnp.where(member, 1.0, 0.0).astype(BF), pieces, ((0,), (0,)))
    count = spans // (2 * spread)
    even = jnp.concatenate([sums[2 * i * count : (2 * i + 1) * count] for i in range(spread)], axis=0)
    odd = jnp.concatenate([sums[(2 * i + 1) * count : (2 * i + 2) * count] for i in range(spread)], axis=0)
    keep_ref[...] = jnp.where(is_first, even, odd)
    send_ref[...] = jnp.where(is_first, odd, even).astype(BF)


def far(pairs, group, p, spread, ids, q, near_sums, gains, halves, arrived, final):
    rows = q.shape[0]
    shapes = [jax.ShapeDtypeStruct((rows, LANES), BF)]
    if final:
        shape = (final[0].shape[1] // 2, len(final) * LANES)
        shapes += [jax.ShapeDtypeStruct(shape, F32), jax.ShapeDtypeStruct(shape, BF)]
    return pl.pallas_call(
        functools.partial(far_kernel, pairs, group, p, 256, spread, len(arrived), bool(final)),
        in_specs=[smem()]
        + [vmem()] * (3 + len(halves))
        + [pl.BlockSpec(memory_space=pl.ANY)] * len(arrived)
        + [vmem()] * len(final),
        out_specs=[vmem()] * len(shapes) + [smem()],
        out_shape=shapes + [TURN],
        compiler_params=pltpu.CompilerParams(vmem_limit_bytes=VMEM_LIMIT),
        cost_estimate=COST,
        name="far",
    )(ids, q, near_sums, gains, *halves, *arrived, *final)


def out_kernel(count, pairs, spans, *refs):
    ids_ref, refs = refs[0], refs[1:]
    tokens, refs = [refs[j * pairs : (j + 1) * pairs] for j in range(count)], refs[count * pairs :]
    pooled, refs = refs[:spans], refs[spans:]
    *refs, turn_ref = refs
    turn_ref[0] = ids_ref[0]
    outs = refs[-2:] if spans else refs[-1:]
    weight_ref, *acc = refs[: -len(outs)]
    rows, width = tokens[0][0].shape[0], pairs * LANES
    tile = min(256, rows)

    def weight(j, size):
        return weight_ref[pl.ds(pl.multiple_of(ids_ref[j] * size, size), size), :]

    for start in range(0, rows, tile):
        at = slice(start, start + tile)
        total = acc[0][at, :] if acc else None
        for j in range(count):
            term = dot(jnp.concatenate([ref[at, :] for ref in tokens[j]], axis=1), weight(j, width))
            total = term if total is None else total + term
        outs[0][at, :] = total.astype(outs[0].dtype)
    if spans:
        outs[1][...] = sum(dot(ref[...], weight(count + k, ref.shape[1])) for k, ref in enumerate(pooled))


def out_part(parts, index, weight, acc, dtype, pooled=()):
    count = len(parts)
    pairs = len(parts[0])
    rows = parts[0][0].shape[0]
    columns = weight.shape[1]
    extra = [] if acc is None else [acc]
    shapes = [jax.ShapeDtypeStruct((rows, columns), dtype)]
    shapes += [jax.ShapeDtypeStruct((pooled[0].shape[0], columns), F32)] if pooled else []
    return pl.pallas_call(
        functools.partial(out_kernel, count, pairs, len(pooled)),
        in_specs=[smem()] + [vmem()] * (count * pairs + len(pooled) + 1 + len(extra)),
        out_specs=[vmem()] * len(shapes) + [smem()],
        out_shape=shapes + [jax.ShapeDtypeStruct((1,), jnp.int32)],
        compiler_params=pltpu.CompilerParams(vmem_limit_bytes=VMEM_LIMIT),
        cost_estimate=COST,
        name="out",
    )(index, *[piece for part in parts for piece in part], *pooled, weight, *extra)


def pieces_kernel(ids_ref, keep_ref, got_ref, *out_refs):
    spread = len(out_refs)
    count = keep_ref.shape[0] // spread
    for k, ref in enumerate(out_refs):
        at = pl.ds(pl.multiple_of(lax.rem(ids_ref[0] + k, spread) * count, count), count)
        ref[...] = (keep_ref[at, :] + got_ref[at, :].astype(F32)).astype(ref.dtype)


def pool_pieces(place, keep, got, spread):
    count = keep.shape[0] // spread
    shape = (count, keep.shape[1])
    return pl.pallas_call(
        pieces_kernel,
        in_specs=[smem(), vmem(), vmem()],
        out_specs=[vmem()] * spread,
        out_shape=[jax.ShapeDtypeStruct(shape, F32)] + [jax.ShapeDtypeStruct(shape, BF)] * (spread - 1),
        compiler_params=pltpu.CompilerParams(vmem_limit_bytes=VMEM_LIMIT),
        cost_estimate=COST,
        name="pool_pieces",
    )(place, keep, got)


def own_kernel(ids_ref, bounds_ref, own_ref, *refs):
    total = own_ref[...]
    for ref in refs[:-1]:
        total = total + ref[...].astype(F32)
    count = total.shape[0]
    rows = [
        total[i : i + 1] / (bounds_ref[1, ids_ref[0] + i] - bounds_ref[0, ids_ref[0] + i]).astype(F32)
        for i in range(count)
    ]
    refs[-1][...] = jnp.concatenate(rows, axis=0).astype(BF)


def pool_own(place, bounds, own, others):
    return pl.pallas_call(
        own_kernel,
        in_specs=[smem(), smem()] + [vmem()] * (1 + len(others)),
        out_specs=vmem(),
        out_shape=jax.ShapeDtypeStruct(own.shape, BF),
        compiler_params=pltpu.CompilerParams(vmem_limit_bytes=VMEM_LIMIT),
        cost_estimate=COST,
        name="pool_own",
    )(place, bounds, own, *others)


def swap(values, axis, step):
    count = lax.axis_size(axis)
    return lax.ppermute(values, axis, [(i, i ^ step) for i in range(count)])


def across_heads(values, step):
    count = lax.axis_size("head")
    return lax.ppermute(values, "head", [(i, (i + step) % count) for i in range(count)])


def add_kernel(a_ref, b_ref, out_ref):
    count = a_ref.shape[0]
    out_ref[...] = (a_ref[...].astype(F32) + b_ref[:count, :].astype(F32)).astype(BF)


def add_call(a, b, cost=COST):
    return pl.pallas_call(
        add_kernel,
        in_specs=[vmem()] * 2,
        out_specs=vmem(),
        out_shape=jax.ShapeDtypeStruct(a.shape, BF),
        compiler_params=pltpu.CompilerParams(vmem_limit_bytes=VMEM_LIMIT),
        cost_estimate=cost,
        name="add",
    )(a, b)


def steps_of(axis):
    step = 1
    while step < lax.axis_size(axis):
        yield step
        step *= 2


def per_device(
    book_tokens,
    norm_gain,
    query_weight,
    key_weight,
    value_weight,
    proj_weight,
    dual_gains,
    out_weight,
    span_bounds,
):
    rows = book_tokens.shape[0]
    seq_devices = lax.axis_size(("seq", "rep"))
    seq_index = lax.axis_index(("seq", "rep"))
    head_devices = lax.axis_size("head")
    head_index = lax.axis_index("head")
    first_row = seq_index * rows
    all_pairs = query_weight.shape[1] // LANES
    groups = 2 if all_pairs == 4 else all_pairs
    pairs = all_pairs // groups
    ids = jnp.stack(
        [lax.axis_index("rep"), (seq_index > 0).astype(jnp.int32), (seq_index < seq_devices - 1).astype(jnp.int32), first_row]
    ).astype(jnp.int32)
    gain = norm_gain[None, :]
    bounds = span_bounds.T

    both = ("seq", "rep")
    chips = [(i, i + 1) for i in range(1, seq_devices - 1, 2)]
    chips = chips + [(b, a) for a, b in chips]
    steps = list(steps_of("seq"))
    tie = lax.optimization_barrier

    fronts, mine, normed = [], [], book_tokens
    turn = ids
    fetched = []
    for g in range(groups):
        last = g == groups - 1
        normed, *outs = front(g == 0, last, g, pairs, turn, normed, gain, key_weight, value_weight, proj_weight,
                              dual_gains, [f[3] for f in fronts], fetched)
        outs, turn, fetched = outs[:4], outs[4], outs[5:]
        fronts.append(outs)
        send, edge = outs[2], outs[3]
        if last:
            for f in range(g):
                for step in steps[:-1]:
                    got, turn = tie((swap(mine[f], "seq", step), turn))
                    mine[f] = add_call(mine[f], got, LONG)
                mine[f], turn = tie((mine[f], turn))
        core = swap(send, "rep", 1)
        if last:
            chip = lax.ppermute(edge, both, chips)
        mine.append(add_call(outs[1], core))
        mine[g], turn = tie((mine[g], turn))

    if groups == 1:
        for step in steps[:-1]:
            mine[0] = add_call(mine[0], swap(mine[0], "seq", step))

    spread = lax.axis_size("seq")
    outs, arrived, others, other_index, queries = [], [], [], [], []
    for g in range(groups):
        source = queries[g] if g else normed
        *made, near_sums, turn = near(pairs, g, groups, turn, source, query_weight, core, chip, fronts[g][0])
        queries = queries if g else made
        q = made[0]
        got, turn = tie((swap(mine[g], "seq", steps[-1]), turn))
        total = add_call(mine[g], got)
        other = swap(total, "rep", 1)
        if g == groups - 2:
            for step in steps[:-1]:
                got, turn = tie((swap(mine[-1], "seq", step), turn))
                mine[-1] = add_call(mine[-1], got)
            mine[-1], turn = tie((mine[-1], turn))
        out = []
        for p in range(pairs):
            final = []
            if g == groups - 1 and p == pairs - 1:
                final = [bounds] + [piece for o in outs for piece in o] + out
            made, *sums, turn = far(pairs, g, p, spread, turn, q, near_sums, dual_gains, [total, other], arrived, final)
            arrived = []
            out.append(made)
        outs.append(out)
        moved = [[across_heads(piece, k) for piece in out] for k in range(1, head_devices)]
        arrived = [moved[0][0]] if g < groups - 1 and moved else []
        others += moved
        other_index += [lax.rem(head_index - k + head_devices, head_devices) * groups + g for k in range(1, head_devices)]

    own_index = [head_index * groups + g for g in range(groups)]
    early = len(others) - (head_devices - 1)

    keep, send = sums
    place = lax.axis_index("seq").astype(jnp.int32)[None]
    own, *pieces = pool_pieces(place, keep, swap(send, "rep", 1), spread)
    pieces = [
        lax.ppermute(piece, "seq", [(i, (i + k + 1) % spread) for i in range(spread)]) for k, piece in enumerate(pieces)
    ]
    parts = outs + others[:early]
    index = jnp.stack(own_index + other_index[:early]).astype(jnp.int32)
    acc, turn = out_part(parts, index, out_weight, None, F32)
    place = (seq_index * own.shape[0]).astype(jnp.int32)[None]
    place = place + (turn - index[:1])
    own = pool_own(place, bounds, own, pieces)
    pooled = [own] + [across_heads(own, k) for k in range(1, head_devices)]
    pooled_index = [lax.rem(head_index - k + head_devices, head_devices) for k in range(head_devices)]
    index = jnp.stack(other_index[early:] + pooled_index).astype(jnp.int32)
    return tuple(out_part(others[early:], index, out_weight, acc, BF, pooled)[:2])


def solution(mesh):
    placed = (
        P(("groups", "seq", "rep"), None),
        P(),
        P(None, "head"),
        P(None, "head"),
        P(None, "head"),
        P(None, "head"),
        P(None, "head"),
        P(None, "head"),
        P("groups", None),
    )
    return jax.shard_map(
        per_device,
        mesh=mesh,
        in_specs=placed,
        out_specs=(P(("groups", "seq", "rep"), "head"), P(("groups", "seq", "rep"), "head")),
        check_vma=False,
    )
```

```python
import functools

import jax
import jax.numpy as jnp
from jax import lax
from jax.experimental import pallas as pl
from jax.experimental.pallas import tpu as pltpu
from jax.sharding import PartitionSpec as P

DH = 64
R = 256
SEG = 128
HALF = SEG // 2
LANES = 2 * DH
SCORE_SCALE = DH ** (-0.5)
LOG2E = 1.4426950408889634

VMEM_LIMIT = 40 << 20
COST = pl.CostEstimate(flops=1 << 20, bytes_accessed=1 << 10, transcendentals=0)

LONG = pl.CostEstimate(flops=1 << 33, bytes_accessed=1 << 10, transcendentals=0)
TURN = jax.ShapeDtypeStruct((4,), jnp.int32)

softcap = 5.0
epsilon = 1e-05

BF = jnp.bfloat16
F32 = jnp.float32


def dot(a, b, dims=((1,), (0,))):
    return lax.dot_general(a, b, (dims, ((), ())), preferred_element_type=F32)


def exp_capped(values, scale):
    return jnp.exp2((softcap * LOG2E) * jnp.tanh(values * (scale / softcap)))


def pass_turn(ids_ref, turn_ref):
    for i in range(4):
        turn_ref[i] = ids_ref[i]


def vmem():
    return pl.BlockSpec(memory_space=pltpu.VMEM)


def smem():
    return pl.BlockSpec(memory_space=pltpu.SMEM)


def head_norm(values, gain):
    out = []
    for at in range(0, values.shape[1], LANES):
        x = values[:, at : at + LANES]
        first = lane_is_first(x.shape)

        def mean(y):
            low = jnp.sum(jnp.where(first, y, 0.0), axis=-1, keepdims=True)
            high = jnp.sum(jnp.where(first, 0.0, y), axis=-1, keepdims=True)
            return jnp.where(first, low, high) * (1.0 / DH)

        centred = x - mean(x)
        spread = mean(centred * centred)
        out.append((centred * lax.rsqrt(spread + epsilon) * gain[:, at : at + LANES]).astype(BF))
    return jnp.concatenate(out, axis=1)


def token_norm(x, gain):
    x = x.astype(F32)
    centred = x - jnp.mean(x, axis=-1, keepdims=True)
    spread = jnp.mean(centred * centred, axis=-1, keepdims=True)
    return (centred * lax.rsqrt(spread + epsilon) * gain).astype(BF)


def edge_rows(near_ref):
    rows = near_ref.shape[0]
    columns = [slice(at, at + 2 * LANES) for at in range(0, near_ref.shape[1], 2 * LANES)]
    return [jnp.concatenate([near_ref[at, c] for c in columns], axis=0) for at in (slice(0, HALF), slice(rows - HALF, rows))]


def front_kernel(first, last, group, pairs, tile, *refs):
    ids_ref, refs = refs[0], list(refs[1:])
    if first:
        x_hbm, gain_hbm, dual_hbm, wk_hbm, wv_hbm, wp_hbm = refs[:6]
        refs = refs[6:]
    else:
        given_ref, dual_ref, kv_ref, wp_ref = refs[:4]
        refs = refs[4:]
        if not last:
            wk_hbm, wv_hbm, wp_hbm = refs[:3]
            refs = refs[3:]
    earlier = [refs.pop(0) for _ in range(group)] if last else []
    normed_ref, near_ref, keep_ref, send_ref, edge_ref, turn_ref = refs[:6]
    refs = refs[6:]
    pass_turn(ids_ref, turn_ref)
    if not last:
        next_kv_ref, next_wp_ref = refs[:2]
        refs = refs[2:]
    raw_ref, p_ref, sem = refs[:3]
    if first:
        kv_ref, wp_ref, x_ref, gain_ref, dual_ref = refs[3:]
    rows = normed_ref.shape[0]
    width = pairs * LANES
    chunks = rows // tile
    used = 0

    def copy(source, target):
        nonlocal used
        made = pltpu.make_async_copy(source, target, sem.at[used])
        used += 1
        made.start()
        return made

    def weight_copies(g, kv, wp):
        own = pl.ds(g * width, width)
        heads = [
            copy(wk_hbm.at[:, own], kv.at[:, pl.ds(0, width)]),
            copy(wv_hbm.at[:, own], kv.at[:, pl.ds(width, width)]),
        ]
        return heads, [copy(wp_hbm.at[:, pl.ds(g * pairs * 2 * R, pairs * 2 * R)], wp)]

    def token_copy(i):
        at = pl.ds(i * tile, tile)
        return copy(x_hbm.at[at, :], x_ref.at[at, :])

    kv_copies, proj_copies, next_copies = [], [], []
    if first:
        token_copies = [token_copy(0)]
        small_copies = [copy(gain_hbm, gain_ref), copy(dual_hbm, dual_ref)]
        kv_copies, proj_copies = weight_copies(group, kv_ref, wp_ref)
        token_copies += [token_copy(i) for i in range(1, chunks)]
    for i in range(chunks):
        at = pl.ds(i * tile, tile)
        if first:
            token_copies[i].wait()
            if i == 0:
                for made in small_copies:
                    made.wait()
            normed_ref[at, :] = token_norm(x_ref[at, :], gain_ref[...])
        normed = normed_ref[at, :]
        if i == 0:
            for made in kv_copies:
                made.wait()
        both = dot(normed, kv_ref[...])
        key, value = both[:, :width], both[:, width:]
        for p in range(pairs):
            cols = slice(p * LANES, (p + 1) * LANES)
            raw = jnp.concatenate([key[:, cols], value[:, cols]], axis=1).astype(BF)
            raw_ref[2 * p * LANES : 2 * (p + 1) * LANES, at] = raw.T
        if i == 0:
            for made in proj_copies:
                made.wait()
        p_ref[at, :] = exp_capped(dot(normed, wp_ref[...]), 1.0).astype(BF)
        if i == 0 and not last:
            next_copies = sum(weight_copies(group + 1, next_kv_ref, next_wp_ref), [])
        near_ref[at, :width] = head_norm(key, dual_ref[0:1, group * width : (group + 1) * width])
        near_ref[at, width:] = head_norm(value, dual_ref[1:2, group * width : (group + 1) * width])
    total = []
    for p in range(pairs):
        full = dot(raw_ref[2 * p * LANES : 2 * (p + 1) * LANES, :], p_ref[:, 2 * p * R : 2 * (p + 1) * R])
        for part in range(4):
            head = part % 2
            total.append(full[part * DH : (part + 1) * DH, head * R : (head + 1) * R])
    for made in next_copies:
        made.wait()
    total = jnp.concatenate(total, axis=0).astype(BF)
    half = total.shape[0] // 2
    mine = ids_ref[0] == 0
    keep_ref[...] = jnp.where(mine, total[:half], total[half:])
    send_ref[:half, :] = jnp.where(mine, total[half:], total[:half])
    head, tail = edge_rows(near_ref)
    edge = head.shape[0]
    if last:
        for i, ref in enumerate(earlier):
            before = jnp.where(mine, ref[edge:, :], ref[:edge, :])
            send_ref[half + i * edge : half + (i + 1) * edge, :] = before
            edge_ref[i * edge : (i + 1) * edge, :] = jnp.where(mine, ref[:edge, :], ref[edge:, :])
        send_ref[half + group * edge :, :] = jnp.where(mine, tail, head)
        edge_ref[group * edge :, :] = jnp.where(mine, head, tail)
    else:
        edge_ref[:edge, :] = head
        edge_ref[edge:, :] = tail


def in_hbm(values):
    return pltpu.with_memory_space_constraint(values, pltpu.HBM)


def front(first, last, group, pairs, ids, tokens, gain, wk, wv, wp, dual, earlier, fetched):
    rows, depth = tokens.shape
    width = pairs * LANES
    half = pairs * R // 2
    tile = min(512 if first else 256, rows)
    edge = (group + 1) * pairs * HALF if last else 0
    outs = [
        jax.ShapeDtypeStruct((rows, depth), BF),
        jax.ShapeDtypeStruct((rows, 2 * width), BF),
        jax.ShapeDtypeStruct((half, R), BF),
        jax.ShapeDtypeStruct((half + edge, R), BF),
        jax.ShapeDtypeStruct((edge if last else 2 * pairs * HALF, R), BF),
        TURN,
    ]
    if not last:
        outs += [jax.ShapeDtypeStruct((depth, 2 * width), BF), jax.ShapeDtypeStruct((depth, 2 * pairs * R), BF)]
    hbm = pl.BlockSpec(memory_space=pltpu.HBM)
    earlier = earlier if last else []
    weights = [in_hbm(wk), in_hbm(wv), in_hbm(wp)]
    if first:
        ins = [hbm] * 6
        args = [in_hbm(tokens), in_hbm(gain), in_hbm(dual)] + weights
    else:
        ins = [vmem()] * 4 + ([] if last else [hbm] * 3)
        args = [tokens, dual, *fetched] + ([] if last else weights)
    ins = [smem()] + ins + [vmem()] * len(earlier)
    args = [ids] + args + earlier
    scratch = [
        pltpu.VMEM((2 * width, rows), BF),
        pltpu.VMEM((rows, 2 * pairs * R), BF),
        pltpu.SemaphoreType.DMA((rows // tile + 8,)),
    ]
    if first:
        scratch += [
            pltpu.VMEM((depth, 2 * width), BF),
            pltpu.VMEM((depth, 2 * pairs * R), BF),
            pltpu.VMEM((rows, depth), BF),
            pltpu.VMEM((1, depth), F32),
            pltpu.VMEM(dual.shape, F32),
        ]
    is_turn = [o is TURN for o in outs]
    return pl.pallas_call(
        functools.partial(front_kernel, first, last, group, pairs, tile),
        input_output_aliases={} if first else {1: 0},
        in_specs=ins,
        out_specs=[smem() if t else vmem() for t in is_turn],
        out_shape=outs,
        scratch_shapes=scratch,
        compiler_params=pltpu.CompilerParams(vmem_limit_bytes=VMEM_LIMIT),
        cost_estimate=pl.CostEstimate(
            flops=2 * rows * depth * (2 * width + 2 * pairs * R), bytes_accessed=4 << 20, transcendentals=0
        ),
        name="front",
    )(*args)


def lane_is_first(shape):
    return lax.broadcasted_iota(jnp.int32, shape, 1) < DH


def stacked(q):
    first = lane_is_first(q.shape)
    zero = jnp.zeros_like(q)
    return jnp.concatenate([jnp.where(first, q, zero), jnp.where(first, zero, q)], axis=0)


def unstack(both):
    rows = both.shape[0] // 2
    first = lane_is_first((rows, LANES))
    return (
        jnp.where(first, both[:rows, :LANES], both[rows:, :LANES]),
        jnp.where(first, both[:rows, LANES:], both[rows:, LANES:]),
    )


def near_kernel(pairs, group, groups, ids_ref, *refs):
    width = pairs * LANES
    if group == 0:
        normed_ref, wq_ref, core_ref, chip_ref, near_ref = refs[:5]
        q_refs, (out_ref, turn_ref, pad_ref) = refs[5:-3], refs[-3:]
        q_ref, rows = q_refs[0], normed_ref.shape[0]
        for start in range(0, rows, 256):
            at = slice(start, start + 256)
            q = dot(normed_ref[at, :], wq_ref[...])
            for g in range(groups):
                q_refs[g][at, :] = q[:, g * width : (g + 1) * width].astype(BF)
    else:
        given_ref, core_ref, chip_ref, near_ref, q_ref, out_ref, turn_ref, pad_ref = refs
        rows = q_ref.shape[0]
    is_first = ids_ref[0] == 0
    row = lax.broadcasted_iota(jnp.int32, (2 * SEG, LANES), 0)
    ones = jnp.ones((2 * SEG, LANES), F32)
    has_prev = jnp.where(ids_ref[1] != 0, 1.0, 0.0)
    has_next = jnp.where(ids_ref[2] != 0, 1.0, 0.0)
    segments = rows // SEG
    offset = core_ref.shape[0] - chip_ref.shape[0]
    pad_ref[HALF : HALF + rows, :] = near_ref[...]
    for c in range(pairs):
        at = (group * pairs + c) * HALF
        core = core_ref[offset + at : offset + at + HALF, :]
        chip = chip_ref[at : at + HALF, :]
        lanes = slice(2 * c * LANES, 2 * (c + 1) * LANES)
        pad_ref[0:HALF, lanes] = jnp.where(is_first, chip, core)
        pad_ref[HALF + rows :, lanes] = jnp.where(is_first, core, chip)
    for s in range(segments):
        count = ones
        if s == 0:
            count = jnp.where(row < HALF, has_prev, count)
        if s == segments - 1:
            count = jnp.where(row >= 3 * HALF, has_next, count)
        count = count.astype(BF)
        window = pl.ds(s * SEG, 2 * SEG)
        here = slice(s * SEG, (s + 1) * SEG)
        for p in range(pairs):
            cols = slice(p * LANES, (p + 1) * LANES)
            scores = dot(stacked(q_ref[here, cols]), pad_ref[window, cols], ((1,), (1,)))
            weights = exp_capped(scores, SCORE_SCALE).astype(BF)
            values = jnp.concatenate([pad_ref[window, width + p * LANES : width + (p + 1) * LANES], count], axis=1)
            top, bottom = unstack(dot(weights, values))
            out_ref[here, 2 * p * LANES : (2 * p + 1) * LANES] = top
            out_ref[here, (2 * p + 1) * LANES : (2 * p + 2) * LANES] = bottom
    pass_turn(ids_ref, turn_ref)


def near(pairs, group, groups, ids, source, wq, core, chip, near_pairs):
    rows = near_pairs.shape[0]
    width = pairs * LANES
    q = jax.ShapeDtypeStruct((rows, width), BF)
    count = groups if group == 0 else 1
    args = [source, wq] if group == 0 else [source]
    return pl.pallas_call(
        functools.partial(near_kernel, pairs, group, groups),
        in_specs=[smem()] + [vmem()] * (len(args) + 3),
        out_specs=[vmem()] * (count + 1) + [smem()],
        out_shape=[q] * count + [jax.ShapeDtypeStruct((rows, 2 * width), F32), TURN],
        input_output_aliases={} if group == 0 else {1: 0},
        scratch_shapes=[pltpu.VMEM((rows + SEG, 2 * width), BF)],
        compiler_params=pltpu.CompilerParams(vmem_limit_bytes=VMEM_LIMIT),
        cost_estimate=COST,
        name="near",
    )(ids, *args, core, chip, near_pairs)


def far_kernel(pairs, group, p, block, spread, waits, final, *refs):
    ids_ref, q_ref, near_ref, gains_ref = refs[:4]
    refs = refs[4:]
    is_first = ids_ref[0] == 0
    mine, other = refs[0][...], refs[1][...]
    total = jnp.concatenate([jnp.where(is_first, mine, other), jnp.where(is_first, other, mine)], axis=0)
    total = total[p * R : (p + 1) * R]
    refs = refs[2 + waits :]
    if final:
        bounds_ref, *earlier = refs[:-4]
        out_ref, keep_ref, send_ref, turn_ref = refs[-4:]
    else:
        out_ref, turn_ref = refs
    pass_turn(ids_ref, turn_ref)
    rows = q_ref.shape[0]

    def lanes(offset, scale=1):
        return pl.ds((offset + p) * scale * LANES, scale * LANES)

    gains = jnp.concatenate([gains_ref[:, lanes(group * pairs)]] * 2, axis=0).T

    def land(kind):
        parts = []
        for h in range(2):
            at = kind * LANES + h * DH
            values = total[at : at + DH].astype(F32)
            centred = values - jnp.mean(values, axis=0, keepdims=True)
            spread = jnp.mean(centred * centred, axis=0, keepdims=True)
            gain = gains[h * DH : (h + 1) * DH, 2 + kind : 3 + kind]
            parts.append((centred * lax.rsqrt(spread + epsilon) * gain).astype(BF))
        return jnp.concatenate(parts, axis=0)

    keys = land(0)
    values = jnp.concatenate([land(1), jnp.ones((LANES, R), BF)], axis=0)
    for start in range(0, rows, block):
        at = slice(start, start + block)
        weights = exp_capped(dot(stacked(q_ref[at, lanes(0)]), keys), SCORE_SCALE).astype(BF)
        top, bottom = unstack(dot(weights, values, ((1,), (1,))))
        near_sums = near_ref[at, lanes(0, 2)]
        out_ref[at, :] = ((top + near_sums[:, :LANES]) / (bottom + near_sums[:, LANES:])).astype(BF)
    if not final:
        return
    spans = bounds_ref.shape[1]
    position = ids_ref[3] + lax.broadcasted_iota(jnp.int32, (rows, spans), 0)
    member = (position >= bounds_ref[0:1, :]) & (position < bounds_ref[1:2, :])
    pieces = jnp.concatenate([ref[...] for ref in earlier + [out_ref]], axis=1)
    sums = dot(jnp.where(member, 1.0, 0.0).astype(BF), pieces, ((0,), (0,)))
    count = spans // (2 * spread)
    even = jnp.concatenate([sums[2 * i * count : (2 * i + 1) * count] for i in range(spread)], axis=0)
    odd = jnp.concatenate([sums[(2 * i + 1) * count : (2 * i + 2) * count] for i in range(spread)], axis=0)
    keep_ref[...] = jnp.where(is_first, even, odd)
    send_ref[...] = jnp.where(is_first, odd, even).astype(BF)


def far(pairs, group, p, spread, ids, q, near_sums, gains, halves, arrived, final):
    rows = q.shape[0]
    shapes = [jax.ShapeDtypeStruct((rows, LANES), BF)]
    if final:
        shape = (final[0].shape[1] // 2, len(final) * LANES)
        shapes += [jax.ShapeDtypeStruct(shape, F32), jax.ShapeDtypeStruct(shape, BF)]
    return pl.pallas_call(
        functools.partial(far_kernel, pairs, group, p, 256, spread, len(arrived), bool(final)),
        in_specs=[smem()]
        + [vmem()] * (3 + len(halves))
        + [pl.BlockSpec(memory_space=pl.ANY)] * len(arrived)
        + [vmem()] * len(final),
        out_specs=[vmem()] * len(shapes) + [smem()],
        out_shape=shapes + [TURN],
        compiler_params=pltpu.CompilerParams(vmem_limit_bytes=VMEM_LIMIT),
        cost_estimate=COST,
        name="far",
    )(ids, q, near_sums, gains, *halves, *arrived, *final)


def out_kernel(count, pairs, spans, *refs):
    ids_ref, refs = refs[0], refs[1:]
    tokens, refs = [refs[j * pairs : (j + 1) * pairs] for j in range(count)], refs[count * pairs :]
    pooled, refs = refs[:spans], refs[spans:]
    *refs, turn_ref = refs
    turn_ref[0] = ids_ref[0]
    outs = refs[-2:] if spans else refs[-1:]
    weight_ref, *acc = refs[: -len(outs)]
    rows, width = tokens[0][0].shape[0], pairs * LANES
    tile = min(256, rows)

    def weight(j, size):
        return weight_ref[pl.ds(pl.multiple_of(ids_ref[j] * size, size), size), :]

    for start in range(0, rows, tile):
        at = slice(start, start + tile)
        total = acc[0][at, :] if acc else None
        for j in range(count):
            term = dot(jnp.concatenate([ref[at, :] for ref in tokens[j]], axis=1), weight(j, width))
            total = term if total is None else total + term
        outs[0][at, :] = total.astype(outs[0].dtype)
    if spans:
        outs[1][...] = sum(dot(ref[...], weight(count + k, ref.shape[1])) for k, ref in enumerate(pooled))


def out_part(parts, index, weight, acc, dtype, pooled=()):
    count = len(parts)
    pairs = len(parts[0])
    rows = parts[0][0].shape[0]
    columns = weight.shape[1]
    extra = [] if acc is None else [acc]
    shapes = [jax.ShapeDtypeStruct((rows, columns), dtype)]
    shapes += [jax.ShapeDtypeStruct((pooled[0].shape[0], columns), F32)] if pooled else []
    return pl.pallas_call(
        functools.partial(out_kernel, count, pairs, len(pooled)),
        in_specs=[smem()] + [vmem()] * (count * pairs + len(pooled) + 1 + len(extra)),
        out_specs=[vmem()] * len(shapes) + [smem()],
        out_shape=shapes + [jax.ShapeDtypeStruct((1,), jnp.int32)],
        compiler_params=pltpu.CompilerParams(vmem_limit_bytes=VMEM_LIMIT),
        cost_estimate=COST,
        name="out",
    )(index, *[piece for part in parts for piece in part], *pooled, weight, *extra)


def pieces_kernel(ids_ref, keep_ref, got_ref, *out_refs):
    spread = len(out_refs)
    count = keep_ref.shape[0] // spread
    for k, ref in enumerate(out_refs):
        at = pl.ds(pl.multiple_of(lax.rem(ids_ref[0] + k, spread) * count, count), count)
        ref[...] = (keep_ref[at, :] + got_ref[at, :].astype(F32)).astype(ref.dtype)


def pool_pieces(place, keep, got, spread):
    count = keep.shape[0] // spread
    shape = (count, keep.shape[1])
    return pl.pallas_call(
        pieces_kernel,
        in_specs=[smem(), vmem(), vmem()],
        out_specs=[vmem()] * spread,
        out_shape=[jax.ShapeDtypeStruct(shape, F32)] + [jax.ShapeDtypeStruct(shape, BF)] * (spread - 1),
        compiler_params=pltpu.CompilerParams(vmem_limit_bytes=VMEM_LIMIT),
        cost_estimate=COST,
        name="pool_pieces",
    )(place, keep, got)


def own_kernel(ids_ref, bounds_ref, own_ref, *refs):
    total = own_ref[...]
    for ref in refs[:-1]:
        total = total + ref[...].astype(F32)
    count = total.shape[0]
    rows = [
        total[i : i + 1] / (bounds_ref[1, ids_ref[0] + i] - bounds_ref[0, ids_ref[0] + i]).astype(F32)
        for i in range(count)
    ]
    refs[-1][...] = jnp.concatenate(rows, axis=0).astype(BF)


def pool_own(place, bounds, own, others):
    return pl.pallas_call(
        own_kernel,
        in_specs=[smem(), smem()] + [vmem()] * (1 + len(others)),
        out_specs=vmem(),
        out_shape=jax.ShapeDtypeStruct(own.shape, BF),
        compiler_params=pltpu.CompilerParams(vmem_limit_bytes=VMEM_LIMIT),
        cost_estimate=COST,
        name="pool_own",
    )(place, bounds, own, *others)


def swap(values, axis, step):
    count = lax.axis_size(axis)
    return lax.ppermute(values, axis, [(i, i ^ step) for i in range(count)])


def across_heads(values, step):
    count = lax.axis_size("head")
    return lax.ppermute(values, "head", [(i, (i + step) % count) for i in range(count)])


def add_kernel(a_ref, b_ref, out_ref):
    count = a_ref.shape[0]
    out_ref[...] = (a_ref[...].astype(F32) + b_ref[:count, :].astype(F32)).astype(BF)


def add_call(a, b, cost=COST):
    return pl.pallas_call(
        add_kernel,
        in_specs=[vmem()] * 2,
        out_specs=vmem(),
        out_shape=jax.ShapeDtypeStruct(a.shape, BF),
        compiler_params=pltpu.CompilerParams(vmem_limit_bytes=VMEM_LIMIT),
        cost_estimate=cost,
        name="add",
    )(a, b)


def steps_of(axis):
    step = 1
    while step < lax.axis_size(axis):
        yield step
        step *= 2


def per_device(
    book_tokens,
    norm_gain,
    query_weight,
    key_weight,
    value_weight,
    proj_weight,
    dual_gains,
    out_weight,
    span_bounds,
):
    rows = book_tokens.shape[0]
    seq_devices = lax.axis_size(("seq", "rep"))
    seq_index = lax.axis_index(("seq", "rep"))
    head_devices = lax.axis_size("head")
    head_index = lax.axis_index("head")
    first_row = seq_index * rows
    all_pairs = query_weight.shape[1] // LANES
    groups = 2 if all_pairs == 4 else all_pairs
    pairs = all_pairs // groups
    ids = jnp.stack(
        [lax.axis_index("rep"), (seq_index > 0).astype(jnp.int32), (seq_index < seq_devices - 1).astype(jnp.int32), first_row]
    ).astype(jnp.int32)
    gain = norm_gain[None, :]
    bounds = span_bounds.T

    both = ("seq", "rep")
    chips = [(i, i + 1) for i in range(1, seq_devices - 1, 2)]
    chips = chips + [(b, a) for a, b in chips]
    steps = list(steps_of("seq"))
    tie = lax.optimization_barrier

    fronts, mine, normed = [], [], book_tokens
    turn = ids
    fetched = []
    for g in range(groups):
        last = g == groups - 1
        normed, *outs = front(g == 0, last, g, pairs, turn, normed, gain, key_weight, value_weight, proj_weight,
                              dual_gains, [f[3] for f in fronts], fetched)
        outs, turn, fetched = outs[:4], outs[4], outs[5:]
        fronts.append(outs)
        send, edge = outs[2], outs[3]
        if last:
            for f in range(g):
                for step in steps[:-1]:
                    got, turn = tie((swap(mine[f], "seq", step), turn))
                    mine[f] = add_call(mine[f], got, LONG)
                mine[f], turn = tie((mine[f], turn))
        core = swap(send, "rep", 1)
        if last:
            chip = lax.ppermute(edge, both, chips)
        mine.append(add_call(outs[1], core))
        mine[g], turn = tie((mine[g], turn))

    if groups == 1:
        for step in steps[:-1]:
            mine[0] = add_call(mine[0], swap(mine[0], "seq", step))

    spread = lax.axis_size("seq")
    outs, arrived, others, other_index, queries = [], [], [], [], []
    for g in range(groups):
        source = queries[g] if g else normed
        *made, near_sums, turn = near(pairs, g, groups, turn, source, query_weight, core, chip, fronts[g][0])
        queries = queries if g else made
        q = made[0]
        got, turn = tie((swap(mine[g], "seq", steps[-1]), turn))
        total = add_call(mine[g], got)
        other = swap(total, "rep", 1)
        if g == groups - 2:
            for step in steps[:-1]:
                got, turn = tie((swap(mine[-1], "seq", step), turn))
                mine[-1] = add_call(mine[-1], got)
            mine[-1], turn = tie((mine[-1], turn))
        out = []
        for p in range(pairs):
            final = []
            if g == groups - 1 and p == pairs - 1:
                final = [bounds] + [piece for o in outs for piece in o] + out
            made, *sums, turn = far(pairs, g, p, spread, turn, q, near_sums, dual_gains, [total, other], arrived, final)
            arrived = []
            out.append(made)
        outs.append(out)
        moved = [[across_heads(piece, k) for piece in out] for k in range(1, head_devices)]
        arrived = [moved[0][0]] if g < groups - 1 and moved else []
        others += moved
        other_index += [lax.rem(head_index - k + head_devices, head_devices) * groups + g for k in range(1, head_devices)]

    own_index = [head_index * groups + g for g in range(groups)]
    early = len(others) - (head_devices - 1)

    keep, send = sums
    place = lax.axis_index("seq").astype(jnp.int32)[None]
    own, *pieces = pool_pieces(place, keep, swap(send, "rep", 1), spread)
    pieces = [
        lax.ppermute(piece, "seq", [(i, (i + k + 1) % spread) for i in range(spread)]) for k, piece in enumerate(pieces)
    ]
    parts = outs + others[:early]
    index = jnp.stack(own_index + other_index[:early]).astype(jnp.int32)
    acc, turn = out_part(parts, index, out_weight, None, F32)
    place = (seq_index * own.shape[0]).astype(jnp.int32)[None]
    place = place + (turn - index[:1])
    own = pool_own(place, bounds, own, pieces)
    pooled = [own] + [across_heads(own, k) for k in range(1, head_devices)]
    pooled_index = [lax.rem(head_index - k + head_devices, head_devices) for k in range(head_devices)]
    index = jnp.stack(other_index[early:] + pooled_index).astype(jnp.int32)
    return tuple(out_part(others[early:], index, out_weight, acc, BF, pooled)[:2])


def solution(mesh):
    placed = (
        P(("groups", "seq", "rep"), None),
        P(),
        P(None, "head"),
        P(None, "head"),
        P(None, "head"),
        P(None, "head"),
        P(None, "head"),
        P(None, "head"),
        P("groups", None),
    )
    return jax.shard_map(
        per_device,
        mesh=mesh,
        in_specs=placed,
        out_specs=(P(("groups", "seq", "rep"), "head"), P(("groups", "seq", "rep"), "head")),
        check_vma=False,
    )
```
